128 devices in a mesh: tm: 32 (over y, x, core), head: 4 (over z).
Axes of the slice: x: 4, y: 4, z: 4, core: 2. Of those that a mesh axis runs over, the one named last changes fastest.
Arguments:
- queries: bfloat16 [16384, 1024], P('tm', 'head'), may hold values from -5.5 to 5.5
- key_states: bfloat16 [16384, 1024], P('tm', 'head'), may hold values from -5.5 to 5.5
- value_states: bfloat16 [16384, 1024], P('tm', 'head'), may hold values from -6 to 6
- out_weight: bfloat16 [1024, 1024], P('head'), may hold values from -6 to 6
- upstream: bfloat16 [16384, 1024], P('tm'), may hold values from -6 to 6
- windows: int32 [16], P('head'), may hold values from 64 to 256, as said below
- offsets: int32 [16], P('head'), may hold values from 0 to 31
Outputs:
- mixed: bfloat16 [16384, 1024], P('tm')
- grad_queries: bfloat16 [16384, 1024], P('tm', 'head')
- grad_keys: bfloat16 [16384, 1024], P('tm', 'head')
- grad_values: bfloat16 [16384, 1024], P('tm', 'head')
The draws below stay inside these ranges and needn't reach their ends.
Inputs may be any that keep to these rules, and one draw needn't show every extreme that they name: `windows`: each head's window reaches at most 256 positions to each side, and some head's window is exactly 256.
All inputs are finite; a program needn't handle non-finite values.
Results may differ from the reference program's by a relative error of at most 0.017.
Values may be sent and summed in bfloat16 or wider, within the bound.
No kernel may reach another device: no remote copies, remote signals or barrier semaphores. Data moves between devices by JAX's collectives and lax.ppermute only.
A program may use at most 128 MiB of HBM per device.

```python
import math
import jax
import jax.numpy as jnp
from jax import lax

HEADS = 16
HEAD_DIM = 64
D = 1024
TOK_DEV = 512
TOKENS = 16384
WIN = 256
LEVELS = 5
N_TM = 32


def base_draw(key):
    return jnp.clip(jax.random.normal(key, (TOKENS, D), jnp.float32), -5.5, 5.5)


def draw_queries(key, part):
    values = base_draw(jax.random.fold_in(key, 11))
    return values.astype(jnp.bfloat16)


def draw_key_states(key, part):
    values = base_draw(jax.random.fold_in(key, 12))
    return values.astype(jnp.bfloat16)


def draw_windows(key, part):
    spans = jax.random.randint(jax.random.fold_in(key, 21), (HEADS,), WIN // 4, WIN + 1)
    chosen = jax.random.randint(jax.random.fold_in(key, 22), (), 0, HEADS)
    return jnp.where(jnp.arange(HEADS) == chosen, WIN, spans).astype(jnp.int32)


def touch_ends(result, own_key, least, high):
    longest = result.shape.index(max(result.shape))
    spots = []
    for shift in (0, 1):
        where = [jax.random.randint(jax.random.fold_in(own_key, axis), (), 0, length) for axis, length in enumerate(result.shape)]
        where[longest] = (where[longest] + shift) % result.shape[longest]
        spots.append(tuple(where))
    return result.at[spots[0]].set(least).at[spots[1]].set(high)


def level_of(key, shape, shards, smallest, largest):
    level, own = 1.0, jax.random.fold_in(key, 6)
    for axis_at, blocks in shards:
        heights = jnp.exp(jax.random.uniform(jax.random.fold_in(own, axis_at), (blocks,), jnp.float32, smallest / len(shards), largest / len(shards)))
        level = level * jnp.repeat(heights, shape[axis_at] // blocks).reshape([-1 if axis == axis_at else 1 for axis in range(len(shape))])
    return level


def normal_values(stream_key, dims, deviation, most, cuts=(), kind=jnp.bfloat16):
    values = deviation * jax.random.normal(stream_key, dims, jnp.float32)
    if cuts:
        values = values * level_of(stream_key, dims, cuts, -0.22, 0.18)
    return jnp.clip(values, -most, most).astype(kind)


def setup_inputs(seed: int = 0) -> dict:
    key_list = jax.random.split(jax.random.key(seed), 8)
    queries = draw_queries(jax.random.fold_in(key_list[7], 71), 0)
    key_states = draw_key_states(jax.random.fold_in(key_list[7], 71), 0)
    value_states = normal_values(key_list[2], (TOKENS, D), 1.0, 6.0, ((0, 32), (1, 4)))
    out_weight = normal_values(key_list[3], (D, D), 1.0, 6.0, ((0, 4),))
    upstream = normal_values(key_list[4], (TOKENS, D), 1.0, 6.0, ((0, 32),))
    windows = draw_windows(jax.random.fold_in(key_list[7], 71), 0)
    offsets = touch_ends(jax.random.randint(key_list[6], (HEADS,), 0, N_TM), jax.random.fold_in(key_list[6], 1), 0, N_TM - 1).astype(jnp.int32)
    return dict(queries=queries, key_states=key_states, value_states=value_states, out_weight=out_weight, upstream=upstream, windows=windows, offsets=offsets)


HIGH = lax.Precision.HIGHEST

def lane_select(grouped, lane_hit):
    lane_mask = lane_hit.reshape(lane_hit.shape + (1,) * (grouped.ndim - 3))
    return lax.optimization_barrier(jnp.sum(jnp.where(lane_mask[None], grouped, jnp.zeros((), grouped.dtype)), axis=1))

def lane_spread(values, lane_hit, filler):
    lane_mask = lane_hit.reshape(lane_hit.shape + (1,) * (values.ndim - 2))
    spread = jnp.where(lane_mask[None], values[:, None], filler)
    return spread.reshape((-1,) + values.shape[1:])

def attend_block(query_block, key_block, value_block, allowed, score_scale):
    scores = jnp.einsum('qhd,khd->hqk', query_block, key_block, precision=HIGH) * score_scale
    scores = jnp.where(allowed, scores, -jnp.inf)
    block_max = lax.optimization_barrier(jnp.max(scores, axis=2))
    weights = jnp.exp(scores - block_max[:, :, None])
    block_sum = lax.optimization_barrier(jnp.sum(weights, axis=2))
    rounded = lax.optimization_barrier(weights.astype(jnp.bfloat16)).astype(jnp.float32)
    block_acc = jnp.einsum('hqk,khd->qhd', rounded, value_block, precision=HIGH)
    return (block_max.T, block_sum.T, block_acc)

def back_block(query_block, key_block, value_block, grad_block, norm_block, delta_block, allowed, score_scale):
    scores = jnp.einsum('qhd,khd->hqk', query_block, key_block, precision=HIGH) * score_scale
    scores = jnp.where(allowed, scores, -jnp.inf)
    probs = jnp.exp(scores - norm_block.T[:, :, None])
    dots = jnp.einsum('qhd,khd->hqk', grad_block, value_block, precision=HIGH)
    score_grad = lax.optimization_barrier((probs * (dots - delta_block.T[:, :, None])).astype(jnp.bfloat16)).astype(jnp.float32)
    prob_round = lax.optimization_barrier(probs.astype(jnp.bfloat16)).astype(jnp.float32)
    query_grad = jnp.einsum('hqk,khd->qhd', score_grad, key_block, precision=HIGH) * score_scale
    key_grad = jnp.einsum('hqk,qhd->khd', score_grad, query_block, precision=HIGH) * score_scale
    value_grad = jnp.einsum('hqk,qhd->khd', prob_round, grad_block, precision=HIGH)
    return (query_grad, key_grad, value_grad)

def merge_stats(running, extra):
    new_max = jnp.maximum(running[0], extra[0])
    old_scale = jnp.exp(running[0] - new_max)
    new_scale = jnp.exp(extra[0] - new_max)
    return (new_max, running[1] * old_scale + extra[1] * new_scale, running[2] * old_scale[:, :, None] + extra[2] * new_scale[:, :, None])

def reference(queries, key_states, value_states, out_weight, upstream, windows, offsets):
    seq_total = TOKENS
    score_scale = 1.0 / math.sqrt(HEAD_DIM)
    half_width = WIN
    block_rows = min(512, TOK_DEV)
    span_rows = block_rows + 2 * half_width
    heads_shape = (seq_total, HEADS, HEAD_DIM)
    query_f = queries.astype(jnp.float32).reshape(heads_shape)
    key_f = key_states.astype(jnp.float32).reshape(heads_shape)
    value_f = value_states.astype(jnp.float32).reshape(heads_shape)
    pad_spec = ((half_width, half_width), (0, 0), (0, 0))
    key_pad = jnp.pad(key_f, pad_spec)
    value_pad = jnp.pad(value_f, pad_spec)
    block_starts = (jnp.arange(seq_total // block_rows) * block_rows).astype(jnp.int32)

    def window_allowed(start):
        query_pos = start + jnp.arange(block_rows)[:, None]
        key_pos = start - half_width + jnp.arange(span_rows)[None, :]
        inside = (key_pos >= 0) & (key_pos < seq_total)
        near = jnp.abs(query_pos - key_pos)[None] <= windows[:, None, None]
        return near & inside[None]

    def window_forward(start):
        return attend_block(lax.dynamic_slice_in_dim(query_f, start, block_rows, 0), lax.dynamic_slice_in_dim(key_pad, start, span_rows, 0), lax.dynamic_slice_in_dim(value_pad, start, span_rows, 0), window_allowed(start), score_scale)
    win_max, win_sum, win_acc = lax.map(window_forward, block_starts)
    running = (win_max.reshape(seq_total, HEADS), win_sum.reshape(seq_total, HEADS), win_acc.reshape(heads_shape))
    level_info = []
    for level_no in range(1, LEVELS + 1):
        level_rate = 2 ** level_no
        seg_count = seq_total // (level_rate * TOK_DEV)
        lane_hit = jnp.arange(level_rate)[:, None] == (offsets % level_rate)[None, :]

        def select_lanes(array):
            grouped = array.reshape((seq_total // level_rate, level_rate) + array.shape[1:])
            return lane_select(grouped, lane_hit).reshape((seg_count, TOK_DEV) + array.shape[1:])
        level_q = select_lanes(query_f)
        level_k = select_lanes(key_f)
        level_v = select_lanes(value_f)

        def level_forward(inputs):
            return attend_block(inputs[0], inputs[1], inputs[2], True, score_scale)
        level_max, level_sum, level_acc = lax.map(level_forward, (level_q, level_k, level_v))
        extra = (lane_spread(level_max.reshape(-1, HEADS), lane_hit, -jnp.inf), lane_spread(level_sum.reshape(-1, HEADS), lane_hit, 0.0), lane_spread(level_acc.reshape(-1, HEADS, HEAD_DIM), lane_hit, 0.0))
        running = merge_stats(running, extra)
        level_info.append((level_rate, seg_count, lane_hit, level_q, level_k, level_v))
    run_max, run_sum, run_acc = running
    attn = (run_acc / run_sum[:, :, None]).astype(jnp.bfloat16)
    log_norm = run_max + jnp.log(run_sum)
    mixed = jnp.dot(attn.reshape(seq_total, D), out_weight, preferred_element_type=jnp.float32).astype(jnp.bfloat16)
    grad_attn = jnp.dot(upstream, out_weight.T, preferred_element_type=jnp.float32).astype(jnp.bfloat16)
    grad_f = grad_attn.astype(jnp.float32).reshape(heads_shape)
    row_delta = lax.optimization_barrier(jnp.sum(grad_f * attn.astype(jnp.float32), axis=2))

    def window_backward(carry, start):
        key_acc, value_acc = carry
        query_grad, key_grad, value_grad = back_block(lax.dynamic_slice_in_dim(query_f, start, block_rows, 0), lax.dynamic_slice_in_dim(key_pad, start, span_rows, 0), lax.dynamic_slice_in_dim(value_pad, start, span_rows, 0), lax.dynamic_slice_in_dim(grad_f, start, block_rows, 0), lax.dynamic_slice_in_dim(log_norm, start, block_rows, 0), lax.dynamic_slice_in_dim(row_delta, start, block_rows, 0), window_allowed(start), score_scale)
        key_acc = lax.dynamic_update_slice_in_dim(key_acc, lax.dynamic_slice_in_dim(key_acc, start, span_rows, 0) + key_grad, start, 0)
        value_acc = lax.dynamic_update_slice_in_dim(value_acc, lax.dynamic_slice_in_dim(value_acc, start, span_rows, 0) + value_grad, start, 0)
        return ((key_acc, value_acc), query_grad)
    zero_pad = jnp.zeros(key_pad.shape, jnp.float32)
    (key_acc, value_acc), query_parts = lax.scan(window_backward, (zero_pad, zero_pad), block_starts)
    query_total = query_parts.reshape(heads_shape)
    key_total = key_acc[half_width:half_width + seq_total]
    value_total = value_acc[half_width:half_width + seq_total]
    for level_rate, seg_count, lane_hit, level_q, level_k, level_v in level_info:

        def select_lanes(array):
            grouped = array.reshape((seq_total // level_rate, level_rate) + array.shape[1:])
            return lane_select(grouped, lane_hit).reshape((seg_count, TOK_DEV) + array.shape[1:])

        def level_backward(inputs):
            return back_block(inputs[0], inputs[1], inputs[2], inputs[3], inputs[4], inputs[5], True, score_scale)
        query_grad, key_grad, value_grad = lax.map(level_backward, (level_q, level_k, level_v, select_lanes(grad_f), select_lanes(log_norm), select_lanes(row_delta)))
        query_total = query_total + lane_spread(query_grad.reshape(-1, HEADS, HEAD_DIM), lane_hit, 0.0)
        key_total = key_total + lane_spread(key_grad.reshape(-1, HEADS, HEAD_DIM), lane_hit, 0.0)
        value_total = value_total + lane_spread(value_grad.reshape(-1, HEADS, HEAD_DIM), lane_hit, 0.0)
    return (mixed, query_total.reshape(seq_total, D).astype(jnp.bfloat16), key_total.reshape(seq_total, D).astype(jnp.bfloat16), value_total.reshape(seq_total, D).astype(jnp.bfloat16))
```

```python
import jax
import jax.numpy as jnp
from jax import lax
from jax.experimental import pallas as pl
from jax.experimental.pallas import tpu as pltpu
from jax.sharding import PartitionSpec as P


F32 = jnp.float32
BF16 = jnp.bfloat16
NEG = -1e30
NT = (((1,), (1,)), ((), ()))
SMEM = pl.BlockSpec(memory_space=pltpu.SMEM)


def sds(shape, dtype):
    return jax.ShapeDtypeStruct(shape, dtype)


def dot(a, b):
    return jnp.dot(a, b, preferred_element_type=F32)


def dot_nt(a, b):
    return lax.dot_general(a, b, NT, preferred_element_type=F32)


def call(body, ins, outs, scratch=(), flops=0, nbytes=0, specs=None, out_specs=None, grid=None, name=None):
    full = lambda x: pl.BlockSpec(x.shape, (lambda *_: (0,) * len(x.shape)))
    specs = specs or [None] * len(ins)
    in_specs = [full(x) if s is None else s for x, s in zip(ins, specs)]
    out_specs = out_specs or [full(o) for o in outs]
    return pl.pallas_call(
        body,
        out_shape=outs,
        grid=grid or (1,),
        in_specs=in_specs,
        out_specs=out_specs,
        scratch_shapes=list(scratch),
        name=name,
        cost_estimate=pl.CostEstimate(flops=int(flops), bytes_accessed=int(nbytes), transcendentals=0),
        compiler_params=pltpu.CompilerParams(vmem_limit_bytes=50 << 20),
    )(*ins)


def iota(shape, axis):
    return lax.broadcasted_iota(jnp.int32, shape, axis)


def place(n, offset):
    u = jnp.where(n >= 128, 2 * (n - 128) + 1, 4 * (n - 64) + 2)
    u = jnp.where(n >= 64, u, 8 * (n - 32) + 4)
    u = jnp.where(n >= 32, u, 16 * (n - 16) + 8)
    u = jnp.where(n >= 16, u, 32 * (n - 8) + 16)
    u = jnp.where(n >= 8, u, 32 * n)
    return (u + offset) & 255


def depth(n):
    d = jnp.where(n < 64, 2, 1)
    d = jnp.where(n < 32, 3, d)
    d = jnp.where(n < 16, 4, d)
    return jnp.where(n < 8, 5, d)


def to_depth(offset):
    s = (256, 256)
    return (iota(s, 1) == place(iota(s, 0), offset)).astype(F32).astype(BF16)


def from_depth(offset):
    s = (256, 256)
    return (iota(s, 0) == place(iota(s, 1), offset)).astype(F32).astype(BF16)


def lane_first(rows, width=128):
    return (iota((rows, width), 1) % 128) < 64


def zero_pad(x, which):
    z = jnp.zeros_like(x)
    return jnp.concatenate([x, z] if which == 0 else [z, x], axis=0)


def transposed(x):
    return x.astype(F32).T.astype(BF16)


def prep_kv(off, par, k, v, kvp, c1, n1, x1):
    keep = lane_first(256, 256)
    for pair in range(2):
        lanes = slice(pair * 128, pair * 128 + 128)
        first, second = to_depth(off[2 * pair]), to_depth(off[2 * pair + 1])
        for b in range(2):
            rows = slice(b * 256, b * 256 + 256)
            kv = jnp.concatenate([k[rows, lanes], v[rows, lanes]], axis=1)
            kvp[rows, pair * 256 : pair * 256 + 256] = jnp.where(
                keep, dot(first, kv), dot(second, kv)
            ).astype(BF16)
    x1[0:64] = kvp[0:64]
    x1[64:128] = kvp[256:320]

    @pl.when(par[0] == 0)
    def _():
        c1[0:256] = kvp[256:512]
        c1[256:384] = kvp[0:128]
        n1[...] = kvp[0:256]

    @pl.when(par[0] == 1)
    def _():
        c1[0:256] = kvp[0:256]
        c1[256:384] = kvp[256:384]
        n1[...] = kvp[256:512]


def prep_qg(off, q, up, w, qt, gt):
    g = dot_nt(w[...], up[...]).astype(BF16)
    qs = (q[...].astype(F32) * 0.125).T.astype(BF16)
    for h in range(4):
        perm = from_depth(off[h])
        hs = slice(64 * h, 64 * h + 64)
        for b in range(2):
            bs = slice(256 * b, 256 * b + 256)
            x = jnp.concatenate([qs[hs, bs], g[hs, bs]], axis=0)
            r = dot(x, perm).astype(BF16)
            qt[hs, bs] = r[0:64]
            gt[hs, bs] = r[64:128]


def pack_rows(pieces):
    return jnp.concatenate([p.astype(F32) for p in pieces], axis=0).astype(BF16)


def asm_x2(kvp, x1, out):
    out[...] = pack_rows([kvp[0:32], kvp[256:288], x1[0:32], x1[64:96]])


def asm_y1(kvp, x1, x2, out):
    out[...] = pack_rows(
        [kvp[0:16], kvp[256:272], x1[0:16], x1[64:80]] + [x2[32 * j : 32 * j + 16] for j in range(4)]
    )


def asm_y2(kvp, x1, x2, y1, out):
    heads = [kvp[0:16], kvp[256:272], x1[0:16], x1[64:80]]
    heads += [x2[32 * j : 32 * j + 16] for j in range(4)]
    heads += [y1[16 * j : 16 * j + 16] for j in range(8)]
    out[...] = jnp.concatenate([h.astype(F32)[0:8] for h in heads], axis=0).astype(BF16)


def fill_ext(par, kv, c1, n1, kx, vx):
    kx[256:768] = kv[:, 0:128]
    vx[256:768] = kv[:, 128:256]

    @pl.when(par[0] == 0)
    def _():
        kx[0:256] = n1[:, 0:128]
        vx[0:256] = n1[:, 128:256]
        kx[768:1024] = c1[0:256, 0:128]
        vx[768:1024] = c1[0:256, 128:256]

    @pl.when(par[0] == 1)
    def _():
        kx[0:256] = c1[0:256, 0:128]
        vx[0:256] = c1[0:256, 128:256]
        kx[768:1024] = n1[:, 0:128]
        vx[768:1024] = n1[:, 128:256]


def near_chunks(kx, c1, lo):
    return [kx[256:384], kx[512:640], c1[0:128, lo : lo + 128], c1[256:384, lo : lo + 128]]


def near_count():
    s = (128, 128)
    return jnp.minimum(depth(iota(s, 0)), depth(iota(s, 1))).astype(F32)


def fwd_near(pair, off, win, par, tm, qt, kv, c1, n1, pw, p1, acc_out, stat, kx, vx, vt, v1t, k1, dist, sw, s1):
    fill_ext(par, kv, c1, n1, kx, vx)
    vt[...] = transposed(vx[...])
    k1[...] = jnp.concatenate(near_chunks(kx, c1, 0), axis=0)
    v1t[...] = transposed(jnp.concatenate(near_chunks(vx, c1, 128), axis=0))
    count = near_count()
    for a in range(2):
        h = 2 * pair + a
        s = (256, 256)
        dist[...] = place(iota(s, 0), off[h]) - place(iota(s, 1), off[h])
        reach = win[h]
        lo = jnp.where(tm[0] == 0, 1000, 256 - reach)
        hi = jnp.where(tm[0] == 31, -1000, reach - 256)
        for b in range(2):
            qz = zero_pad(qt[64 * a : 64 * a + 64, 256 * b : 256 * b + 256], a)
            top = None
            for c in range(3):
                sc = dot(kx[256 * (b + c) : 256 * (b + c) + 256], qz)
                d = dist[...]
                if c == 0:
                    ok = d >= (lo if b == 0 else 256 - reach)
                elif c == 1:
                    ok = jnp.abs(d) <= reach
                else:
                    ok = d <= (hi if b == 1 else reach - 256)
                sc = jnp.where(ok, sc, NEG)
                sw[256 * c : 256 * c + 256] = sc
                part = jnp.max(sc, axis=0, keepdims=True)
                top = part if top is None else jnp.maximum(top, part)
            sc = dot(k1[...], qz[:, 0:128])
            s1[...] = sc
            near_top = jnp.maximum(top[:, 0:128], jnp.max(sc, axis=0, keepdims=True))
            top = jnp.concatenate([near_top, top[:, 128:256]], axis=1)
            total = jnp.zeros((1, 256), F32)
            for c in range(3):
                e = jnp.exp(sw[256 * c : 256 * c + 256] - top)
                total += jnp.sum(e, axis=0, keepdims=True)
                pw[a, b, 256 * c : 256 * c + 256, :] = e.astype(BF16)
            vh = slice(64 * a, 64 * a + 64)
            acc = dot(vt[vh, 256 * b : 256 * b + 768], pw[a, b])
            near_sum = jnp.zeros((1, 128), F32)
            bs = slice(128 * b, 128 * b + 128)
            for c in range(4):
                e = count * jnp.exp(s1[128 * c : 128 * c + 128] - near_top)
                near_sum += jnp.sum(e, axis=0, keepdims=True)
                p1[a, 128 * c : 128 * c + 128, bs] = e.astype(BF16)
            near_acc = dot(v1t[vh, :], p1[a, :, bs])
            acc_out[vh, 256 * b : 256 * b + 128] = acc[:, 0:128] + near_acc
            acc_out[vh, 256 * b + 128 : 256 * b + 256] = acc[:, 128:256]
            stat[a : a + 1, 256 * b : 256 * b + 256] = top
            stat[2 + a : 3 + a, 256 * b : 256 * b + 128] = total[:, 0:128] + near_sum
            stat[2 + a : 3 + a, 256 * b + 128 : 256 * b + 256] = total[:, 128:256]


def far_count():
    s = (1024, 128)
    j, i = iota(s, 0), iota(s, 1)
    level = 2 + j // 256
    chunk = jnp.where(level == 2, 64, jnp.where(level == 3, 32, jnp.where(level == 4, 16, 8)))
    both = jnp.minimum(depth(j & (chunk - 1)), depth(i & 63))
    return jnp.maximum(both - level + 1, 0).astype(F32)


def far_lanes(x):
    return jnp.concatenate([x[:, 0:64], x[:, 256:320]], axis=1)


def wide(x, b, filler):
    rows = x.shape[0]
    return jnp.concatenate([x[:, 64 * b : 64 * b + 64], jnp.full((rows, 192), filler, F32)], axis=1)


def fwd_far(pair0, off, qt, gt, acc_in, stat, *rest):
    bufs, (pf, attn, stat2, kf, vft, mult, at) = rest[:8], rest[8:]
    pair = pl.program_id(0)
    for j, buf in enumerate(bufs):
        kf[128 * j : 128 * j + 128] = buf[:, 0:128]
    vft[...] = transposed(jnp.concatenate([buf[:, 128:256] for buf in bufs], axis=0))
    mult[...] = far_count()
    for a in range(2):
        vh = slice(64 * a, 64 * a + 64)
        qz = zero_pad(far_lanes(qt[vh, :]), a)
        cnt = mult[...]
        sc = jnp.where(cnt > 0, dot(kf[...], qz), NEG)
        ftop = jnp.max(sc, axis=0, keepdims=True)
        e = cnt * jnp.exp(sc - ftop)
        fsum = jnp.sum(e, axis=0, keepdims=True)
        pf[a] = e.astype(BF16)
        facc = dot(vft[vh, :], pf[a])
        for b in range(2):
            bs = slice(256 * b, 256 * b + 256)
            ntop, nsum = stat[a : a + 1, bs], stat[2 + a : 3 + a, bs]
            ftopw = wide(ftop, b, NEG)
            top = jnp.maximum(ntop, ftopw)
            wn, wf = jnp.exp(ntop - top), jnp.exp(ftopw - top)
            norm = nsum * wn + wide(fsum, b, 0.0) * wf
            acc = acc_in[vh, bs] * wn + wide(facc, b, 0.0) * wf
            o = (acc / norm).astype(BF16)
            at[vh, bs] = o
            stat2[a : a + 1, bs] = wn / norm
            stat2[2 + a : 3 + a, bs] = wf / norm
            stat2[4 + a : 5 + a, bs] = jnp.sum(
                gt[vh, bs].astype(F32) * o.astype(F32), axis=0, keepdims=True
            )
    unperm_pair(off, pair, at, attn)


def unperm_pair(off, pair, src, out):
    keep = lane_first(256)
    first, second = from_depth(off[2 * pair]), from_depth(off[2 * pair + 1])
    for b in range(2):
        x = src[:, 256 * b : 256 * b + 256]
        out[256 * b : 256 * b + 256, :] = jnp.where(keep, dot_nt(first, x), dot_nt(second, x)).astype(BF16)


def bwd_far(par, qt, gt, stat2, kv, c1, pf, p1, *rest):
    bufs, (ret, own_far, own_near, dq, kx, vx) = rest[:8], rest[8:]
    for j, buf in enumerate(bufs):
        kx[128 * j : 128 * j + 128] = buf[:, 0:128]
        vx[128 * j : 128 * j + 128] = buf[:, 128:256]
    kt = transposed(kx[...])
    grads = []
    scaled_q, scaled_g = [], []
    for a in range(2):
        vh = slice(64 * a, 64 * a + 64)
        cf = far_lanes(stat2[2 + a : 3 + a, :])
        delta = far_lanes(stat2[4 + a : 5 + a, :])
        q, g = far_lanes(qt[vh, :]), far_lanes(gt[vh, :])
        dp = dot(vx[...], zero_pad(g, a))
        ds = (pf[a].astype(F32) * (dp - delta)).astype(BF16)
        grads.append(ds)
        scaled_q.append(zero_pad((q.astype(F32) * cf).astype(BF16), a))
        scaled_g.append(zero_pad((g.astype(F32) * cf).astype(BF16), a))
        fq = dot(kt[vh, :], ds) * cf
        dq[vh, :] = jnp.zeros((64, 512), F32)
        dq[vh, 0:64] = fq[:, 0:64]
        dq[vh, 256:320] = fq[:, 64:128]
    dk = dot_nt(jnp.concatenate(grads, axis=1), jnp.concatenate(scaled_q, axis=1))
    dv = dot_nt(jnp.concatenate([pf[0], pf[1]], axis=1), jnp.concatenate(scaled_g, axis=1))
    for j in range(4):
        mine, theirs = slice(256 * j, 256 * j + 128), slice(256 * j + 128, 256 * j + 256)
        own_far[128 * j : 128 * j + 128, 0:128] = dk[mine]
        own_far[128 * j : 128 * j + 128, 128:256] = dv[mine]
        ret[256 + 128 * j : 384 + 128 * j, 0:128] = dk[theirs].astype(BF16)
        ret[256 + 128 * j : 384 + 128 * j, 128:256] = dv[theirs].astype(BF16)
    lo, hi = slice(0, 128), slice(128, 256)
    k1 = jnp.concatenate([kv[0:128, lo], kv[256:384, lo], c1[0:128, lo], c1[256:384, lo]], axis=0)
    v1 = jnp.concatenate([kv[0:128, hi], kv[256:384, hi], c1[0:128, hi], c1[256:384, hi]], axis=0)
    k1t = transposed(k1)
    grads, scaled_q, scaled_g, probs = [], [], [], []
    for a in range(2):
        vh = slice(64 * a, 64 * a + 64)
        for b in range(2):
            bs = slice(256 * b, 256 * b + 128)
            cn, delta = stat2[a : a + 1, bs], stat2[4 + a : 5 + a, bs]
            g = gt[vh, bs]
            p = p1[a, :, 128 * b : 128 * b + 128]
            ds = (p.astype(F32) * (dot(v1, zero_pad(g, a)) - delta)).astype(BF16)
            grads.append(ds)
            probs.append(p)
            scaled_q.append(zero_pad((qt[vh, bs].astype(F32) * cn).astype(BF16), a))
            scaled_g.append(zero_pad((g.astype(F32) * cn).astype(BF16), a))
            dq[vh, bs] += dot(k1t[vh, :], ds) * cn
    dk = dot_nt(jnp.concatenate(grads, axis=1), jnp.concatenate(scaled_q, axis=1))
    dv = dot_nt(jnp.concatenate(probs, axis=1), jnp.concatenate(scaled_g, axis=1))
    own_near[:, 0:128] = dk[0:256]
    own_near[:, 128:256] = dv[0:256]
    ret[0:256, 0:128] = dk[256:512].astype(BF16)
    ret[0:256, 128:256] = dv[256:512].astype(BF16)


def bwd_near(pair, off, par, qt, gt, stat2, kv, c1, n1, pw, dq_in, own_near, own, halo_c, halo_n, gq, kx, vx, kt, dk, dv, dqt):
    fill_ext(par, kv, c1, n1, kx, vx)
    kt[...] = transposed(kx[...])
    dk[...] = jnp.zeros((1024, 128), F32)
    dv[...] = jnp.zeros((1024, 128), F32)
    for (dst, lanes) in ((dk, slice(0, 128)), (dv, slice(128, 256))):
        dst[256:384] = own_near[0:128, lanes]
        dst[512:640] = own_near[128:256, lanes]
    for b in range(2):
        bs = slice(256 * b, 256 * b + 256)
        ext = slice(256 * b, 256 * b + 768)
        for a in range(2):
            vh = slice(64 * a, 64 * a + 64)
            cn, delta = stat2[a : a + 1, bs], stat2[4 + a : 5 + a, bs]
            g = gt[vh, bs]
            dp = dot(vx[ext], zero_pad(g, a))
            p = pw[a, b]
            ds = (p.astype(F32) * (dp - delta)).astype(BF16)
            qs = zero_pad((qt[vh, bs].astype(F32) * cn).astype(BF16), a)
            gs = zero_pad((g.astype(F32) * cn).astype(BF16), a)
            dk[ext] += dot_nt(ds, qs)
            dv[ext] += dot_nt(p, gs)
            dqt[vh, bs] = ((dot(kt[vh, ext], ds) * cn + dq_in[vh, bs]) * 0.125).astype(BF16)
    own[:, 0:128] = dk[256:768]
    own[:, 128:256] = dv[256:768]
    low = jnp.concatenate([dk[0:256], dv[0:256]], axis=1).astype(BF16)
    high = jnp.concatenate([dk[768:1024], dv[768:1024]], axis=1).astype(BF16)

    @pl.when(par[0] == 0)
    def _():
        halo_n[...] = low
        halo_c[...] = high

    @pl.when(par[0] == 1)
    def _():
        halo_c[...] = low
        halo_n[...] = high

    unperm_pair(off, pair, dqt, gq)


def ret_y2(own_far, ret, rest, send):
    total = own_far[...] + ret[256:768].astype(F32)
    rest[...] = total[0:384]
    send[...] = total[384:512].astype(BF16)


def ret_y1(rest, got, left, send):
    y2 = got[...].astype(F32)
    left[...] = rest[0:256]
    for j in range(2):
        left[64 * j : 64 * j + 8] += y2[16 + 8 * j : 24 + 8 * j]
    for j in range(4):
        left[128 + 32 * j : 136 + 32 * j] += y2[32 + 8 * j : 40 + 8 * j]
    zero = jnp.zeros((8, 512), F32)
    extra = []
    for j in range(8):
        extra += [y2[64 + 8 * j : 72 + 8 * j], zero]
    send[...] = (rest[256:384] + jnp.concatenate(extra, axis=0)).astype(BF16)


def ret_x2(rest, got, left, send):
    y1 = got[...].astype(F32)
    left[...] = rest[0:128]
    for j in range(2):
        left[64 * j : 64 * j + 16] += y1[32 + 16 * j : 48 + 16 * j]
    zero = jnp.zeros((16, 512), F32)
    extra = []
    for j in range(4):
        extra += [y1[64 + 16 * j : 80 + 16 * j], zero]
    send[...] = (rest[128:256] + jnp.concatenate(extra, axis=0)).astype(BF16)


def ret_x1(rest, got, send):
    x2 = got[...].astype(F32)
    zero = jnp.zeros((32, 512), F32)
    extra = [x2[64:96], zero, x2[96:128], zero]
    send[...] = (rest[...] + jnp.concatenate(extra, axis=0)).astype(BF16)


def finish(off, par, own0, own1, ret, hc, hn, y2, y1, x2, x1, gk, gv, acc):
    acc[:, 0:256] = own0[...]
    acc[:, 256:512] = own1[...]
    for b in range(2):
        at = 256 * b
        acc[at : at + 64] += x1[64 * b : 64 * b + 64].astype(F32)
        acc[at : at + 32] += x2[32 * b : 32 * b + 32].astype(F32)
        acc[at : at + 16] += y1[16 * b : 16 * b + 16].astype(F32)
        acc[at : at + 8] += y2[0:16].astype(F32)[8 * b : 8 * b + 8]

    @pl.when(par[0] == 0)
    def _():
        acc[256:512] += hc[...].astype(F32)
        acc[0:256] += hn[...].astype(F32)
        acc[256:384] += ret[0:128].astype(F32)
        acc[0:128] += ret[128:256].astype(F32)

    @pl.when(par[0] == 1)
    def _():
        acc[0:256] += hc[...].astype(F32)
        acc[256:512] += hn[...].astype(F32)
        acc[0:128] += ret[0:128].astype(F32)
        acc[256:384] += ret[128:256].astype(F32)

    keep = lane_first(256, 256)
    for pair in range(2):
        first, second = from_depth(off[2 * pair]), from_depth(off[2 * pair + 1])
        lanes = slice(128 * pair, 128 * pair + 128)
        for b in range(2):
            rows = slice(256 * b, 256 * b + 256)
            x = acc[rows, 256 * pair : 256 * pair + 256].astype(BF16)
            r = jnp.where(keep, dot(first, x), dot(second, x)).astype(BF16)
            gk[rows, lanes] = r[:, 0:128]
            gv[rows, lanes] = r[:, 128:256]


def project(a0, a1, a2, a3, w0, w1, w2, w3, out):
    a = jnp.concatenate([a0[...], a1[...], a2[...], a3[...]], axis=1)
    w = jnp.concatenate([w0[...], w1[...], w2[...], w3[...]], axis=0)
    out[...] = dot(a, w).astype(BF16)


def swap(x, axis, mask):
    return lax.ppermute(x, axis, [(i, i ^ mask) for i in range(lax.axis_size(axis))])


def side(x):
    return lax.ppermute(x, "tm", [(i, (i + 1) % 32 if i % 2 else (i - 1) % 32) for i in range(32)])


def pair_rows(x, pair):
    return pl.BlockSpec((x.shape[0], 256), lambda *_: (0, pair))


def bind(f, *args):
    def body(*refs):
        f(*args, *refs)

    return body


def on_device(q, k, v, w, up, win, off):
    tm = lax.axis_index("tm").astype(jnp.int32).reshape(1)
    par = tm % 2
    VM = pltpu.VMEM
    kvp, c1s, n1s, x1s = call(
        prep_kv, (off, par, k, v),
        [sds((512, 512), BF16), sds((384, 512), BF16), sds((256, 512), BF16), sds((128, 512), BF16)],
        specs=[SMEM, SMEM, None, None], flops=3e8, nbytes=3e6, name="prep_kv",
    )
    x1 = swap(x1s, "tm", 2)
    c1 = swap(c1s, "tm", 1)
    n1 = side(n1s)
    wa, wb = swap(w, "head", 1), swap(w, "head", 3)
    wc = swap(wa, "head", 3)
    qt, gt = call(
        prep_qg, (off, q, up, w), [sds((256, 512), BF16), sds((256, 512), BF16)],
        specs=[SMEM, None, None, None], flops=6e8, nbytes=3e6, name="prep_qg",
    )
    head_rows = pl.BlockSpec((512, 512), lambda *_: (0, 0))
    del head_rows
    top_rows = lambda x: pl.BlockSpec((512, 512), lambda *_: (0, 0))
    x2 = swap(call(asm_x2, (kvp, x1), [sds((128, 512), BF16)], name="asm_x2")[0], "tm", 6)

    near = []
    for pair in range(2):
        qspec = pl.BlockSpec((128, 512), lambda *_, pair=pair: (pair, 0))
        near.append(
            call(
                bind(fwd_near, pair), (off, win, par, tm, qt, kvp, c1, n1),
                [sds((2, 2, 768, 256), BF16), sds((2, 512, 256), BF16), sds((128, 512), F32), sds((8, 512), F32)],
                specs=[SMEM] * 4 + [qspec] + [pair_rows(x, pair) for x in (kvp, c1, n1)],
                scratch=[
                    VM((1024, 128), BF16), VM((1024, 128), BF16), VM((128, 1024), BF16), VM((128, 512), BF16),
                    VM((512, 128), BF16), VM((256, 256), jnp.int32), VM((768, 256), F32), VM((512, 128), F32),
                ],
                flops=4e9, nbytes=4e6, name=f"fwd_near{pair}",
            )
        )
    y1 = swap(call(asm_y1, (kvp, x1, x2), [sds((128, 512), BF16)], name="asm_y1")[0], "tm", 8)
    y2 = swap(call(asm_y2, (kvp, x1, x2, y1), [sds((128, 512), BF16)], name="asm_y2")[0], "tm", 24)
    bufs = []
    for mine in (x1, x2, y1, y2):
        bufs += [mine, swap(mine, "tm", 1)]

    acc = [n[2] for n in near]
    pfs, attns, stats = [], [], []
    by_pair = lambda rows, cols: pl.BlockSpec((rows, cols), lambda p: (p, 0))
    lane_pair = lambda rows, cols: pl.BlockSpec((rows, cols), lambda p: (0, p))
    acc_all = jnp.concatenate(acc, axis=0)
    stat_all = jnp.concatenate([n[3] for n in near], axis=0)
    pf, attn, stat2 = call(
        bind(fwd_far, 0), (off, qt, gt, acc_all, stat_all, *bufs),
        [sds((4, 1024, 128), BF16), sds((512, 256), BF16), sds((16, 512), F32)],
        specs=[SMEM, by_pair(128, 512), by_pair(128, 512), by_pair(128, 512), by_pair(8, 512)]
        + [lane_pair(128, 256)] * 8,
        out_specs=[pl.BlockSpec((2, 1024, 128), lambda p: (p, 0, 0)), lane_pair(512, 128), by_pair(8, 512)],
        scratch=[VM((1024, 128), BF16), VM((128, 1024), BF16), VM((1024, 128), F32), VM((128, 512), BF16)],
        grid=(2,), flops=3e9, nbytes=4e6, name="fwd_far",
    )
    a1, a2 = swap(attn, "head", 1), swap(attn, "head", 3)
    a3 = swap(a1, "head", 3)

    p1_all = jnp.concatenate([n[1] for n in near], axis=0)
    ret_s, own_far, own_near, dq = call(
        bwd_far, (par, qt, gt, stat2, kvp, c1, pf, p1_all, *bufs),
        [sds((768, 512), BF16), sds((512, 512), F32), sds((256, 512), F32), sds((256, 512), F32)],
        specs=[SMEM, by_pair(128, 512), by_pair(128, 512), by_pair(8, 512), lane_pair(512, 256), lane_pair(384, 256),
               pl.BlockSpec((2, 1024, 128), lambda p: (p, 0, 0)), pl.BlockSpec((2, 512, 256), lambda p: (p, 0, 0))]
        + [lane_pair(128, 256)] * 8,
        out_specs=[lane_pair(768, 256), lane_pair(512, 256), lane_pair(256, 256), by_pair(128, 512)],
        scratch=[VM((1024, 128), BF16), VM((1024, 128), BF16)],
        grid=(2,), flops=5e9, nbytes=5e6, name="bwd_far",
    )
    ret = swap(ret_s, "tm", 1)
    back = []
    for pair in range(2):
        row_block = lambda rows, cols: pl.BlockSpec((rows, cols), lambda *_, pair=pair: (pair, 0))
        back.append(
            call(
                bind(bwd_near, pair), (off, par, qt, gt, stat2, kvp, c1, n1, near[pair][0], dq, own_near),
                [sds((512, 256), F32), sds((256, 256), BF16), sds((256, 256), BF16), sds((512, 128), BF16)],
                specs=[SMEM] * 2 + [row_block(128, 512), row_block(128, 512), row_block(8, 512)]
                + [pair_rows(x, pair) for x in (kvp, c1, n1)] + [None, row_block(128, 512), pair_rows(own_near, pair)],
                scratch=[
                    VM((1024, 128), BF16), VM((1024, 128), BF16), VM((128, 1024), BF16),
                    VM((1024, 128), F32), VM((1024, 128), F32), VM((128, 512), BF16),
                ],
                flops=5e9, nbytes=4e6, name=f"bwd_near{pair}",
            )
        )
    rest, y2s = call(ret_y2, (own_far, ret), [sds((384, 512), F32), sds((128, 512), BF16)], name="ret_y2")
    y2r = swap(y2s, "tm", 24)
    rest, y1s = call(ret_y1, (rest, y2r), [sds((256, 512), F32), sds((128, 512), BF16)], name="ret_y1")
    y1r = swap(y1s, "tm", 8)
    rest, x2s = call(ret_x2, (rest, y1r), [sds((128, 512), F32), sds((128, 512), BF16)], name="ret_x2")
    x2r = swap(x2s, "tm", 6)
    (x1s,) = call(ret_x1, (rest, x2r), [sds((128, 512), BF16)], name="ret_x1")
    x1r = swap(x1s, "tm", 2)
    hc = swap(jnp.concatenate([b[1] for b in back], axis=1), "tm", 1)
    hn = side(jnp.concatenate([b[2] for b in back], axis=1))
    gk, gv = call(
        finish, (off, par, back[0][0], back[1][0], ret, hc, hn, y2r, y1r, x2r, x1r),
        [sds((512, 256), BF16), sds((512, 256), BF16)],
        specs=[SMEM] * 2 + [None] * 9, scratch=[VM((512, 512), F32)], flops=3e8, nbytes=3e6, name="finish",
    )
    (mixed,) = call(
        project, (attn, a1, a2, a3, w, wa, wb, wc), [sds((512, 1024), BF16)], flops=1e9, nbytes=4e6, name="project"
    )
    gq = jnp.concatenate([back[0][3], back[1][3]], axis=1)
    return mixed, gq, gk, gv


def solution(mesh):
    placed = (P("tm", "head"),) * 3 + (P("head", None), P("tm", None), P("head"), P("head"))
    return jax.shard_map(
        on_device,
        mesh=mesh,
        in_specs=placed,
        out_specs=(P("tm", None), P("tm", "head"), P("tm", "head"), P("tm", "head")),
        check_vma=False,
    )
```

```python
import jax
import jax.numpy as jnp
from jax import lax
from jax.experimental import pallas as pl
from jax.experimental.pallas import tpu as pltpu
from jax.sharding import PartitionSpec as P


F32 = jnp.float32
BF16 = jnp.bfloat16
NEG = -1e30
NT = (((1,), (1,)), ((), ()))
SMEM = pl.BlockSpec(memory_space=pltpu.SMEM)


def sds(shape, dtype):
    return jax.ShapeDtypeStruct(shape, dtype)


def dot(a, b):
    return jnp.dot(a, b, preferred_element_type=F32)


def dot_nt(a, b):
    return lax.dot_general(a, b, NT, preferred_element_type=F32)


def call(body, ins, outs, scratch=(), flops=0, nbytes=0, specs=None, out_specs=None, vmem=24):
    full = lambda x: pl.BlockSpec(x.shape, (lambda *_: (0,) * len(x.shape)))
    specs = specs or [None] * len(ins)
    in_specs = [full(x) if s is None else s for x, s in zip(ins, specs)]
    out_specs = out_specs or [full(o) for o in outs]
    return pl.pallas_call(
        body,
        out_shape=outs,
        grid=(1,),
        in_specs=in_specs,
        out_specs=out_specs,
        scratch_shapes=list(scratch),
        cost_estimate=pl.CostEstimate(flops=int(flops), bytes_accessed=int(nbytes), transcendentals=0),
        compiler_params=pltpu.CompilerParams(vmem_limit_bytes=vmem << 20),
    )(*ins)


def iota(shape, axis):
    return lax.broadcasted_iota(jnp.int32, shape, axis)


def place(n, offset):
    u = jnp.where(n >= 128, 2 * (n - 128) + 1, 4 * (n - 64) + 2)
    u = jnp.where(n >= 64, u, 8 * (n - 32) + 4)
    u = jnp.where(n >= 32, u, 16 * (n - 16) + 8)
    u = jnp.where(n >= 16, u, 32 * (n - 8) + 16)
    u = jnp.where(n >= 8, u, 32 * n)
    return (u + offset) & 255


def depth(n):
    d = jnp.where(n < 64, 2, 1)
    d = jnp.where(n < 32, 3, d)
    d = jnp.where(n < 16, 4, d)
    return jnp.where(n < 8, 5, d)


def to_depth(offset):
    s = (256, 256)
    return (iota(s, 1) == place(iota(s, 0), offset)).astype(F32).astype(BF16)


def from_depth(offset):
    s = (256, 256)
    return (iota(s, 0) == place(iota(s, 1), offset)).astype(F32).astype(BF16)


def lane_first(rows, width=128):
    return (iota((rows, width), 1) % 128) < 64


def zero_pad(x, which):
    z = jnp.zeros_like(x)
    return jnp.concatenate([x, z] if which == 0 else [z, x], axis=0)


def transposed(x):
    return x.astype(F32).T.astype(BF16)


def prep_kv(off, par, k, v, kvp, c1, n1, x1):
    keep = lane_first(256, 256)
    for pair in range(2):
        lanes = slice(pair * 128, pair * 128 + 128)
        first, second = to_depth(off[2 * pair]), to_depth(off[2 * pair + 1])
        for b in range(2):
            rows = slice(b * 256, b * 256 + 256)
            kv = jnp.concatenate([k[rows, lanes], v[rows, lanes]], axis=1)
            kvp[rows, pair * 256 : pair * 256 + 256] = jnp.where(
                keep, dot(first, kv), dot(second, kv)
            ).astype(BF16)
    x1[0:64] = kvp[0:64]
    x1[64:128] = kvp[256:320]

    @pl.when(par[0] == 0)
    def _():
        c1[0:256] = kvp[256:512]
        c1[256:384] = kvp[0:128]
        n1[...] = kvp[0:256]

    @pl.when(par[0] == 1)
    def _():
        c1[0:256] = kvp[0:256]
        c1[256:384] = kvp[256:384]
        n1[...] = kvp[256:512]


def prep_qg(off, q, up, w, qt, gt):
    g = dot_nt(w[...], up[...]).astype(BF16)
    qs = (q[...].astype(F32) * 0.125).T.astype(BF16)
    for h in range(4):
        perm = from_depth(off[h])
        hs = slice(64 * h, 64 * h + 64)
        for b in range(2):
            bs = slice(256 * b, 256 * b + 256)
            x = jnp.concatenate([qs[hs, bs], g[hs, bs]], axis=0)
            r = dot(x, perm).astype(BF16)
            qt[hs, bs] = r[0:64]
            gt[hs, bs] = r[64:128]


def pack_rows(pieces):
    return jnp.concatenate([p.astype(F32) for p in pieces], axis=0).astype(BF16)


def asm_x2(kvp, x1, out):
    out[...] = pack_rows([kvp[0:32], kvp[256:288], x1[0:32], x1[64:96]])


def asm_y1(kvp, x1, x2, out):
    out[...] = pack_rows(
        [kvp[0:16], kvp[256:272], x1[0:16], x1[64:80]] + [x2[32 * j : 32 * j + 16] for j in range(4)]
    )


def asm_y2(kvp, x1, x2, y1, out):
    heads = [kvp[0:16], kvp[256:272], x1[0:16], x1[64:80]]
    heads += [x2[32 * j : 32 * j + 16] for j in range(4)]
    heads += [y1[16 * j : 16 * j + 16] for j in range(8)]
    out[...] = jnp.concatenate([h.astype(F32)[0:8] for h in heads], axis=0).astype(BF16)


def fill_ext(par, kv, c1, n1, kx, vx):
    kx[256:768] = kv[:, 0:128]
    vx[256:768] = kv[:, 128:256]

    @pl.when(par[0] == 0)
    def _():
        kx[0:256] = n1[:, 0:128]
        vx[0:256] = n1[:, 128:256]
        kx[768:1024] = c1[0:256, 0:128]
        vx[768:1024] = c1[0:256, 128:256]

    @pl.when(par[0] == 1)
    def _():
        kx[0:256] = c1[0:256, 0:128]
        vx[0:256] = c1[0:256, 128:256]
        kx[768:1024] = n1[:, 0:128]
        vx[768:1024] = n1[:, 128:256]


def near_chunks(kx, c1, lo):
    return [kx[256:384], kx[512:640], c1[0:128, lo : lo + 128], c1[256:384, lo : lo + 128]]


def near_count():
    s = (128, 128)
    return jnp.minimum(depth(iota(s, 0)), depth(iota(s, 1))).astype(F32)


def fwd_near(pair, off, win, par, tm, qt, kv, c1, n1, pw, p1, acc_out, stat, kx, vx, vt, v1t, k1, dist, sw, s1):
    fill_ext(par, kv, c1, n1, kx, vx)
    vt[...] = transposed(vx[...])
    k1[...] = jnp.concatenate(near_chunks(kx, c1, 0), axis=0)
    v1t[...] = transposed(jnp.concatenate(near_chunks(vx, c1, 128), axis=0))
    count = near_count()
    for a in range(2):
        h = 2 * pair + a
        s = (256, 256)
        dist[...] = place(iota(s, 0), off[h]) - place(iota(s, 1), off[h])
        reach = win[h]
        lo = jnp.where(tm[0] == 0, 1000, 256 - reach)
        hi = jnp.where(tm[0] == 31, -1000, reach - 256)
        for b in range(2):
            qz = zero_pad(qt[64 * a : 64 * a + 64, 256 * b : 256 * b + 256], a)
            top = None
            for c in range(3):
                sc = dot(kx[256 * (b + c) : 256 * (b + c) + 256], qz)
                d = dist[...]
                if c == 0:
                    ok = d >= (lo if b == 0 else 256 - reach)
                elif c == 1:
                    ok = jnp.abs(d) <= reach
                else:
                    ok = d <= (hi if b == 1 else reach - 256)
                sc = jnp.where(ok, sc, NEG)
                sw[256 * c : 256 * c + 256] = sc
                part = jnp.max(sc, axis=0, keepdims=True)
                top = part if top is None else jnp.maximum(top, part)
            sc = dot(k1[...], qz[:, 0:128])
            s1[...] = sc
            near_top = jnp.maximum(top[:, 0:128], jnp.max(sc, axis=0, keepdims=True))
            top = jnp.concatenate([near_top, top[:, 128:256]], axis=1)
            total = jnp.zeros((1, 256), F32)
            for c in range(3):
                e = jnp.exp(sw[256 * c : 256 * c + 256] - top)
                total += jnp.sum(e, axis=0, keepdims=True)
                pw[a, b, 256 * c : 256 * c + 256, :] = e.astype(BF16)
            vh = slice(64 * a, 64 * a + 64)
            acc = dot(vt[vh, 256 * b : 256 * b + 768], pw[a, b])
            near_sum = jnp.zeros((1, 128), F32)
            bs = slice(128 * b, 128 * b + 128)
            for c in range(4):
                e = count * jnp.exp(s1[128 * c : 128 * c + 128] - near_top)
                near_sum += jnp.sum(e, axis=0, keepdims=True)
                p1[a, 128 * c : 128 * c + 128, bs] = e.astype(BF16)
            near_acc = dot(v1t[vh, :], p1[a, :, bs])
            acc_out[vh, 256 * b : 256 * b + 128] = acc[:, 0:128] + near_acc
            acc_out[vh, 256 * b + 128 : 256 * b + 256] = acc[:, 128:256]
            stat[a : a + 1, 256 * b : 256 * b + 256] = top
            stat[2 + a : 3 + a, 256 * b : 256 * b + 128] = total[:, 0:128] + near_sum
            stat[2 + a : 3 + a, 256 * b + 128 : 256 * b + 256] = total[:, 128:256]


def far_count():
    s = (1024, 128)
    j, i = iota(s, 0), iota(s, 1)
    level = 2 + j // 256
    chunk = jnp.where(level == 2, 64, jnp.where(level == 3, 32, jnp.where(level == 4, 16, 8)))
    both = jnp.minimum(depth(j & (chunk - 1)), depth(i & 63))
    return jnp.maximum(both - level + 1, 0).astype(F32)


def far_lanes(x):
    return jnp.concatenate([x[:, 0:64], x[:, 256:320]], axis=1)


def wide(x, b, filler):
    rows = x.shape[0]
    return jnp.concatenate([x[:, 64 * b : 64 * b + 64], jnp.full((rows, 192), filler, F32)], axis=1)


def fwd_far(off, qt, gt, acc0, acc1, st0, st1, *rest):
    bufs, (pf, attn, stat2, kf, vft, mult, at) = rest[:8], rest[8:]
    mult[...] = far_count()
    for pair in range(2):
        acc_in, stat = (acc0, st0) if pair == 0 else (acc1, st1)
        lo, hi = slice(256 * pair, 256 * pair + 128), slice(256 * pair + 128, 256 * pair + 256)
        for j, buf in enumerate(bufs):
            kf[128 * j : 128 * j + 128] = buf[:, lo]
        vft[...] = transposed(jnp.concatenate([buf[:, hi] for buf in bufs], axis=0))
        for a in range(2):
            vh = slice(64 * a, 64 * a + 64)
            h = 2 * pair + a
            hs = slice(64 * h, 64 * h + 64)
            qz = zero_pad(far_lanes(qt[hs, :]), a)
            cnt = mult[...]
            sc = jnp.where(cnt > 0, dot(kf[...], qz), NEG)
            ftop = jnp.max(sc, axis=0, keepdims=True)
            e = cnt * jnp.exp(sc - ftop)
            fsum = jnp.sum(e, axis=0, keepdims=True)
            pf[h] = e.astype(BF16)
            facc = dot(vft[vh, :], pf[h])
            for b in range(2):
                bs = slice(256 * b, 256 * b + 256)
                ntop, nsum = stat[a : a + 1, bs], stat[2 + a : 3 + a, bs]
                ftopw = wide(ftop, b, NEG)
                top = jnp.maximum(ntop, ftopw)
                wn, wf = jnp.exp(ntop - top), jnp.exp(ftopw - top)
                norm = nsum * wn + wide(fsum, b, 0.0) * wf
                acc = acc_in[vh, bs] * wn + wide(facc, b, 0.0) * wf
                o = (acc / norm).astype(BF16)
                at[vh, bs] = o
                stat2[h : h + 1, bs] = wn / norm
                stat2[4 + h : 5 + h, bs] = wf / norm
                stat2[8 + h : 9 + h, bs] = jnp.sum(
                    gt[hs, bs].astype(F32) * o.astype(F32), axis=0, keepdims=True
                )
        unperm_pair(off, pair, at, attn, slice(128 * pair, 128 * pair + 128))


def unperm_pair(off, pair, src, out, lanes):
    keep = lane_first(256)
    first, second = from_depth(off[2 * pair]), from_depth(off[2 * pair + 1])
    for b in range(2):
        x = src[:, 256 * b : 256 * b + 256]
        out[256 * b : 256 * b + 256, lanes] = jnp.where(keep, dot_nt(first, x), dot_nt(second, x)).astype(BF16)


def bwd_far(qt, gt, stat2, pf, *rest):
    bufs, (ret, own_far, dq, kx, vx) = rest[:8], rest[8:]
    for pair in range(2):
        lo, hi = slice(256 * pair, 256 * pair + 128), slice(256 * pair + 128, 256 * pair + 256)
        for j, buf in enumerate(bufs):
            kx[128 * j : 128 * j + 128] = buf[:, lo]
            vx[128 * j : 128 * j + 128] = buf[:, hi]
        kt = transposed(kx[...])
        grads, scaled_q, scaled_g = [], [], []
        for a in range(2):
            h = 2 * pair + a
            hs, vh = slice(64 * h, 64 * h + 64), slice(64 * a, 64 * a + 64)
            cf = far_lanes(stat2[4 + h : 5 + h, :])
            delta = far_lanes(stat2[8 + h : 9 + h, :])
            q, g = far_lanes(qt[hs, :]), far_lanes(gt[hs, :])
            dp = dot(vx[...], zero_pad(g, a))
            ds = (pf[h].astype(F32) * (dp - delta)).astype(BF16)
            grads.append(ds)
            scaled_q.append(zero_pad((q.astype(F32) * cf).astype(BF16), a))
            scaled_g.append(zero_pad((g.astype(F32) * cf).astype(BF16), a))
            dq[hs, :] = dot(kt[vh, :], ds) * cf
        dk = dot_nt(jnp.concatenate(grads, axis=1), jnp.concatenate(scaled_q, axis=1))
        dv = dot_nt(jnp.concatenate([pf[2 * pair], pf[2 * pair + 1]], axis=1), jnp.concatenate(scaled_g, axis=1))
        for j in range(4):
            mine, theirs = slice(256 * j, 256 * j + 128), slice(256 * j + 128, 256 * j + 256)
            rows = slice(128 * j, 128 * j + 128)
            own_far[rows, lo] = dk[mine]
            own_far[rows, hi] = dv[mine]
            ret[rows, lo] = dk[theirs].astype(BF16)
            ret[rows, hi] = dv[theirs].astype(BF16)


def bwd_near_keys(qt, gt, stat2, kv, c1, p10, p11, ret, own_near, dq):
    for pair in range(2):
        p1 = p10 if pair == 0 else p11
        lo, hi = slice(256 * pair, 256 * pair + 128), slice(256 * pair + 128, 256 * pair + 256)
        k1 = jnp.concatenate([kv[0:128, lo], kv[256:384, lo], c1[0:128, lo], c1[256:384, lo]], axis=0)
        v1 = jnp.concatenate([kv[0:128, hi], kv[256:384, hi], c1[0:128, hi], c1[256:384, hi]], axis=0)
        k1t = transposed(k1)
        grads, scaled_q, scaled_g, probs = [], [], [], []
        for a in range(2):
            h = 2 * pair + a
            hs, vh = slice(64 * h, 64 * h + 64), slice(64 * a, 64 * a + 64)
            for b in range(2):
                bs = slice(256 * b, 256 * b + 128)
                cn, delta = stat2[h : h + 1, bs], stat2[8 + h : 9 + h, bs]
                g = gt[hs, bs]
                p = p1[a, :, 128 * b : 128 * b + 128]
                ds = (p.astype(F32) * (dot(v1, zero_pad(g, a)) - delta)).astype(BF16)
                grads.append(ds)
                probs.append(p)
                scaled_q.append(zero_pad((qt[hs, bs].astype(F32) * cn).astype(BF16), a))
                scaled_g.append(zero_pad((g.astype(F32) * cn).astype(BF16), a))
                dq[hs, 128 * b : 128 * b + 128] = dot(k1t[vh, :], ds) * cn
        dk = dot_nt(jnp.concatenate(grads, axis=1), jnp.concatenate(scaled_q, axis=1))
        dv = dot_nt(jnp.concatenate(probs, axis=1), jnp.concatenate(scaled_g, axis=1))
        own_near[:, lo] = dk[0:256]
        own_near[:, hi] = dv[0:256]
        ret[:, lo] = dk[256:512].astype(BF16)
        ret[:, hi] = dv[256:512].astype(BF16)


def bwd_near(pair, off, par, qt, gt, stat2, kv, c1, n1, pw, dqf, dqn, own_near, *rest):
    if pair == 0:
        own, halo_c, halo_n, gq, kx, vx, kt, dk, dv, dqt = rest
        lanes = slice(0, 256)
    else:
        hc0, hn0, gq0, own, halo_c, halo_n, gq, kx, vx, kt, dk, dv, dqt = rest
        halo_c[:, 0:256] = hc0[...]
        halo_n[:, 0:256] = hn0[...]
        gq[:, 0:128] = gq0[...]
        lanes = slice(256, 512)
    fill_ext(par, kv, c1, n1, kx, vx)
    kt[...] = transposed(kx[...])
    dk[...] = jnp.zeros((1024, 128), F32)
    dv[...] = jnp.zeros((1024, 128), F32)
    for (dst, part) in ((dk, slice(0, 128)), (dv, slice(128, 256))):
        dst[256:384] = own_near[0:128, part]
        dst[512:640] = own_near[128:256, part]
    for b in range(2):
        bs = slice(256 * b, 256 * b + 256)
        ext = slice(256 * b, 256 * b + 768)
        for a in range(2):
            h = 2 * pair + a
            vh = slice(64 * a, 64 * a + 64)
            cn, delta = stat2[h : h + 1, bs], stat2[8 + h : 9 + h, bs]
            g = gt[vh, bs]
            dp = dot(vx[ext], zero_pad(g, a))
            p = pw[a, b]
            ds = (p.astype(F32) * (dp - delta)).astype(BF16)
            qs = zero_pad((qt[vh, bs].astype(F32) * cn).astype(BF16), a)
            gs = zero_pad((g.astype(F32) * cn).astype(BF16), a)
            dk[ext] += dot_nt(ds, qs)
            dv[ext] += dot_nt(p, gs)
            near = jnp.concatenate([dqn[vh, 128 * b : 128 * b + 128], jnp.zeros((64, 128), F32)], axis=1)
            total = dot(kt[vh, ext], ds) * cn + near + wide(dqf[vh, :], b, 0.0)
            dqt[vh, bs] = (total * 0.125).astype(BF16)
    own[:, 0:128] = dk[256:768]
    own[:, 128:256] = dv[256:768]
    low = jnp.concatenate([dk[0:256], dv[0:256]], axis=1).astype(BF16)
    high = jnp.concatenate([dk[768:1024], dv[768:1024]], axis=1).astype(BF16)

    @pl.when(par[0] == 0)
    def _():
        halo_n[:, lanes] = low
        halo_c[:, lanes] = high

    @pl.when(par[0] == 1)
    def _():
        halo_c[:, lanes] = low
        halo_n[:, lanes] = high

    unperm_pair(off, pair, dqt, gq, slice(128 * pair, 128 * pair + 128))


def ret_y2(own_far, ret, rest, send):
    total = own_far[...] + ret[...].astype(F32)
    rest[...] = total[0:384]
    send[...] = total[384:512].astype(BF16)


def ret_y1(rest, got, left, send):
    y2 = got[...].astype(F32)
    left[...] = rest[0:256]
    for j in range(2):
        left[64 * j : 64 * j + 8] += y2[16 + 8 * j : 24 + 8 * j]
    for j in range(4):
        left[128 + 32 * j : 136 + 32 * j] += y2[32 + 8 * j : 40 + 8 * j]
    zero = jnp.zeros((8, 512), F32)
    extra = []
    for j in range(8):
        extra += [y2[64 + 8 * j : 72 + 8 * j], zero]
    send[...] = (rest[256:384] + jnp.concatenate(extra, axis=0)).astype(BF16)


def ret_x2(rest, got, left, send):
    y1 = got[...].astype(F32)
    left[...] = rest[0:128]
    for j in range(2):
        left[64 * j : 64 * j + 16] += y1[32 + 16 * j : 48 + 16 * j]
    zero = jnp.zeros((16, 512), F32)
    extra = []
    for j in range(4):
        extra += [y1[64 + 16 * j : 80 + 16 * j], zero]
    send[...] = (rest[128:256] + jnp.concatenate(extra, axis=0)).astype(BF16)


def ret_x1(rest, got, send):
    x2 = got[...].astype(F32)
    zero = jnp.zeros((32, 512), F32)
    extra = [x2[64:96], zero, x2[96:128], zero]
    send[...] = (rest[...] + jnp.concatenate(extra, axis=0)).astype(BF16)


def finish(off, par, own0, own1, ret, hc, hn, y2, y1, x2, x1, gk, gv, acc):
    acc[:, 0:256] = own0[...]
    acc[:, 256:512] = own1[...]
    for b in range(2):
        at = 256 * b
        acc[at : at + 64] += x1[64 * b : 64 * b + 64].astype(F32)
        acc[at : at + 32] += x2[32 * b : 32 * b + 32].astype(F32)
        acc[at : at + 16] += y1[16 * b : 16 * b + 16].astype(F32)
        acc[at : at + 8] += y2[0:16].astype(F32)[8 * b : 8 * b + 8]

    @pl.when(par[0] == 0)
    def _():
        acc[256:512] += hc[...].astype(F32)
        acc[0:256] += hn[...].astype(F32)
        acc[256:384] += ret[0:128].astype(F32)
        acc[0:128] += ret[128:256].astype(F32)

    @pl.when(par[0] == 1)
    def _():
        acc[0:256] += hc[...].astype(F32)
        acc[256:512] += hn[...].astype(F32)
        acc[0:128] += ret[0:128].astype(F32)
        acc[256:384] += ret[128:256].astype(F32)

    keep = lane_first(256, 256)
    for pair in range(2):
        first, second = from_depth(off[2 * pair]), from_depth(off[2 * pair + 1])
        lanes = slice(128 * pair, 128 * pair + 128)
        for b in range(2):
            rows = slice(256 * b, 256 * b + 256)
            x = acc[rows, 256 * pair : 256 * pair + 256].astype(BF16)
            r = jnp.where(keep, dot(first, x), dot(second, x)).astype(BF16)
            gk[rows, lanes] = r[:, 0:128]
            gv[rows, lanes] = r[:, 128:256]


def project(a0, a1, a2, a3, w0, w1, w2, w3, out):
    a = jnp.concatenate([a0[...], a1[...], a2[...], a3[...]], axis=1)
    w = jnp.concatenate([w0[...], w1[...], w2[...], w3[...]], axis=0)
    out[...] = dot(a, w).astype(BF16)


def swap(x, axis, mask):
    return lax.ppermute(x, axis, [(i, i ^ mask) for i in range(lax.axis_size(axis))])


def side(x):
    pairs = [(i, (i + 1) % 32 if i % 2 else (i - 1) % 32) for i in range(32)]
    return lax.ppermute(x, "tm", pairs)


def bind(f, *args):
    def body(*refs):
        f(*args, *refs)

    return body


def layer(q, k, v, w, up, win, off):
    tm = lax.axis_index("tm").astype(jnp.int32).reshape(1)
    par = tm % 2
    VM = pltpu.VMEM
    kvp, c1s, n1s, x1s = call(
        prep_kv, (off, par, k, v),
        [sds((512, 512), BF16), sds((384, 512), BF16), sds((256, 512), BF16), sds((128, 512), BF16)],
        specs=[SMEM, SMEM, None, None], flops=3e8, nbytes=3e6,
    )
    x1 = swap(x1s, "tm", 2)
    c1 = swap(c1s, "tm", 1)
    n1 = side(n1s)
    wa, wb = swap(w, "head", 1), swap(w, "head", 3)
    wc = swap(wa, "head", 3)
    qt, gt = call(
        prep_qg, (off, q, up, w), [sds((256, 512), BF16), sds((256, 512), BF16)],
        specs=[SMEM, None, None, None], flops=6e8, nbytes=3e6,
    )
    x2 = swap(call(asm_x2, (kvp, x1), [sds((128, 512), BF16)])[0], "tm", 6)

    pair_lanes = lambda rows, pair: pl.BlockSpec((rows, 256), lambda *_: (0, pair))
    pair_rows = lambda cols, pair: pl.BlockSpec((128, cols), lambda *_: (pair, 0))
    near = []
    for pair in range(2):
        near.append(
            call(
                bind(fwd_near, pair), (off, win, par, tm, qt, kvp, c1, n1),
                [sds((2, 2, 768, 256), BF16), sds((2, 512, 256), BF16), sds((128, 512), F32), sds((8, 512), F32)],
                specs=[SMEM] * 4 + [pair_rows(512, pair)] + [pair_lanes(r, pair) for r in (512, 384, 256)],
                scratch=[
                    VM((1024, 128), BF16), VM((1024, 128), BF16), VM((128, 1024), BF16), VM((128, 512), BF16),
                    VM((512, 128), BF16), VM((256, 256), jnp.int32), VM((768, 256), F32), VM((512, 128), F32),
                ],
                flops=3e9, nbytes=4e6,
            )
        )
    y1 = swap(call(asm_y1, (kvp, x1, x2), [sds((128, 512), BF16)])[0], "tm", 8)
    y2 = swap(call(asm_y2, (kvp, x1, x2, y1), [sds((128, 512), BF16)])[0], "tm", 24)
    bufs = []
    for mine in (x1, x2, y1, y2):
        bufs += [mine, swap(mine, "tm", 1)]

    pf, attn, stat2 = call(
        fwd_far, (off, qt, gt, near[0][2], near[1][2], near[0][3], near[1][3], *bufs),
        [sds((4, 1024, 128), BF16), sds((512, 256), BF16), sds((16, 512), F32)],
        specs=[SMEM] + [None] * 14,
        scratch=[VM((1024, 128), BF16), VM((128, 1024), BF16), VM((1024, 128), F32), VM((128, 512), BF16)],
        flops=3e9, nbytes=4e6,
    )
    a1, a2 = swap(attn, "head", 1), swap(attn, "head", 3)
    a3 = swap(a1, "head", 3)

    ret_s, own_far, dqf = call(
        bwd_far, (qt, gt, stat2, pf, *bufs),
        [sds((512, 512), BF16), sds((512, 512), F32), sds((256, 128), F32)],
        scratch=[VM((1024, 128), BF16), VM((1024, 128), BF16)], flops=4e9, nbytes=5e6,
    )
    ret = swap(ret_s, "tm", 1)
    near_s, own_near, dqn = call(
        bwd_near_keys, (qt, gt, stat2, kvp, c1, near[0][1], near[1][1]),
        [sds((256, 512), BF16), sds((256, 512), F32), sds((256, 256), F32)],
        flops=4e9, nbytes=5e6,
    )
    near_r = swap(near_s, "tm", 1)
    back = []
    for pair in range(2):
        more = [] if pair == 0 else [back[0][1], back[0][2], back[0][3]]
        wide_out = 256 if pair == 0 else 512
        back.append(
            call(
                bind(bwd_near, pair),
                (off, par, qt, gt, stat2, kvp, c1, n1, near[pair][0], dqf, dqn, own_near, *more),
                [sds((512, 256), F32), sds((256, wide_out), BF16), sds((256, wide_out), BF16), sds((512, wide_out // 2), BF16)],
                specs=[SMEM] * 2 + [pair_rows(512, pair), pair_rows(512, pair), None]
                + [pair_lanes(r, pair) for r in (512, 384, 256)]
                + [None, pair_rows(128, pair), pair_rows(256, pair), pair_lanes(256, pair)] + [None] * len(more),
                scratch=[
                    VM((1024, 128), BF16), VM((1024, 128), BF16), VM((128, 1024), BF16),
                    VM((1024, 128), F32), VM((1024, 128), F32), VM((128, 512), BF16),
                ],
                flops=4e9, nbytes=4e6,
            )
        )
    rest, y2s = call(ret_y2, (own_far, ret), [sds((384, 512), F32), sds((128, 512), BF16)])
    y2r = swap(y2s, "tm", 24)
    rest, y1s = call(ret_y1, (rest, y2r), [sds((256, 512), F32), sds((128, 512), BF16)])
    y1r = swap(y1s, "tm", 8)
    rest, x2s = call(ret_x2, (rest, y1r), [sds((128, 512), F32), sds((128, 512), BF16)])
    x2r = swap(x2s, "tm", 6)
    (x1s,) = call(ret_x1, (rest, x2r), [sds((128, 512), BF16)])
    x1r = swap(x1s, "tm", 2)
    hc = swap(back[1][1], "tm", 1)
    hn = side(back[1][2])
    gk, gv = call(
        finish, (off, par, back[0][0], back[1][0], near_r, hc, hn, y2r, y1r, x2r, x1r),
        [sds((512, 256), BF16), sds((512, 256), BF16)],
        specs=[SMEM] * 2 + [None] * 9, scratch=[VM((512, 512), F32)], flops=3e8, nbytes=3e6,
    )
    (mixed,) = call(project, (attn, a1, a2, a3, w, wa, wb, wc), [sds((512, 1024), BF16)], flops=1e9, nbytes=4e6)
    return mixed, back[1][3], gk, gv


def solution(mesh):
    placed = (P("tm", "head"),) * 3 + (P("head", None), P("tm", None), P("head"), P("head"))
    return jax.shard_map(
        layer,
        mesh=mesh,
        in_specs=placed,
        out_specs=(P("tm", None), P("tm", "head"), P("tm", "head"), P("tm", "head")),
        check_vma=False,
    )
```

```python
import jax
import jax.numpy as jnp
from jax import lax
from jax.experimental import pallas as pl
from jax.experimental.pallas import tpu as pltpu
from jax.sharding import PartitionSpec as P


F32 = jnp.float32
BF16 = jnp.bfloat16
NEG = -1e30
NT = (((1,), (1,)), ((), ()))
SMEM = pl.BlockSpec(memory_space=pltpu.SMEM)


def sds(shape, dtype):
    return jax.ShapeDtypeStruct(shape, dtype)


def dot(a, b):
    return jnp.dot(a, b, preferred_element_type=F32)


def dot_nt(a, b):
    return lax.dot_general(a, b, NT, preferred_element_type=F32)


def call(body, ins, outs, scratch=(), flops=0, nbytes=0, specs=None, out_specs=None, vmem=24):
    full = lambda x: pl.BlockSpec(x.shape, (lambda *_: (0,) * len(x.shape)))
    specs = specs or [None] * len(ins)
    in_specs = [full(x) if s is None else s for x, s in zip(ins, specs)]
    out_specs = out_specs or [full(o) for o in outs]
    return pl.pallas_call(
        body,
        out_shape=outs,
        grid=(1,),
        in_specs=in_specs,
        out_specs=out_specs,
        scratch_shapes=list(scratch),
        cost_estimate=pl.CostEstimate(flops=int(flops), bytes_accessed=int(nbytes), transcendentals=0),
        compiler_params=pltpu.CompilerParams(vmem_limit_bytes=vmem << 20),
    )(*ins)


def iota(shape, axis):
    return lax.broadcasted_iota(jnp.int32, shape, axis)


def place_row(offset):
    n = iota((1, 256), 1)
    u = jnp.where(n >= 128, 2 * (n - 128) + 1, 4 * (n - 64) + 2)
    u = jnp.where(n >= 64, u, 8 * (n - 32) + 4)
    u = jnp.where(n >= 32, u, 16 * (n - 16) + 8)
    u = jnp.where(n >= 16, u, 32 * (n - 8) + 16)
    u = jnp.where(n >= 8, u, 32 * n)
    return (u + offset) & 255


def rank_row(offset):
    u = (iota((1, 256), 1) - offset) & 255
    n = jnp.where((u & 16) != 0, 8 + (u >> 5), u >> 5)
    n = jnp.where((u & 8) != 0, 16 + (u >> 4), n)
    n = jnp.where((u & 4) != 0, 32 + (u >> 3), n)
    n = jnp.where((u & 2) != 0, 64 + (u >> 2), n)
    return jnp.where((u & 1) != 0, 128 + (u >> 1), n)


def depth(n):
    d = jnp.where(n < 64, 2, 1)
    d = jnp.where(n < 32, 3, d)
    d = jnp.where(n < 16, 4, d)
    return jnp.where(n < 8, 5, d)


def to_depth(offset):
    return (iota((256, 256), 0) == rank_row(offset)).astype(F32).astype(BF16)


def from_depth(offset):
    return (iota((256, 256), 0) == place_row(offset)).astype(F32).astype(BF16)


def lane_first(rows, width=128):
    return (iota((rows, width), 1) % 128) < 64


def zero_pad(x, which):
    z = jnp.zeros_like(x)
    return jnp.concatenate([x, z] if which == 0 else [z, x], axis=0)


def transposed(x):
    return x.astype(F32).T.astype(BF16)


def parity(tm):
    return tm[0] & 1


def block_rows(tm, which):
    block = (1 - parity(tm)) if which == 0 else parity(tm)
    return pl.ds(pl.multiple_of(256 * block, 256), 256)


def prep_kv(off, tm, k, v, q, up, w, kvp, c1, n1, x1, qv, upv, wv, kb, vb, sem):
    copies = []
    for src, dst in ((k, kb), (v, vb), (q, qv), (up, upv)):
        for which in range(2):
            copies.append(
                pltpu.make_async_copy(
                    src.at[block_rows(tm, which)], dst.at[pl.ds(256 * which, 256)], sem.at[len(copies)]
                )
            )
    copies.append(pltpu.make_async_copy(w, wv, sem.at[8]))
    for c in copies:
        c.start()
    perms = [to_depth(off[h]) for h in range(4)]
    for c in copies[:4]:
        c.wait()
    keep = lane_first(256, 256)
    for pair in range(2):
        lanes = slice(pair * 128, pair * 128 + 128)
        for b in range(2):
            rows = slice(b * 256, b * 256 + 256)
            kv = jnp.concatenate([kb[rows, lanes], vb[rows, lanes]], axis=1)
            kvp[rows, pair * 256 : pair * 256 + 256] = jnp.where(
                keep, dot(perms[2 * pair], kv), dot(perms[2 * pair + 1], kv)
            ).astype(BF16)
    x1[0:64] = kvp[0:64]
    x1[64:128] = kvp[256:320]
    c1[...] = kvp[0:384]
    n1[...] = kvp[256:512]
    for c in copies[4:]:
        c.wait()


def prep_qg(off, q, up, w, qt, gt):
    g = dot_nt(w[...], up[...]).astype(BF16)
    qs = (q[...].astype(F32) * 0.125).T.astype(BF16)
    for h in range(4):
        perm = from_depth(off[h])
        hs = slice(64 * h, 64 * h + 64)
        for b in range(2):
            bs = slice(256 * b, 256 * b + 256)
            x = jnp.concatenate([qs[hs, bs], g[hs, bs]], axis=0)
            r = dot(x, perm).astype(BF16)
            qt[b, hs] = r[0:64]
            gt[b, hs] = r[64:128]


def pack_rows(pieces):
    return jnp.concatenate([p.astype(F32) for p in pieces], axis=0).astype(BF16)


def asm_x2(kvp, x1, out):
    out[...] = pack_rows([kvp[0:32], kvp[256:288], x1[0:32], x1[64:96]])


def asm_y1(kvp, x1, x2, out):
    out[...] = pack_rows(
        [kvp[0:16], kvp[256:272], x1[0:16], x1[64:80]] + [x2[32 * j : 32 * j + 16] for j in range(4)]
    )


def asm_y2(kvp, x1, x2, y1, out):
    heads = [kvp[0:16], kvp[256:272], x1[0:16], x1[64:80]]
    heads += [x2[32 * j : 32 * j + 16] for j in range(4)]
    heads += [y1[16 * j : 16 * j + 16] for j in range(8)]
    out[...] = jnp.concatenate([h.astype(F32)[0:8] for h in heads], axis=0).astype(BF16)


def near_count():
    s = (128, 128)
    return jnp.minimum(depth(iota(s, 0)), depth(iota(s, 1))).astype(F32)


def near_keys(kv, c1, lanes):
    return jnp.concatenate([kv[0:128, lanes], kv[256:384, lanes], c1[0:128, lanes], c1[256:384, lanes]], axis=0)


def pair_slices(pair):
    return slice(256 * pair, 256 * pair + 128), slice(256 * pair + 128, 256 * pair + 256)


def side_chunks(which, kv, halo, lanes):
    own, other = slice(256 * which, 256 * which + 256), slice(256 - 256 * which, 512 - 256 * which)
    return [halo[0:256, lanes], kv[own, lanes], kv[other, lanes]]


def fwd_near(which, off, win, tm, qt, kv, c1, *rest):
    if which == 0:
        halo = c1
        pw, p1, acc_out, stat, vt, v1t, k1, dist, sw, s1 = rest
    else:
        halo, pw, p1, acc_out, stat, vt, v1t, k1, dist, sw, s1 = rest
    count = near_count()
    sign = (1 - 2 * parity(tm)) * (1 if which == 0 else -1)
    for h in range(4):
        a, pair = h % 2, h // 2
        lo, hi = pair_slices(pair)
        if a == 0:
            vt[...] = transposed(jnp.concatenate(side_chunks(which, kv, halo, hi), axis=0))
            k1[...] = near_keys(kv, c1, lo)
            v1t[...] = transposed(near_keys(kv, c1, hi))
        row = place_row(off[h]).astype(F32) * sign.astype(F32)
        col = jnp.broadcast_to(row, (128, 256)).T
        dist[...] = jnp.concatenate([col, col], axis=1) - row
        reach = win[h].astype(F32)
        if which == 0:
            outer = reach - 256.0
        else:
            outer = jnp.where((tm[0] == 0) | (tm[0] == 31), -1000.0, reach - 256.0)
        qz = zero_pad(qt[which, 64 * h : 64 * h + 64, :], a)
        top = None
        for c, keys in enumerate(side_chunks(which, kv, halo, lo)):
            sc = dot(keys, qz)
            d = dist[...]
            ok = (d <= outer, jnp.abs(d) <= reach, d >= 256.0 - reach)[c]
            sc = jnp.where(ok, sc, NEG)
            sw[256 * c : 256 * c + 256] = sc
            part = jnp.max(sc, axis=0, keepdims=True)
            top = part if top is None else jnp.maximum(top, part)
        sc = dot(k1[...], qz[:, 0:128])
        s1[...] = sc
        near_top = jnp.maximum(top[:, 0:128], jnp.max(sc, axis=0, keepdims=True))
        top = jnp.concatenate([near_top, top[:, 128:256]], axis=1)
        total = jnp.zeros((1, 256), F32)
        for c in range(3):
            e = jnp.exp(sw[256 * c : 256 * c + 256] - top)
            total += jnp.sum(e, axis=0, keepdims=True)
            pw[h, 256 * c : 256 * c + 256, :] = e.astype(BF16)
        vh, hs = slice(64 * a, 64 * a + 64), slice(64 * h, 64 * h + 64)
        acc = dot(vt[vh, :], pw[h])
        near_sum = jnp.zeros((1, 128), F32)
        for c in range(4):
            e = count * jnp.exp(s1[128 * c : 128 * c + 128] - near_top)
            near_sum += jnp.sum(e, axis=0, keepdims=True)
            p1[h, 128 * c : 128 * c + 128, :] = e.astype(BF16)
        near_acc = dot(v1t[vh, :], p1[h])
        acc_out[hs, 0:128] = acc[:, 0:128] + near_acc
        acc_out[hs, 128:256] = acc[:, 128:256]
        stat[h : h + 1, :] = top
        stat[4 + h : 5 + h, 0:128] = total[:, 0:128] + near_sum
        stat[4 + h : 5 + h, 128:256] = total[:, 128:256]


def far_count(level):
    s = (256 >> level, 128)
    both = jnp.minimum(depth(iota(s, 0)), depth(iota(s, 1) & 63))
    return jnp.maximum(both - level + 1, 0).astype(F32)


def far_lanes(x):
    return jnp.concatenate([x[:, 0:64], x[:, 256:320]], axis=1)


def far_cols(x, hs):
    return jnp.concatenate([x[0, hs, 0:64], x[1, hs, 0:64]], axis=1)


def wide(x, b, filler):
    rows = x.shape[0]
    return jnp.concatenate([x[:, 64 * b : 64 * b + 64], jnp.full((rows, 192), filler, F32)], axis=1)


def unperm_pair(off, pair, src):
    first, second = from_depth(off[2 * pair]), from_depth(off[2 * pair + 1])
    return jnp.where(lane_first(256), dot_nt(first, src), dot_nt(second, src)).astype(BF16)


def fwd_far(off, qt, gt, acc0, acc1, st0, st1, *rest):
    bufs, (pf, attn, stat2, kf, vft, mult, at) = rest[:8], rest[8:]
    for level in range(2, 6):
        n = 256 >> level
        piece = far_count(level)
        for j in range(256 // n):
            mult[256 * (level - 2) + n * j : 256 * (level - 2) + n * j + n] = piece
    for pair in range(2):
        lo, hi = pair_slices(pair)
        for j, buf in enumerate(bufs):
            kf[128 * j : 128 * j + 128] = buf[:, lo]
        vft[...] = transposed(jnp.concatenate([buf[:, hi] for buf in bufs], axis=0))
        for a in range(2):
            vh = slice(64 * a, 64 * a + 64)
            h = 2 * pair + a
            hs = slice(64 * h, 64 * h + 64)
            qz = zero_pad(far_cols(qt, hs), a)
            cnt = mult[...]
            sc = jnp.where(cnt > 0, dot(kf[...], qz), NEG)
            ftop = jnp.max(sc, axis=0, keepdims=True)
            e = cnt * jnp.exp(sc - ftop)
            fsum = jnp.sum(e, axis=0, keepdims=True)
            pf[h] = e.astype(BF16)
            facc = dot(vft[vh, :], pf[h])
            for b in range(2):
                bs = slice(256 * b, 256 * b + 256)
                acc_in, stat = (acc0, st0) if b == 0 else (acc1, st1)
                ntop, nsum = stat[h : h + 1, :], stat[4 + h : 5 + h, :]
                ftopw = wide(ftop, b, NEG)
                top = jnp.maximum(ntop, ftopw)
                wn, wf = jnp.exp(ntop - top), jnp.exp(ftopw - top)
                norm = nsum * wn + wide(fsum, b, 0.0) * wf
                acc = acc_in[hs, :] * wn + wide(facc, b, 0.0) * wf
                o = (acc / norm).astype(BF16)
                at[vh, bs] = o
                stat2[h : h + 1, bs] = wn / norm
                stat2[4 + h : 5 + h, bs] = wf / norm
                stat2[8 + h : 9 + h, bs] = jnp.sum(
                    gt[b, hs].astype(F32) * o.astype(F32), axis=0, keepdims=True
                )
        for b in range(2):
            bs = slice(256 * b, 256 * b + 256)
            attn[bs, 128 * pair : 128 * pair + 128] = unperm_pair(off, pair, at[:, bs])


def bwd_far(qt, gt, stat2, pf, *rest):
    bufs, (ret, own_far, dq, kx, vx) = rest[:8], rest[8:]
    for pair in range(2):
        lo, hi = pair_slices(pair)
        for j, buf in enumerate(bufs):
            kx[128 * j : 128 * j + 128] = buf[:, lo]
            vx[128 * j : 128 * j + 128] = buf[:, hi]
        kt = transposed(kx[...])
        grads, scaled_q, scaled_g = [], [], []
        for a in range(2):
            h = 2 * pair + a
            hs, vh = slice(64 * h, 64 * h + 64), slice(64 * a, 64 * a + 64)
            cf = far_lanes(stat2[4 + h : 5 + h, :])
            delta = far_lanes(stat2[8 + h : 9 + h, :])
            q, g = far_cols(qt, hs), far_cols(gt, hs)
            dp = dot(vx[...], zero_pad(g, a))
            ds = (pf[h].astype(F32) * (dp - delta)).astype(BF16)
            grads.append(ds)
            scaled_q.append(zero_pad((q.astype(F32) * cf).astype(BF16), a))
            scaled_g.append(zero_pad((g.astype(F32) * cf).astype(BF16), a))
            dq[hs, :] = dot(kt[vh, :], ds) * cf
        dk = dot_nt(jnp.concatenate(grads, axis=1), jnp.concatenate(scaled_q, axis=1))
        dv = dot_nt(jnp.concatenate([pf[2 * pair], pf[2 * pair + 1]], axis=1), jnp.concatenate(scaled_g, axis=1))
        for j in range(4):
            mine, theirs = slice(256 * j, 256 * j + 128), slice(256 * j + 128, 256 * j + 256)
            rows = slice(128 * j, 128 * j + 128)
            own_far[rows, lo] = dk[mine]
            own_far[rows, hi] = dv[mine]
            ret[rows, lo] = dk[theirs].astype(BF16)
            ret[rows, hi] = dv[theirs].astype(BF16)


def bwd_keys(qt, gt, stat2, kv, c1, p10, p11, ret, own_near, dq):
    for pair in range(2):
        lo, hi = pair_slices(pair)
        k1t = transposed(near_keys(kv, c1, lo))
        v1 = near_keys(kv, c1, hi)
        grads, scaled_q, scaled_g, probs = [], [], [], []
        for a in range(2):
            h = 2 * pair + a
            hs, vh = slice(64 * h, 64 * h + 64), slice(64 * a, 64 * a + 64)
            for b in range(2):
                bs = slice(256 * b, 256 * b + 128)
                cn, delta = stat2[h : h + 1, bs], stat2[8 + h : 9 + h, bs]
                g = gt[b, hs, 0:128]
                p = (p10 if b == 0 else p11)[h]
                ds = (p.astype(F32) * (dot(v1, zero_pad(g, a)) - delta)).astype(BF16)
                grads.append(ds)
                probs.append(p)
                scaled_q.append(zero_pad((qt[b, hs, 0:128].astype(F32) * cn).astype(BF16), a))
                scaled_g.append(zero_pad((g.astype(F32) * cn).astype(BF16), a))
                dq[hs, 128 * b : 128 * b + 128] = dot(k1t[vh, :], ds) * cn
        dk = dot_nt(jnp.concatenate(grads, axis=1), jnp.concatenate(scaled_q, axis=1))
        dv = dot_nt(jnp.concatenate(probs, axis=1), jnp.concatenate(scaled_g, axis=1))
        own_near[:, lo] = dk[0:256]
        own_near[:, hi] = dv[0:256]
        ret[:, lo] = dk[256:512].astype(BF16)
        ret[:, hi] = dv[256:512].astype(BF16)


def bwd_near(which, off, tm, qt, gt, stat2, kv, halo, pw, dqf, dqn, *rest):
    if which == 1:
        own, halo_out, gq, dqt = rest
    else:
        own_in, own_near, gq_in, own, halo_out, gq, dqt = rest
        gq[block_rows(tm, 1), :] = gq_in[...]
    bs = slice(256 * which, 256 * which + 256)
    ob = slice(256 - 256 * which, 512 - 256 * which)
    for pair in range(2):
        lo, hi = pair_slices(pair)
        vx = jnp.concatenate(side_chunks(which, kv, halo, hi), axis=0)
        kt = transposed(jnp.concatenate(side_chunks(which, kv, halo, lo), axis=0))
        grads, scaled_q, scaled_g = [], [], []
        for a in range(2):
            h = 2 * pair + a
            hs, vh = slice(64 * h, 64 * h + 64), slice(64 * a, 64 * a + 64)
            cn, delta = stat2[h : h + 1, bs], stat2[8 + h : 9 + h, bs]
            g = gt[which, hs]
            dp = dot(vx, zero_pad(g, a))
            ds = (pw[h].astype(F32) * (dp - delta)).astype(BF16)
            grads.append(ds)
            scaled_q.append(zero_pad((qt[which, hs].astype(F32) * cn).astype(BF16), a))
            scaled_g.append(zero_pad((g.astype(F32) * cn).astype(BF16), a))
            near = jnp.concatenate(
                [dqn[hs, 128 * which : 128 * which + 128], jnp.zeros((64, 128), F32)], axis=1
            )
            total = dot(kt[vh, :], ds) * cn + near + wide(dqf[hs, :], which, 0.0)
            dqt[vh, :] = (total * 0.125).astype(BF16)
        probs = jnp.concatenate([pw[2 * pair], pw[2 * pair + 1]], axis=1)
        for lanes, left, right in ((lo, jnp.concatenate(grads, axis=1), scaled_q), (hi, probs, scaled_g)):
            d = dot_nt(left, jnp.concatenate(right, axis=1))
            halo_out[:, lanes] = d[0:256].astype(BF16)
            if which == 1:
                own[bs, lanes] = d[256:512]
                own[ob, lanes] = d[512:768]
            else:
                own[bs, lanes] = d[256:512] + own_in[bs, lanes]
                own[ob, lanes] = d[512:768] + own_in[ob, lanes]
                own[0:128, lanes] += own_near[0:128, lanes]
                own[256:384, lanes] += own_near[128:256, lanes]
        r = unperm_pair(off, pair, dqt[...])
        if which == 1:
            gq[:, 128 * pair : 128 * pair + 128] = r
        else:
            gq[block_rows(tm, 0), 128 * pair : 128 * pair + 128] = r


def ret_y2(own_far, ret, rest, send):
    total = own_far[...] + ret[...].astype(F32)
    rest[...] = total[0:384]
    send[...] = total[384:512].astype(BF16)


def ret_y1(rest, got, left, send):
    y2 = got[...].astype(F32)
    left[...] = rest[0:256]
    for j in range(2):
        left[64 * j : 64 * j + 8] += y2[16 + 8 * j : 24 + 8 * j]
    for j in range(4):
        left[128 + 32 * j : 136 + 32 * j] += y2[32 + 8 * j : 40 + 8 * j]
    zero = jnp.zeros((8, 512), F32)
    extra = []
    for j in range(8):
        extra += [y2[64 + 8 * j : 72 + 8 * j], zero]
    send[...] = (rest[256:384] + jnp.concatenate(extra, axis=0)).astype(BF16)


def ret_x2(rest, got, left, send):
    y1 = got[...].astype(F32)
    left[...] = rest[0:128]
    for j in range(2):
        left[64 * j : 64 * j + 16] += y1[32 + 16 * j : 48 + 16 * j]
    zero = jnp.zeros((16, 512), F32)
    extra = []
    for j in range(4):
        extra += [y1[64 + 16 * j : 80 + 16 * j], zero]
    send[...] = (rest[128:256] + jnp.concatenate(extra, axis=0)).astype(BF16)


def ret_x1(rest, got, send):
    x2 = got[...].astype(F32)
    zero = jnp.zeros((32, 512), F32)
    extra = [x2[64:96], zero, x2[96:128], zero]
    send[...] = (rest[...] + jnp.concatenate(extra, axis=0)).astype(BF16)


def gather_own(own, near_r, hc, hn, y2, y1, x2, acc):
    acc[...] = own[...]
    acc[0:256] += hc[...].astype(F32)
    acc[256:512] += hn[...].astype(F32)
    for b in range(2):
        at = 256 * b
        acc[at : at + 128] += near_r[128 * b : 128 * b + 128].astype(F32)
        acc[at : at + 32] += x2[32 * b : 32 * b + 32].astype(F32)
        acc[at : at + 16] += y1[16 * b : 16 * b + 16].astype(F32)
        acc[at : at + 8] += y2[0:16].astype(F32)[8 * b : 8 * b + 8]


def finish(off, tm, acc, x1, gk, gv):
    keep = lane_first(256, 256)
    for pair in range(2):
        first, second = from_depth(off[2 * pair]), from_depth(off[2 * pair + 1])
        lanes = slice(128 * pair, 128 * pair + 128)
        cols = slice(256 * pair, 256 * pair + 256)
        for b in range(2):
            at = 256 * b
            head = acc[at : at + 64, cols] + x1[64 * b : 64 * b + 64, cols].astype(F32)
            x = jnp.concatenate([head, acc[at + 64 : at + 256, cols]], axis=0).astype(BF16)
            r = jnp.where(keep, dot(first, x), dot(second, x)).astype(BF16)
            gk[block_rows(tm, b), lanes] = r[:, 0:128]
            gv[block_rows(tm, b), lanes] = r[:, 128:256]


def project(attn, w, ma, mb):
    ma[...] = dot(attn[0:256], w[...]).astype(BF16)
    mb[...] = dot(attn[256:512], w[...]).astype(BF16)


def add_first(ma, mb, ra, rb, sa, sb):
    sa[...] = (ma[...].astype(F32) + ra[...].astype(F32)).astype(BF16)
    sb[...] = (mb[...].astype(F32) + rb[...].astype(F32)).astype(BF16)


def add_second(tm, ma, mb, ra, rb, out):
    out[block_rows(tm, 0), :] = (ma[...].astype(F32) + ra[...].astype(F32)).astype(BF16)
    out[block_rows(tm, 1), :] = (mb[...].astype(F32) + rb[...].astype(F32)).astype(BF16)


def swap(x, axis, mask):
    return lax.ppermute(x, axis, [(i, i ^ mask) for i in range(lax.axis_size(axis))])


def side(x):
    pairs = [(i, (i + 1) % 32 if i % 2 else (i - 1) % 32) for i in range(32)]
    return lax.ppermute(x, "tm", pairs)


def bind(f, *args):
    def body(*refs):
        f(*args, *refs)

    return body


def layer(q, k, v, w, up, win, off):
    tm = lax.axis_index("tm").astype(jnp.int32).reshape(1)
    VM = pltpu.VMEM
    hbm = pl.BlockSpec(memory_space=pltpu.HBM)
    kvp, c1s, n1s, x1s, qv, upv, wv = call(
        prep_kv, (off, tm) + tuple(pltpu.with_memory_space_constraint(x, pltpu.HBM) for x in (k, v, q, up, w)),
        [sds((512, 512), BF16), sds((384, 512), BF16), sds((256, 512), BF16), sds((128, 512), BF16),
         sds((512, 256), BF16), sds((512, 1024), BF16), sds((256, 1024), BF16)],
        specs=[SMEM, SMEM] + [hbm] * 5,
        scratch=[VM((512, 256), BF16), VM((512, 256), BF16), pltpu.SemaphoreType.DMA((9,))],
        flops=3e8, nbytes=3e6,
    )
    x1 = swap(x1s, "tm", 2)
    c1 = swap(c1s, "tm", 1)
    n1 = side(n1s)
    qt, gt = call(
        prep_qg, (off, qv, upv, wv), [sds((2, 256, 256), BF16), sds((2, 256, 256), BF16)],
        specs=[SMEM, None, None, None], flops=6e8, nbytes=3e6,
    )
    x2 = swap(call(asm_x2, (kvp, x1), [sds((128, 512), BF16)])[0], "tm", 6)
    near = []
    for which in range(2):
        near.append(
            call(
                bind(fwd_near, which), (off, win, tm, qt, kvp, c1) + ((n1,) if which else ()),
                [sds((4, 768, 256), BF16), sds((4, 512, 128), BF16), sds((256, 256), F32), sds((8, 256), F32)],
                specs=[SMEM] * 3 + [None] * (3 + which),
                scratch=[
                    VM((128, 768), BF16), VM((128, 512), BF16), VM((512, 128), BF16), VM((256, 256), F32),
                    VM((768, 256), F32), VM((512, 128), F32),
                ],
                flops=3e9, nbytes=4e6,
            )
        )
    y1 = swap(call(asm_y1, (kvp, x1, x2), [sds((128, 512), BF16)])[0], "tm", 8)
    y2 = swap(call(asm_y2, (kvp, x1, x2, y1), [sds((128, 512), BF16)])[0], "tm", 24)
    bufs = []
    for mine in (x1, x2, y1, y2):
        bufs += [mine, swap(mine, "tm", 1)]
    pf, attn, stat2 = call(
        fwd_far, (off, qt, gt, near[0][2], near[1][2], near[0][3], near[1][3], *bufs),
        [sds((4, 1024, 128), BF16), sds((512, 256), BF16), sds((16, 512), F32)],
        specs=[SMEM] + [None] * 14,
        scratch=[VM((1024, 128), BF16), VM((128, 1024), BF16), VM((1024, 128), F32), VM((128, 512), BF16)],
        flops=3e9, nbytes=4e6,
    )
    ma, mb = call(project, (attn, wv), [sds((256, 1024), BF16)] * 2, flops=3e8, nbytes=2e6)
    sa, sb = call(
        add_first, (ma, mb, swap(ma, "head", 1), swap(mb, "head", 3)),
        [sds((256, 1024), BF16)] * 2, nbytes=3e6,
    )
    (mixed,) = call(
        add_second, (tm, sa, sb, swap(sa, "head", 3), swap(sb, "head", 1)),
        [sds((512, 1024), BF16)], specs=[SMEM] + [None] * 4, nbytes=3e6,
    )
    ret_s, own_far, dqf = call(
        bwd_far, (qt, gt, stat2, pf, *bufs),
        [sds((512, 512), BF16), sds((512, 512), F32), sds((256, 128), F32)],
        scratch=[VM((1024, 128), BF16), VM((1024, 128), BF16)], flops=4e9, nbytes=5e6,
    )
    ret = swap(ret_s, "tm", 1)
    near_s, own_near, dqn = call(
        bwd_keys, (qt, gt, stat2, kvp, c1, near[0][1], near[1][1]),
        [sds((256, 512), BF16), sds((256, 512), F32), sds((256, 256), F32)],
        flops=4e9, nbytes=5e6,
    )
    near_r = swap(near_s, "tm", 1)

    def back(which, halo, gq_rows, more):
        return call(
            bind(bwd_near, which), (off, tm, qt, gt, stat2, kvp, halo, near[which][0], dqf, dqn, *more),
            [sds((512, 512), F32), sds((256, 512), BF16), sds((gq_rows, 256), BF16)],
            specs=[SMEM] * 2 + [None] * (8 + len(more)),
            scratch=[VM((128, 256), BF16)], flops=4e9, nbytes=4e6,
        )

    own1, hn_s, gq1 = back(1, n1, 256, ())
    own, hc_s, gq = back(0, c1, 512, (own1, own_near, gq1))
    rest, y2s = call(ret_y2, (own_far, ret), [sds((384, 512), F32), sds((128, 512), BF16)])
    y2r = swap(y2s, "tm", 24)
    rest, y1s = call(ret_y1, (rest, y2r), [sds((256, 512), F32), sds((128, 512), BF16)])
    y1r = swap(y1s, "tm", 8)
    rest, x2s = call(ret_x2, (rest, y1r), [sds((128, 512), F32), sds((128, 512), BF16)])
    x2r = swap(x2s, "tm", 6)
    (x1s,) = call(ret_x1, (rest, x2r), [sds((128, 512), BF16)])
    x1r = swap(x1s, "tm", 2)
    hc, hn = swap(hc_s, "tm", 1), side(hn_s)
    (acc,) = call(gather_own, (own, near_r, hc, hn, y2r, y1r, x2r), [sds((512, 512), F32)], nbytes=3e6)
    gk, gv = call(
        finish, (off, tm, acc, x1r), [sds((512, 256), BF16), sds((512, 256), BF16)],
        specs=[SMEM] * 2 + [None] * 2, flops=3e8, nbytes=3e6,
    )
    return mixed, gq, gk, gv


def solution(mesh):
    placed = (P("tm", "head"),) * 3 + (P("head", None), P("tm", None), P("head"), P("head"))
    return jax.shard_map(
        layer,
        mesh=mesh,
        in_specs=placed,
        out_specs=(P("tm", None), P("tm", "head"), P("tm", "head"), P("tm", "head")),
        check_vma=False,
    )
```

```python
import jax
import jax.numpy as jnp
from jax import lax
from jax.experimental import pallas as pl
from jax.experimental.pallas import tpu as pltpu
from jax.sharding import PartitionSpec as P


F32 = jnp.float32
BF16 = jnp.bfloat16
NEG = -1e30
NT = (((1,), (1,)), ((), ()))
SMEM = pl.BlockSpec(memory_space=pltpu.SMEM)


def sds(shape, dtype):
    return jax.ShapeDtypeStruct(shape, dtype)


def dot(a, b):
    return jnp.dot(a, b, preferred_element_type=F32)


def dot_nt(a, b):
    return lax.dot_general(a, b, NT, preferred_element_type=F32)


def call(body, ins, outs, scratch=(), flops=0, nbytes=0, specs=None, out_specs=None, vmem=24):
    full = lambda x: pl.BlockSpec(x.shape, (lambda *_: (0,) * len(x.shape)))
    specs = specs or [None] * len(ins)
    in_specs = [full(x) if s is None else s for x, s in zip(ins, specs)]
    out_specs = out_specs or [full(o) for o in outs]
    return pl.pallas_call(
        body,
        out_shape=outs,
        grid=(1,),
        in_specs=in_specs,
        out_specs=out_specs,
        scratch_shapes=list(scratch),
        cost_estimate=pl.CostEstimate(flops=int(flops), bytes_accessed=int(nbytes), transcendentals=0),
        compiler_params=pltpu.CompilerParams(vmem_limit_bytes=vmem << 20),
    )(*ins)


def iota(shape, axis):
    return lax.broadcasted_iota(jnp.int32, shape, axis)


def place_row(offset):
    n = iota((1, 256), 1)
    u = jnp.where(n >= 128, 2 * (n - 128) + 1, 4 * (n - 64) + 2)
    u = jnp.where(n >= 64, u, 8 * (n - 32) + 4)
    u = jnp.where(n >= 32, u, 16 * (n - 16) + 8)
    u = jnp.where(n >= 16, u, 32 * (n - 8) + 16)
    u = jnp.where(n >= 8, u, 32 * n)
    return (u + offset) & 255


def rank_row(offset):
    u = (iota((1, 256), 1) - offset) & 255
    n = jnp.where((u & 16) != 0, 8 + (u >> 5), u >> 5)
    n = jnp.where((u & 8) != 0, 16 + (u >> 4), n)
    n = jnp.where((u & 4) != 0, 32 + (u >> 3), n)
    n = jnp.where((u & 2) != 0, 64 + (u >> 2), n)
    return jnp.where((u & 1) != 0, 128 + (u >> 1), n)


def depth(n):
    d = jnp.where(n < 64, 2, 1)
    d = jnp.where(n < 32, 3, d)
    d = jnp.where(n < 16, 4, d)
    return jnp.where(n < 8, 5, d)


def to_depth(offset):
    return (iota((256, 256), 0) == rank_row(offset)).astype(F32).astype(BF16)


def from_depth(offset):
    return (iota((256, 256), 0) == place_row(offset)).astype(F32).astype(BF16)


def lane_first(rows, width=128):
    return (iota((rows, width), 1) % 128) < 64


def zero_pad(x, which):
    z = jnp.zeros_like(x)
    return jnp.concatenate([x, z] if which == 0 else [z, x], axis=0)


def transposed(x):
    return x.astype(F32).T.astype(BF16)


def parity(tm):
    return tm[0] & 1


def block_rows(tm, which):
    block = (1 - parity(tm)) if which == 0 else parity(tm)
    return pl.ds(pl.multiple_of(256 * block, 256), 256)


def prep_kv(off, tm, k, v, q, up, w, kvp, c1, n1, x1, x2, qv, upv, wv, kb, vb, sem):
    copies = []
    for src, dst in ((k, kb), (v, vb), (q, qv), (up, upv)):
        for which in range(2):
            copies.append(
                pltpu.make_async_copy(
                    src.at[block_rows(tm, which)], dst.at[pl.ds(256 * which, 256)], sem.at[len(copies)]
                )
            )
    copies.append(pltpu.make_async_copy(w, wv, sem.at[8]))
    for c in copies:
        c.start()
    perms = [to_depth(off[h]) for h in range(4)]
    for c in copies[:4]:
        c.wait()
    keep = lane_first(256, 256)
    for pair in range(2):
        lanes = slice(pair * 128, pair * 128 + 128)
        for b in range(2):
            rows = slice(b * 256, b * 256 + 256)
            kv = jnp.concatenate([kb[rows, lanes], vb[rows, lanes]], axis=1)
            kvp[rows, pair * 256 : pair * 256 + 256] = jnp.where(
                keep, dot(perms[2 * pair], kv), dot(perms[2 * pair + 1], kv)
            ).astype(BF16)
    x1[0:64] = kvp[0:64]
    x1[64:128] = kvp[256:320]
    x2[0:32] = kvp[0:32]
    x2[32:64] = kvp[256:288]
    c1[...] = kvp[0:384]
    n1[...] = kvp[256:512]
    for c in copies[4:]:
        c.wait()


def prep_qg(off, q, up, w, qt, gt):
    g = dot_nt(w[...], up[...]).astype(BF16)
    qs = (q[...].astype(F32) * 0.125).T.astype(BF16)
    for h in range(4):
        perm = from_depth(off[h])
        hs = slice(64 * h, 64 * h + 64)
        for b in range(2):
            bs = slice(256 * b, 256 * b + 256)
            x = jnp.concatenate([qs[hs, bs], g[hs, bs]], axis=0)
            r = dot(x, perm).astype(BF16)
            qt[b, hs] = r[0:64]
            gt[b, hs] = r[64:128]


def asm_y(kvp, x1, x2a, x2b, y1, y2, both):
    heads = [kvp[0:16], kvp[256:272], x1[0:16], x1[64:80], x2a[0:16], x2a[32:48], x2b[0:16], x2b[32:48]]
    heads = [h.astype(F32) for h in heads]
    y1[...] = jnp.concatenate(heads, axis=0).astype(BF16)
    y2[...] = jnp.concatenate([h[0:8] for h in heads], axis=0).astype(BF16)
    stack(x1, x2a, x2b, both)


def stack(*refs):
    out, at = refs[-1], 0
    for ref in refs[:-1]:
        out[at : at + ref.shape[0]] = ref[...]
        at += ref.shape[0]


def beside(left, right, out):
    out[:, 0 : left.shape[1]] = left[...]
    out[:, left.shape[1] :] = right[...]


def far_rows(bufs, lanes):
    mine_x, other_x, mine_y, other_y = bufs
    out = []
    for mine, other in ((mine_x, other_x), (mine_y, other_y)):
        for half in (slice(0, 128), slice(128, 256)):
            out += [mine[half, lanes], other[half, lanes]]
    return jnp.concatenate(out, axis=0)


def near_count():
    s = (128, 128)
    return jnp.minimum(depth(iota(s, 0)), depth(iota(s, 1))).astype(F32)


def near_keys(kv, c1, lanes):
    return jnp.concatenate([kv[0:128, lanes], kv[256:384, lanes], c1[0:128, lanes], c1[256:384, lanes]], axis=0)


def pair_slices(pair):
    return slice(256 * pair, 256 * pair + 128), slice(256 * pair + 128, 256 * pair + 256)


def side_chunks(which, kv, halo, lanes):
    own, other = slice(256 * which, 256 * which + 256), slice(256 - 256 * which, 512 - 256 * which)
    return [halo[0:256, lanes], kv[own, lanes], kv[other, lanes]]


def fwd_near(which, off, win, tm, qt, kv, c1, *rest):
    if which == 0:
        halo = c1
        pw, p1, acc_out, stat, vt, v1t, k1, dist, sw, s1 = rest
    else:
        halo, pw, p1, acc_out, stat, vt, v1t, k1, dist, sw, s1 = rest
    count = near_count()
    sign = (1 - 2 * parity(tm)) * (1 if which == 0 else -1)
    for h in range(4):
        a, pair = h % 2, h // 2
        lo, hi = pair_slices(pair)
        if a == 0:
            vt[...] = transposed(jnp.concatenate(side_chunks(which, kv, halo, hi), axis=0))
            k1[...] = near_keys(kv, c1, lo)
            v1t[...] = transposed(near_keys(kv, c1, hi))
        row = place_row(off[h]).astype(F32) * sign.astype(F32)
        col = jnp.broadcast_to(row, (128, 256)).T
        dist[...] = jnp.concatenate([col, col], axis=1) - row
        reach = win[h].astype(F32)
        if which == 0:
            outer = reach - 256.0
        else:
            outer = jnp.where((tm[0] == 0) | (tm[0] == 31), -1000.0, reach - 256.0)
        qz = zero_pad(qt[which, 64 * h : 64 * h + 64, :], a)
        top = None
        for c, keys in enumerate(side_chunks(which, kv, halo, lo)):
            sc = dot(keys, qz)
            d = dist[...]
            ok = (d <= outer, jnp.abs(d) <= reach, d >= 256.0 - reach)[c]
            sc = jnp.where(ok, sc, NEG)
            sw[256 * c : 256 * c + 256] = sc
            part = jnp.max(sc, axis=0, keepdims=True)
            top = part if top is None else jnp.maximum(top, part)
        sc = dot(k1[...], qz[:, 0:128])
        s1[...] = sc
        near_top = jnp.maximum(top[:, 0:128], jnp.max(sc, axis=0, keepdims=True))
        top = jnp.concatenate([near_top, top[:, 128:256]], axis=1)
        total = jnp.zeros((1, 256), F32)
        for c in range(3):
            e = jnp.exp(sw[256 * c : 256 * c + 256] - top)
            total += jnp.sum(e, axis=0, keepdims=True)
            pw[h, 256 * c : 256 * c + 256, :] = e.astype(BF16)
        vh, hs = slice(64 * a, 64 * a + 64), slice(64 * h, 64 * h + 64)
        acc = dot(vt[vh, :], pw[h])
        near_sum = jnp.zeros((1, 128), F32)
        for c in range(4):
            e = count * jnp.exp(s1[128 * c : 128 * c + 128] - near_top)
            near_sum += jnp.sum(e, axis=0, keepdims=True)
            p1[h, 128 * c : 128 * c + 128, :] = e.astype(BF16)
        near_acc = dot(v1t[vh, :], p1[h])
        acc_out[hs, 0:128] = acc[:, 0:128] + near_acc
        acc_out[hs, 128:256] = acc[:, 128:256]
        stat[h : h + 1, :] = top
        stat[4 + h : 5 + h, 0:128] = total[:, 0:128] + near_sum
        stat[4 + h : 5 + h, 128:256] = total[:, 128:256]


def far_count(level):
    s = (256 >> level, 128)
    both = jnp.minimum(depth(iota(s, 0)), depth(iota(s, 1) & 63))
    return jnp.maximum(both - level + 1, 0).astype(F32)


def far_lanes(x):
    return jnp.concatenate([x[:, 0:64], x[:, 256:320]], axis=1)


def far_cols(x, hs):
    return jnp.concatenate([x[0, hs, 0:64], x[1, hs, 0:64]], axis=1)


def wide(x, b, filler):
    rows = x.shape[0]
    return jnp.concatenate([x[:, 64 * b : 64 * b + 64], jnp.full((rows, 192), filler, F32)], axis=1)


def unperm_pair(off, pair, src):
    first, second = from_depth(off[2 * pair]), from_depth(off[2 * pair + 1])
    return jnp.where(lane_first(256), dot_nt(first, src), dot_nt(second, src)).astype(BF16)


def fwd_far(off, qt, gt, acc0, acc1, st0, st1, *rest):
    bufs, (pf, attn, stat2, kf, vft, mult, at) = rest[:4], rest[4:]
    for level in range(2, 6):
        n = 256 >> level
        piece = far_count(level)
        for j in range(256 // n):
            mult[256 * (level - 2) + n * j : 256 * (level - 2) + n * j + n] = piece
    for pair in range(2):
        lo, hi = pair_slices(pair)
        kf[...] = far_rows(bufs, lo)
        vft[...] = transposed(far_rows(bufs, hi))
        for a in range(2):
            vh = slice(64 * a, 64 * a + 64)
            h = 2 * pair + a
            hs = slice(64 * h, 64 * h + 64)
            qz = zero_pad(far_cols(qt, hs), a)
            cnt = mult[...]
            sc = jnp.where(cnt > 0, dot(kf[...], qz), NEG)
            ftop = jnp.max(sc, axis=0, keepdims=True)
            e = cnt * jnp.exp(sc - ftop)
            fsum = jnp.sum(e, axis=0, keepdims=True)
            pf[h] = e.astype(BF16)
            facc = dot(vft[vh, :], pf[h])
            for b in range(2):
                bs = slice(256 * b, 256 * b + 256)
                acc_in, stat = (acc0, st0) if b == 0 else (acc1, st1)
                ntop, nsum = stat[h : h + 1, :], stat[4 + h : 5 + h, :]
                ftopw = wide(ftop, b, NEG)
                top = jnp.maximum(ntop, ftopw)
                wn, wf = jnp.exp(ntop - top), jnp.exp(ftopw - top)
                norm = nsum * wn + wide(fsum, b, 0.0) * wf
                acc = acc_in[hs, :] * wn + wide(facc, b, 0.0) * wf
                o = (acc / norm).astype(BF16)
                at[vh, bs] = o
                stat2[h : h + 1, bs] = wn / norm
                stat2[4 + h : 5 + h, bs] = wf / norm
                stat2[8 + h : 9 + h, bs] = jnp.sum(
                    gt[b, hs].astype(F32) * o.astype(F32), axis=0, keepdims=True
                )
        for b in range(2):
            bs = slice(256 * b, 256 * b + 256)
            attn[bs, 128 * pair : 128 * pair + 128] = unperm_pair(off, pair, at[:, bs])


def bwd_far(qt, gt, stat2, pf, *rest):
    bufs, (ret, own_far, dq, kx, vx) = rest[:4], rest[4:]
    for pair in range(2):
        lo, hi = pair_slices(pair)
        kx[...] = far_rows(bufs, lo)
        vx[...] = far_rows(bufs, hi)
        kt = transposed(kx[...])
        grads, scaled_q, scaled_g = [], [], []
        for a in range(2):
            h = 2 * pair + a
            hs, vh = slice(64 * h, 64 * h + 64), slice(64 * a, 64 * a + 64)
            cf = far_lanes(stat2[4 + h : 5 + h, :])
            delta = far_lanes(stat2[8 + h : 9 + h, :])
            q, g = far_cols(qt, hs), far_cols(gt, hs)
            dp = dot(vx[...], zero_pad(g, a))
            ds = (pf[h].astype(F32) * (dp - delta)).astype(BF16)
            grads.append(ds)
            scaled_q.append(zero_pad((q.astype(F32) * cf).astype(BF16), a))
            scaled_g.append(zero_pad((g.astype(F32) * cf).astype(BF16), a))
            dq[hs, :] = dot(kt[vh, :], ds) * cf
        dk = dot_nt(jnp.concatenate(grads, axis=1), jnp.concatenate(scaled_q, axis=1))
        dv = dot_nt(jnp.concatenate([pf[2 * pair], pf[2 * pair + 1]], axis=1), jnp.concatenate(scaled_g, axis=1))
        for j in range(4):
            mine, theirs = slice(256 * j, 256 * j + 128), slice(256 * j + 128, 256 * j + 256)
            rows = slice(128 * j, 128 * j + 128)
            own_far[rows, lo] = dk[mine]
            own_far[rows, hi] = dv[mine]
            ret[rows, lo] = dk[theirs].astype(BF16)
            ret[rows, hi] = dv[theirs].astype(BF16)


def bwd_keys(qt, gt, stat2, kv, c1, p10, p11, ret, own_near, dq):
    for pair in range(2):
        lo, hi = pair_slices(pair)
        k1t = transposed(near_keys(kv, c1, lo))
        v1 = near_keys(kv, c1, hi)
        grads, scaled_q, scaled_g, probs = [], [], [], []
        for a in range(2):
            h = 2 * pair + a
            hs, vh = slice(64 * h, 64 * h + 64), slice(64 * a, 64 * a + 64)
            for b in range(2):
                bs = slice(256 * b, 256 * b + 128)
                cn, delta = stat2[h : h + 1, bs], stat2[8 + h : 9 + h, bs]
                g = gt[b, hs, 0:128]
                p = (p10 if b == 0 else p11)[h]
                ds = (p.astype(F32) * (dot(v1, zero_pad(g, a)) - delta)).astype(BF16)
                grads.append(ds)
                probs.append(p)
                scaled_q.append(zero_pad((qt[b, hs, 0:128].astype(F32) * cn).astype(BF16), a))
                scaled_g.append(zero_pad((g.astype(F32) * cn).astype(BF16), a))
                dq[hs, 128 * b : 128 * b + 128] = dot(k1t[vh, :], ds) * cn
        dk = dot_nt(jnp.concatenate(grads, axis=1), jnp.concatenate(scaled_q, axis=1))
        dv = dot_nt(jnp.concatenate(probs, axis=1), jnp.concatenate(scaled_g, axis=1))
        own_near[:, lo] = dk[0:256]
        own_near[:, hi] = dv[0:256]
        ret[:, lo] = dk[256:512].astype(BF16)
        ret[:, hi] = dv[256:512].astype(BF16)


def bwd_near(which, off, tm, qt, gt, stat2, kv, halo, pw, dqf, dqn, *rest):
    if which == 1:
        own, halo_out, gq, dqt = rest
    else:
        own_in, own_near, gq_in, own, halo_out, gq, dqt = rest
        gq[block_rows(tm, 1), :] = gq_in[...]
    bs = slice(256 * which, 256 * which + 256)
    ob = slice(256 - 256 * which, 512 - 256 * which)
    for pair in range(2):
        lo, hi = pair_slices(pair)
        vx = jnp.concatenate(side_chunks(which, kv, halo, hi), axis=0)
        kt = transposed(jnp.concatenate(side_chunks(which, kv, halo, lo), axis=0))
        grads, scaled_q, scaled_g = [], [], []
        for a in range(2):
            h = 2 * pair + a
            hs, vh = slice(64 * h, 64 * h + 64), slice(64 * a, 64 * a + 64)
            cn, delta = stat2[h : h + 1, bs], stat2[8 + h : 9 + h, bs]
            g = gt[which, hs]
            dp = dot(vx, zero_pad(g, a))
            ds = (pw[h].astype(F32) * (dp - delta)).astype(BF16)
            grads.append(ds)
            scaled_q.append(zero_pad((qt[which, hs].astype(F32) * cn).astype(BF16), a))
            scaled_g.append(zero_pad((g.astype(F32) * cn).astype(BF16), a))
            near = jnp.concatenate(
                [dqn[hs, 128 * which : 128 * which + 128], jnp.zeros((64, 128), F32)], axis=1
            )
            total = dot(kt[vh, :], ds) * cn + near + wide(dqf[hs, :], which, 0.0)
            dqt[vh, :] = (total * 0.125).astype(BF16)
        probs = jnp.concatenate([pw[2 * pair], pw[2 * pair + 1]], axis=1)
        for lanes, left, right in ((lo, jnp.concatenate(grads, axis=1), scaled_q), (hi, probs, scaled_g)):
            d = dot_nt(left, jnp.concatenate(right, axis=1))
            halo_out[:, lanes] = d[0:256].astype(BF16)
            if which == 1:
                own[bs, lanes] = d[256:512]
                own[ob, lanes] = d[512:768]
            else:
                own[bs, lanes] = d[256:512] + own_in[bs, lanes]
                own[ob, lanes] = d[512:768] + own_in[ob, lanes]
                own[0:128, lanes] += own_near[0:128, lanes]
                own[256:384, lanes] += own_near[128:256, lanes]
        r = unperm_pair(off, pair, dqt[...])
        if which == 1:
            gq[:, 128 * pair : 128 * pair + 128] = r
        else:
            gq[block_rows(tm, 0), 128 * pair : 128 * pair + 128] = r


def ret_y(own_far, ret, rest, y1, y2a, y2b):
    total = own_far[...] + ret[...].astype(F32)
    rest[...] = total[0:256]
    y1[...] = total[256:384].astype(BF16)
    y2a[...] = total[384:448].astype(BF16)
    y2b[...] = total[448:512].astype(BF16)


def ret_x(rest, y1, y2a, y2b, x1, x2a, x2b):
    deep = y1[...].astype(F32)
    deeper = y2a[...].astype(F32) + y2b[...].astype(F32)
    total = []
    for j, at in enumerate((0, 64, 128, 160, 192, 224)):
        size = 64 if at < 128 else 32
        top = deep[32 + 16 * j : 48 + 16 * j]
        head = rest[at : at + 16] + top
        total += [head[0:8] + deeper[16 + 8 * j : 24 + 8 * j], head[8:16], rest[at + 16 : at + size]]
    x1[...] = jnp.concatenate(total[0:6], axis=0).astype(BF16)
    x2a[...] = jnp.concatenate(total[6:12], axis=0).astype(BF16)
    x2b[...] = jnp.concatenate(total[12:18], axis=0).astype(BF16)


def gather_own(own, near_r, hc, hn, y1, y2a, y2b, acc):
    acc[...] = own[...]
    acc[0:256] += hc[...].astype(F32)
    acc[256:512] += hn[...].astype(F32)
    for b in range(2):
        at = 256 * b
        acc[at : at + 128] += near_r[128 * b : 128 * b + 128].astype(F32)
        acc[at : at + 16] += y1[16 * b : 16 * b + 16].astype(F32)
        acc[at : at + 8] += (y2a[0:16].astype(F32) + y2b[0:16].astype(F32))[8 * b : 8 * b + 8]


def finish(off, tm, acc, x1, x2a, x2b, gk, gv):
    keep = lane_first(256, 256)
    for pair in range(2):
        first, second = from_depth(off[2 * pair]), from_depth(off[2 * pair + 1])
        lanes = slice(128 * pair, 128 * pair + 128)
        cols = slice(256 * pair, 256 * pair + 256)
        for b in range(2):
            at = 256 * b
            head = acc[at : at + 64, cols] + x1[64 * b : 64 * b + 64, cols].astype(F32)
            deep = x2a[32 * b : 32 * b + 32, cols].astype(F32) + x2b[32 * b : 32 * b + 32, cols].astype(F32)
            x = jnp.concatenate([head[0:32] + deep, head[32:64], acc[at + 64 : at + 256, cols]], axis=0).astype(BF16)
            r = jnp.where(keep, dot(first, x), dot(second, x)).astype(BF16)
            gk[block_rows(tm, b), lanes] = r[:, 0:128]
            gv[block_rows(tm, b), lanes] = r[:, 128:256]


def project(tm, a01, a23, w02, w13, out):
    w = jnp.concatenate([w02[0:256], w13[0:256], w02[256:512], w13[256:512]], axis=0)
    for b in range(2):
        bs = slice(256 * b, 256 * b + 256)
        a = jnp.concatenate([a01[bs], a23[bs]], axis=1)
        out[block_rows(tm, b), :] = dot(a, w).astype(BF16)


def swap(x, axis, mask):
    return lax.ppermute(x, axis, [(i, i ^ mask) for i in range(lax.axis_size(axis))])


def side(x):
    pairs = [(i, i + 1 if i % 2 else i - 1) for i in range(1, lax.axis_size("tm") - 1)]
    return lax.ppermute(x, "tm", pairs)


def bind(f, *args):
    def body(*refs):
        f(*args, *refs)

    return body


def layer(q, k, v, w, up, win, off):
    tm = lax.axis_index("tm").astype(jnp.int32).reshape(1)
    VM = pltpu.VMEM
    hbm = pl.BlockSpec(memory_space=pltpu.HBM)
    rows = lambda n: sds((n, 512), BF16)
    kvp, c1s, n1s, x1s, x2s, qv, upv, wv = call(
        prep_kv, (off, tm) + tuple(pltpu.with_memory_space_constraint(x, pltpu.HBM) for x in (k, v, q, up, w)),
        [rows(512), rows(384), rows(256), rows(128), rows(64),
         sds((512, 256), BF16), sds((512, 1024), BF16), sds((256, 1024), BF16)],
        specs=[SMEM, SMEM] + [hbm] * 5,
        scratch=[VM((512, 256), BF16), VM((512, 256), BF16), pltpu.SemaphoreType.DMA((9,))],
        flops=3e8, nbytes=3e6,
    )
    x1, x2a, x2b = swap(x1s, "tm", 2), swap(x2s, "tm", 4), swap(x2s, "tm", 6)
    c1 = swap(c1s, "tm", 1)
    n1 = side(n1s)
    w1 = swap(wv, "head", 3)
    (w02,) = call(stack, (wv, w1), [sds((512, 1024), BF16)])
    w13 = swap(w02, "head", 1)
    qt, gt = call(
        prep_qg, (off, qv, upv, wv), [sds((2, 256, 256), BF16), sds((2, 256, 256), BF16)],
        specs=[SMEM] + [None] * 3, flops=6e8, nbytes=3e6,
    )
    near = []
    for which in range(2):
        near.append(
            call(
                bind(fwd_near, which), (off, win, tm, qt, kvp, c1) + ((n1,) if which else ()),
                [sds((4, 768, 256), BF16), sds((4, 512, 128), BF16), sds((256, 256), F32), sds((8, 256), F32)],
                specs=[SMEM] * 3 + [None] * (3 + which),
                scratch=[
                    VM((128, 768), BF16), VM((128, 512), BF16), VM((512, 128), BF16), VM((256, 256), F32),
                    VM((768, 256), F32), VM((512, 128), F32),
                ],
                flops=3e9, nbytes=4e6,
            )
        )
    y1s, y2s, mine_x = call(asm_y, (kvp, x1, x2a, x2b), [rows(128), rows(64), rows(256)])
    y1, y2a, y2b = swap(y1s, "tm", 8), swap(y2s, "tm", 16), swap(y2s, "tm", 24)
    (mine_y,) = call(stack, (y1, y2a, y2b), [rows(256)])
    bufs = (mine_x, swap(mine_x, "tm", 1), mine_y, swap(mine_y, "tm", 1))
    pf, attn, stat2 = call(
        fwd_far, (off, qt, gt, near[0][2], near[1][2], near[0][3], near[1][3], *bufs),
        [sds((4, 1024, 128), BF16), sds((512, 256), BF16), sds((16, 512), F32)],
        specs=[SMEM] + [None] * 10,
        scratch=[VM((1024, 128), BF16), VM((128, 1024), BF16), VM((1024, 128), F32), VM((128, 512), BF16)],
        flops=3e9, nbytes=4e6,
    )
    a1 = swap(attn, "head", 1)
    (a01,) = call(beside, (attn, a1), [rows(512)])
    a23 = swap(a01, "head", 3)
    (mixed,) = call(
        project, (tm, a01, a23, w02, w13), [sds((512, 1024), BF16)],
        specs=[SMEM] + [None] * 4, flops=1e9, nbytes=4e6,
    )
    ret_s, own_far, dqf = call(
        bwd_far, (qt, gt, stat2, pf, *bufs),
        [sds((512, 512), BF16), sds((512, 512), F32), sds((256, 128), F32)],
        scratch=[VM((1024, 128), BF16), VM((1024, 128), BF16)], flops=4e9, nbytes=5e6,
    )
    ret = swap(ret_s, "tm", 1)
    near_s, own_near, dqn = call(
        bwd_keys, (qt, gt, stat2, kvp, c1, near[0][1], near[1][1]),
        [sds((256, 512), BF16), sds((256, 512), F32), sds((256, 256), F32)],
        flops=4e9, nbytes=5e6,
    )
    near_r = swap(near_s, "tm", 1)

    def back(which, halo, gq_rows, more):
        return call(
            bind(bwd_near, which), (off, tm, qt, gt, stat2, kvp, halo, near[which][0], dqf, dqn, *more),
            [sds((512, 512), F32), sds((256, 512), BF16), sds((gq_rows, 256), BF16)],
            specs=[SMEM] * 2 + [None] * (8 + len(more)),
            scratch=[VM((128, 256), BF16)], flops=4e9, nbytes=4e6,
        )

    own1, hn_s, gq1 = back(1, n1, 256, ())
    own, hc_s, gq = back(0, c1, 512, (own1, own_near, gq1))
    rest, y1s, y2as, y2bs = call(ret_y, (own_far, ret), [sds((256, 512), F32), rows(128), rows(64), rows(64)])
    yr = [swap(x, "tm", m) for x, m in ((y1s, 8), (y2as, 16), (y2bs, 24))]
    x1s, x2as, x2bs = call(ret_x, (rest, *yr), [rows(128), rows(64), rows(64)])
    xr = [swap(x, "tm", m) for x, m in ((x1s, 2), (x2as, 4), (x2bs, 6))]
    hc, hn = swap(hc_s, "tm", 1), side(hn_s)
    (acc,) = call(gather_own, (own, near_r, hc, hn, *yr), [sds((512, 512), F32)], nbytes=3e6)
    gk, gv = call(
        finish, (off, tm, acc, *xr), [sds((512, 256), BF16), sds((512, 256), BF16)],
        specs=[SMEM] * 2 + [None] * 4, flops=3e8, nbytes=3e6,
    )
    return mixed, gq, gk, gv


def solution(mesh):
    placed = (P("tm", "head"),) * 3 + (P("head", None), P("tm", None), P("head"), P("head"))
    return jax.shard_map(
        layer,
        mesh=mesh,
        in_specs=placed,
        out_specs=(P("tm", None), P("tm", "head"), P("tm", "head"), P("tm", "head")),
        check_vma=False,
    )
```

```python
import jax
import jax.numpy as jnp
from jax import lax
from jax.experimental import pallas as pl
from jax.experimental.pallas import tpu as pltpu
from jax.sharding import PartitionSpec as P


F32 = jnp.float32
BF16 = jnp.bfloat16
NEG = -1e30
NT = (((1,), (1,)), ((), ()))
SMEM = pl.BlockSpec(memory_space=pltpu.SMEM)


def sds(shape, dtype):
    return jax.ShapeDtypeStruct(shape, dtype)


def dot(a, b):
    return jnp.dot(a, b, preferred_element_type=F32)


def dot_nt(a, b):
    return lax.dot_general(a, b, NT, preferred_element_type=F32)


def call(body, ins, outs, scratch=(), flops=0, nbytes=0, specs=None, out_specs=None, vmem=24):
    full = lambda x: pl.BlockSpec(x.shape, (lambda *_: (0,) * len(x.shape)))
    specs = specs or [None] * len(ins)
    in_specs = [full(x) if s is None else s for x, s in zip(ins, specs)]
    out_specs = out_specs or [full(o) for o in outs]
    return pl.pallas_call(
        body,
        out_shape=outs,
        grid=(1,),
        in_specs=in_specs,
        out_specs=out_specs,
        scratch_shapes=list(scratch),
        cost_estimate=pl.CostEstimate(flops=int(flops), bytes_accessed=int(nbytes), transcendentals=0),
        compiler_params=pltpu.CompilerParams(vmem_limit_bytes=vmem << 20),
    )(*ins)


def iota(shape, axis):
    return lax.broadcasted_iota(jnp.int32, shape, axis)


def place_row(offset):
    n = iota((1, 256), 1)
    u = jnp.where(n >= 128, 2 * (n - 128) + 1, 4 * (n - 64) + 2)
    u = jnp.where(n >= 64, u, 8 * (n - 32) + 4)
    u = jnp.where(n >= 32, u, 16 * (n - 16) + 8)
    u = jnp.where(n >= 16, u, 32 * (n - 8) + 16)
    u = jnp.where(n >= 8, u, 32 * n)
    return (u + offset) & 255


def rank_row(offset):
    u = (iota((1, 256), 1) - offset) & 255
    n = jnp.where((u & 16) != 0, 8 + (u >> 5), u >> 5)
    n = jnp.where((u & 8) != 0, 16 + (u >> 4), n)
    n = jnp.where((u & 4) != 0, 32 + (u >> 3), n)
    n = jnp.where((u & 2) != 0, 64 + (u >> 2), n)
    return jnp.where((u & 1) != 0, 128 + (u >> 1), n)


def depth(n):
    d = jnp.where(n < 64, 2, 1)
    d = jnp.where(n < 32, 3, d)
    d = jnp.where(n < 16, 4, d)
    return jnp.where(n < 8, 5, d)


def to_depth(offset):
    return (iota((256, 256), 0) == rank_row(offset)).astype(F32).astype(BF16)


def from_depth(offset):
    return (iota((256, 256), 0) == place_row(offset)).astype(F32).astype(BF16)


def lane_first(rows, width=128):
    return (iota((rows, width), 1) % 128) < 64


def zero_pad(x, which):
    z = jnp.zeros_like(x)
    return jnp.concatenate([x, z] if which == 0 else [z, x], axis=0)


def transposed(x):
    return x.astype(F32).T.astype(BF16)


def parity(tm):
    return tm[0] & 1


def block_rows(tm, which):
    block = (1 - parity(tm)) if which == 0 else parity(tm)
    return pl.ds(pl.multiple_of(256 * block, 256), 256)


def prep_kv(tm, off_hbm, k, v, q, up, w, kvp, c1, n1, x1, x2, qv, upv, wv, kb, vb, off, sem):
    copies = []
    for src, dst in ((k, kb), (v, vb), (q, qv), (up, upv)):
        for which in range(2):
            copies.append(
                pltpu.make_async_copy(
                    src.at[block_rows(tm, which)], dst.at[pl.ds(256 * which, 256)], sem.at[len(copies)]
                )
            )
    copies.append(pltpu.make_async_copy(w, wv, sem.at[8]))
    table = pltpu.make_async_copy(off_hbm, off, sem.at[9])
    table.start()
    for c in copies:
        c.start()
    table.wait()
    perms = [to_depth(off[h]) for h in range(4)]
    for c in copies[:4]:
        c.wait()
    keep = lane_first(256, 256)
    for pair in range(2):
        lanes = slice(pair * 128, pair * 128 + 128)
        for b in range(2):
            rows = slice(b * 256, b * 256 + 256)
            kv = jnp.concatenate([kb[rows, lanes], vb[rows, lanes]], axis=1)
            kvp[rows, pair * 256 : pair * 256 + 256] = jnp.where(
                keep, dot(perms[2 * pair], kv), dot(perms[2 * pair + 1], kv)
            ).astype(BF16)
    x1[0:64] = kvp[0:64]
    x1[64:128] = kvp[256:320]
    x2[0:32] = kvp[0:32]
    x2[32:64] = kvp[256:288]
    c1[...] = kvp[0:384]
    n1[...] = kvp[256:512]
    for c in copies[4:]:
        c.wait()


def prep_qg(off, q, up, w, qt, gt):
    g = dot_nt(w[...], up[...]).astype(BF16)
    qs = (q[...].astype(F32) * 0.125).T.astype(BF16)
    for h in range(4):
        perm = from_depth(off[h])
        hs = slice(64 * h, 64 * h + 64)
        for b in range(2):
            bs = slice(256 * b, 256 * b + 256)
            x = jnp.concatenate([qs[hs, bs], g[hs, bs]], axis=0)
            r = dot(x, perm).astype(BF16)
            qt[b, hs] = r[0:64]
            gt[b, hs] = r[64:128]


def asm_y(kvp, x1, x2a, x2b, y1, y2, both):
    heads = [kvp[0:16], kvp[256:272], x1[0:16], x1[64:80], x2a[0:16], x2a[32:48], x2b[0:16], x2b[32:48]]
    heads = [h.astype(F32) for h in heads]
    y1[...] = jnp.concatenate(heads, axis=0).astype(BF16)
    y2[...] = jnp.concatenate([h[0:8] for h in heads], axis=0).astype(BF16)
    stack(x1, x2a, x2b, both)


def stack(*refs):
    out, at = refs[-1], 0
    for ref in refs[:-1]:
        out[at : at + ref.shape[0]] = ref[...]
        at += ref.shape[0]


def beside(left, right, out):
    out[:, 0 : left.shape[1]] = left[...]
    out[:, left.shape[1] :] = right[...]


def far_rows(bufs, lanes):
    mine_x, other_x, mine_y, other_y = bufs
    out = []
    for mine, other in ((mine_x, other_x), (mine_y, other_y)):
        for half in (slice(0, 128), slice(128, 256)):
            out += [mine[half, lanes], other[half, lanes]]
    return jnp.concatenate(out, axis=0)


def near_count():
    s = (128, 128)
    return jnp.minimum(depth(iota(s, 0)), depth(iota(s, 1))).astype(F32)


def near_keys(kv, c1, lanes):
    return jnp.concatenate([kv[0:128, lanes], kv[256:384, lanes], c1[0:128, lanes], c1[256:384, lanes]], axis=0)


def pair_slices(pair):
    return slice(256 * pair, 256 * pair + 128), slice(256 * pair + 128, 256 * pair + 256)


def side_chunks(which, kv, halo, lanes):
    own, other = slice(256 * which, 256 * which + 256), slice(256 - 256 * which, 512 - 256 * which)
    return [halo[0:256, lanes], kv[own, lanes], kv[other, lanes]]


def fwd_near(which, off, win, tm, qt, kv, c1, *rest):
    if which == 0:
        halo = c1
        pw, p1, acc_out, stat, vt, v1t, k1, dist, sw, s1 = rest
    else:
        halo, pw, p1, acc_out, stat, vt, v1t, k1, dist, sw, s1 = rest
    count = near_count()
    sign = (1 - 2 * parity(tm)) * (1 if which == 0 else -1)
    for h in range(4):
        a, pair = h % 2, h // 2
        lo, hi = pair_slices(pair)
        if a == 0:
            vt[...] = transposed(jnp.concatenate(side_chunks(which, kv, halo, hi), axis=0))
            k1[...] = near_keys(kv, c1, lo)
            v1t[...] = transposed(near_keys(kv, c1, hi))
        row = place_row(off[h]).astype(F32) * sign.astype(F32)
        col = jnp.broadcast_to(row, (128, 256)).T
        dist[...] = jnp.concatenate([col, col], axis=1) - row
        reach = win[h].astype(F32)
        if which == 0:
            outer = reach - 256.0
        else:
            outer = jnp.where((tm[0] == 0) | (tm[0] == 31), -1000.0, reach - 256.0)
        qz = zero_pad(qt[which, 64 * h : 64 * h + 64, :], a)
        top = None
        for c, keys in enumerate(side_chunks(which, kv, halo, lo)):
            sc = dot(keys, qz)
            d = dist[...]
            ok = (d <= outer, jnp.abs(d) <= reach, d >= 256.0 - reach)[c]
            sc = jnp.where(ok, sc, NEG)
            sw[256 * c : 256 * c + 256] = sc
            part = jnp.max(sc, axis=0, keepdims=True)
            top = part if top is None else jnp.maximum(top, part)
        sc = dot(k1[...], qz[:, 0:128])
        s1[...] = sc
        near_top = jnp.maximum(top[:, 0:128], jnp.max(sc, axis=0, keepdims=True))
        top = jnp.concatenate([near_top, top[:, 128:256]], axis=1)
        total = jnp.zeros((1, 256), F32)
        for c in range(3):
            e = jnp.exp(sw[256 * c : 256 * c + 256] - top)
            total += jnp.sum(e, axis=0, keepdims=True)
            pw[h, 256 * c : 256 * c + 256, :] = e.astype(BF16)
        vh, hs = slice(64 * a, 64 * a + 64), slice(64 * h, 64 * h + 64)
        acc = dot(vt[vh, :], pw[h])
        near_sum = jnp.zeros((1, 128), F32)
        for c in range(4):
            e = count * jnp.exp(s1[128 * c : 128 * c + 128] - near_top)
            near_sum += jnp.sum(e, axis=0, keepdims=True)
            p1[h, 128 * c : 128 * c + 128, :] = e.astype(BF16)
        near_acc = dot(v1t[vh, :], p1[h])
        acc_out[hs, 0:128] = acc[:, 0:128] + near_acc
        acc_out[hs, 128:256] = acc[:, 128:256]
        stat[h : h + 1, :] = top
        stat[4 + h : 5 + h, 0:128] = total[:, 0:128] + near_sum
        stat[4 + h : 5 + h, 128:256] = total[:, 128:256]


def far_count(level):
    s = (256 >> level, 128)
    both = jnp.minimum(depth(iota(s, 0)), depth(iota(s, 1) & 63))
    return jnp.maximum(both - level + 1, 0).astype(F32)


def far_lanes(x):
    return jnp.concatenate([x[:, 0:64], x[:, 256:320]], axis=1)


def far_cols(x, hs):
    return jnp.concatenate([x[0, hs, 0:64], x[1, hs, 0:64]], axis=1)


def wide(x, b, filler):
    rows = x.shape[0]
    return jnp.concatenate([x[:, 64 * b : 64 * b + 64], jnp.full((rows, 192), filler, F32)], axis=1)


def unperm_pair(off, pair, src):
    first, second = from_depth(off[2 * pair]), from_depth(off[2 * pair + 1])
    return jnp.where(lane_first(256), dot_nt(first, src), dot_nt(second, src)).astype(BF16)


def fwd_far(off, qt, gt, acc0, acc1, st0, st1, *rest):
    bufs, (pf, attn, stat2, kf, vft, mult, at) = rest[:4], rest[4:]
    for level in range(2, 6):
        n = 256 >> level
        piece = far_count(level)
        for j in range(256 // n):
            mult[256 * (level - 2) + n * j : 256 * (level - 2) + n * j + n] = piece
    for pair in range(2):
        lo, hi = pair_slices(pair)
        kf[...] = far_rows(bufs, lo)
        vft[...] = transposed(far_rows(bufs, hi))
        for a in range(2):
            vh = slice(64 * a, 64 * a + 64)
            h = 2 * pair + a
            hs = slice(64 * h, 64 * h + 64)
            qz = zero_pad(far_cols(qt, hs), a)
            cnt = mult[...]
            sc = jnp.where(cnt > 0, dot(kf[...], qz), NEG)
            ftop = jnp.max(sc, axis=0, keepdims=True)
            e = cnt * jnp.exp(sc - ftop)
            fsum = jnp.sum(e, axis=0, keepdims=True)
            pf[h] = e.astype(BF16)
            facc = dot(vft[vh, :], pf[h])
            for b in range(2):
                bs = slice(256 * b, 256 * b + 256)
                acc_in, stat = (acc0, st0) if b == 0 else (acc1, st1)
                ntop, nsum = stat[h : h + 1, :], stat[4 + h : 5 + h, :]
                ftopw = wide(ftop, b, NEG)
                top = jnp.maximum(ntop, ftopw)
                wn, wf = jnp.exp(ntop - top), jnp.exp(ftopw - top)
                norm = nsum * wn + wide(fsum, b, 0.0) * wf
                acc = acc_in[hs, :] * wn + wide(facc, b, 0.0) * wf
                o = (acc / norm).astype(BF16)
                at[vh, bs] = o
                stat2[h : h + 1, bs] = wn / norm
                stat2[4 + h : 5 + h, bs] = wf / norm
                stat2[8 + h : 9 + h, bs] = jnp.sum(
                    gt[b, hs].astype(F32) * o.astype(F32), axis=0, keepdims=True
                )
        for b in range(2):
            bs = slice(256 * b, 256 * b + 256)
            attn[bs, 128 * pair : 128 * pair + 128] = unperm_pair(off, pair, at[:, bs])


def bwd_far(qt, gt, stat2, pf, *rest):
    bufs, (ret, own_far, dq, kx, vx) = rest[:4], rest[4:]
    for pair in range(2):
        lo, hi = pair_slices(pair)
        kx[...] = far_rows(bufs, lo)
        vx[...] = far_rows(bufs, hi)
        kt = transposed(kx[...])
        grads, scaled_q, scaled_g = [], [], []
        for a in range(2):
            h = 2 * pair + a
            hs, vh = slice(64 * h, 64 * h + 64), slice(64 * a, 64 * a + 64)
            cf = far_lanes(stat2[4 + h : 5 + h, :])
            delta = far_lanes(stat2[8 + h : 9 + h, :])
            q, g = far_cols(qt, hs), far_cols(gt, hs)
            dp = dot(vx[...], zero_pad(g, a))
            ds = (pf[h].astype(F32) * (dp - delta)).astype(BF16)
            grads.append(ds)
            scaled_q.append(zero_pad((q.astype(F32) * cf).astype(BF16), a))
            scaled_g.append(zero_pad((g.astype(F32) * cf).astype(BF16), a))
            dq[hs, :] = dot(kt[vh, :], ds) * cf
        dk = dot_nt(jnp.concatenate(grads, axis=1), jnp.concatenate(scaled_q, axis=1))
        dv = dot_nt(jnp.concatenate([pf[2 * pair], pf[2 * pair + 1]], axis=1), jnp.concatenate(scaled_g, axis=1))
        for j in range(4):
            mine, theirs = slice(256 * j, 256 * j + 128), slice(256 * j + 128, 256 * j + 256)
            rows = slice(128 * j, 128 * j + 128)
            own_far[rows, lo] = dk[mine]
            own_far[rows, hi] = dv[mine]
            ret[rows, lo] = dk[theirs].astype(BF16)
            ret[rows, hi] = dv[theirs].astype(BF16)


def bwd_keys(qt, gt, stat2, kv, c1, p10, p11, ret, own_near, dq):
    for pair in range(2):
        lo, hi = pair_slices(pair)
        k1t = transposed(near_keys(kv, c1, lo))
        v1 = near_keys(kv, c1, hi)
        grads, scaled_q, scaled_g, probs = [], [], [], []
        for a in range(2):
            h = 2 * pair + a
            hs, vh = slice(64 * h, 64 * h + 64), slice(64 * a, 64 * a + 64)
            for b in range(2):
                bs = slice(256 * b, 256 * b + 128)
                cn, delta = stat2[h : h + 1, bs], stat2[8 + h : 9 + h, bs]
                g = gt[b, hs, 0:128]
                p = (p10 if b == 0 else p11)[h]
                ds = (p.astype(F32) * (dot(v1, zero_pad(g, a)) - delta)).astype(BF16)
                grads.append(ds)
                probs.append(p)
                scaled_q.append(zero_pad((qt[b, hs, 0:128].astype(F32) * cn).astype(BF16), a))
                scaled_g.append(zero_pad((g.astype(F32) * cn).astype(BF16), a))
                dq[hs, 128 * b : 128 * b + 128] = dot(k1t[vh, :], ds) * cn
        dk = dot_nt(jnp.concatenate(grads, axis=1), jnp.concatenate(scaled_q, axis=1))
        dv = dot_nt(jnp.concatenate(probs, axis=1), jnp.concatenate(scaled_g, axis=1))
        own_near[:, lo] = dk[0:256]
        own_near[:, hi] = dv[0:256]
        ret[:, lo] = dk[256:512].astype(BF16)
        ret[:, hi] = dv[256:512].astype(BF16)


def bwd_near(which, off, tm, qt, gt, stat2, kv, halo, pw, dqf, dqn, *rest):
    if which == 1:
        own, halo_out, gq, dqt = rest
    else:
        own_in, own_near, near_s, gq_in, own, halo_out, gq, dqt = rest
        halo_out[256:384] = near_s[128:256]
        gq[block_rows(tm, 1), :] = gq_in[...]
    bs = slice(256 * which, 256 * which + 256)
    ob = slice(256 - 256 * which, 512 - 256 * which)
    for pair in range(2):
        lo, hi = pair_slices(pair)
        vx = jnp.concatenate(side_chunks(which, kv, halo, hi), axis=0)
        kt = transposed(jnp.concatenate(side_chunks(which, kv, halo, lo), axis=0))
        grads, scaled_q, scaled_g = [], [], []
        for a in range(2):
            h = 2 * pair + a
            hs, vh = slice(64 * h, 64 * h + 64), slice(64 * a, 64 * a + 64)
            cn, delta = stat2[h : h + 1, bs], stat2[8 + h : 9 + h, bs]
            g = gt[which, hs]
            dp = dot(vx, zero_pad(g, a))
            ds = (pw[h].astype(F32) * (dp - delta)).astype(BF16)
            grads.append(ds)
            scaled_q.append(zero_pad((qt[which, hs].astype(F32) * cn).astype(BF16), a))
            scaled_g.append(zero_pad((g.astype(F32) * cn).astype(BF16), a))
            near = jnp.concatenate(
                [dqn[hs, 128 * which : 128 * which + 128], jnp.zeros((64, 128), F32)], axis=1
            )
            total = dot(kt[vh, :], ds) * cn + near + wide(dqf[hs, :], which, 0.0)
            dqt[vh, :] = (total * 0.125).astype(BF16)
        probs = jnp.concatenate([pw[2 * pair], pw[2 * pair + 1]], axis=1)
        for lanes, left, right in ((lo, jnp.concatenate(grads, axis=1), scaled_q), (hi, probs, scaled_g)):
            d = dot_nt(left, jnp.concatenate(right, axis=1))
            if which == 1:
                halo_out[:, lanes] = d[0:256].astype(BF16)
            else:
                halo_out[0:128, lanes] = (d[0:128] + near_s[0:128, lanes].astype(F32)).astype(BF16)
                halo_out[128:256, lanes] = d[128:256].astype(BF16)
            if which == 1:
                own[bs, lanes] = d[256:512]
                own[ob, lanes] = d[512:768]
            else:
                own[bs, lanes] = d[256:512] + own_in[bs, lanes]
                own[ob, lanes] = d[512:768] + own_in[ob, lanes]
                own[0:128, lanes] += own_near[0:128, lanes]
                own[256:384, lanes] += own_near[128:256, lanes]
        r = unperm_pair(off, pair, dqt[...])
        if which == 1:
            gq[:, 128 * pair : 128 * pair + 128] = r
        else:
            gq[block_rows(tm, 0), 128 * pair : 128 * pair + 128] = r


def ret_y(own_far, ret, rest, y1, y2a, y2b):
    total = own_far[...] + ret[...].astype(F32)
    rest[...] = total[0:256]
    y1[...] = total[256:384].astype(BF16)
    y2a[...] = total[384:448].astype(BF16)
    y2b[...] = total[448:512].astype(BF16)


def ret_x(rest, y1, y2a, y2b, x1, x2a, x2b):
    deep = y1[...].astype(F32)
    deeper = y2a[...].astype(F32) + y2b[...].astype(F32)
    total = []
    for j, at in enumerate((0, 64, 128, 160, 192, 224)):
        size = 64 if at < 128 else 32
        top = deep[32 + 16 * j : 48 + 16 * j]
        head = rest[at : at + 16] + top
        total += [head[0:8] + deeper[16 + 8 * j : 24 + 8 * j], head[8:16], rest[at + 16 : at + size]]
    x1[...] = jnp.concatenate(total[0:6], axis=0).astype(BF16)
    x2a[...] = jnp.concatenate(total[6:12], axis=0).astype(BF16)
    x2b[...] = jnp.concatenate(total[12:18], axis=0).astype(BF16)


def gather_own(own, hc, hn, y1, y2a, y2b, acc):
    acc[...] = own[...]
    acc[0:384] += hc[...].astype(F32)
    acc[256:512] += hn[...].astype(F32)
    for b in range(2):
        at = 256 * b
        acc[at : at + 16] += y1[16 * b : 16 * b + 16].astype(F32)
        acc[at : at + 8] += (y2a[0:16].astype(F32) + y2b[0:16].astype(F32))[8 * b : 8 * b + 8]


def finish(off, tm, acc, x1, x2a, x2b, gk, gv):
    keep = lane_first(256, 256)
    for pair in range(2):
        first, second = from_depth(off[2 * pair]), from_depth(off[2 * pair + 1])
        lanes = slice(128 * pair, 128 * pair + 128)
        cols = slice(256 * pair, 256 * pair + 256)
        for b in range(2):
            at = 256 * b
            head = acc[at : at + 64, cols] + x1[64 * b : 64 * b + 64, cols].astype(F32)
            deep = x2a[32 * b : 32 * b + 32, cols].astype(F32) + x2b[32 * b : 32 * b + 32, cols].astype(F32)
            x = jnp.concatenate([head[0:32] + deep, head[32:64], acc[at + 64 : at + 256, cols]], axis=0).astype(BF16)
            r = jnp.where(keep, dot(first, x), dot(second, x)).astype(BF16)
            gk[block_rows(tm, b), lanes] = r[:, 0:128]
            gv[block_rows(tm, b), lanes] = r[:, 128:256]


def half_rows(tm, w, out):
    out[...] = w[pl.ds(pl.multiple_of(128 * parity(tm), 128), 128), :]


def asm_w(tm, own, first, other, mine, theirs, out):
    out[0:256] = own[...]
    out[256:512] = first[...]
    out[512:768] = other[...]
    p = parity(tm)
    out[pl.ds(pl.multiple_of(768 + 128 * p, 128), 128), :] = mine[...]
    out[pl.ds(pl.multiple_of(896 - 128 * p, 128), 128), :] = theirs[...]


def project(tm, a01, a23, w, out):
    for b in range(2):
        bs = slice(256 * b, 256 * b + 256)
        a = jnp.concatenate([a01[bs], a23[bs]], axis=1)
        out[block_rows(tm, b), :] = dot(a, w[...]).astype(BF16)


def swap(x, axis, mask):
    return lax.ppermute(x, axis, [(i, i ^ mask) for i in range(lax.axis_size(axis))])


def cross(x, masks):
    heads = lax.axis_size("head")
    pairs = []
    for i in range(lax.axis_size("tm")):
        pairs += [(i * heads + z, i * heads + (z ^ masks[i % 2])) for z in range(heads)]
    return lax.ppermute(x, ("tm", "head"), pairs)


def side(x):
    pairs = [(i, i + 1 if i % 2 else i - 1) for i in range(1, lax.axis_size("tm") - 1)]
    return lax.ppermute(x, "tm", pairs)


def bind(f, *args):
    def body(*refs):
        f(*args, *refs)

    return body


def layer(q, k, v, w, up, win, off):
    tm = lax.axis_index("tm").astype(jnp.int32).reshape(1)
    VM = pltpu.VMEM
    hbm = pl.BlockSpec(memory_space=pltpu.HBM)
    rows = lambda n: sds((n, 512), BF16)
    kvp, c1s, n1s, x1s, x2s, qv, upv, wv = call(
        prep_kv, (tm,) + tuple(pltpu.with_memory_space_constraint(x, pltpu.HBM) for x in (off, k, v, q, up, w)),
        [rows(512), rows(384), rows(256), rows(128), rows(64),
         sds((512, 256), BF16), sds((512, 1024), BF16), sds((256, 1024), BF16)],
        specs=[SMEM] + [hbm] * 6,
        scratch=[VM((512, 256), BF16), VM((512, 256), BF16), pltpu.SMEM((4,), jnp.int32), pltpu.SemaphoreType.DMA((10,))],
        flops=3e8, nbytes=3e6,
    )
    x1, x2a, x2b = swap(x1s, "tm", 2), swap(x2s, "tm", 4), swap(x2s, "tm", 6)
    c1 = swap(c1s, "tm", 1)
    n1 = side(n1s)
    w1 = cross(wv, (1, 3))
    (w1h,) = call(half_rows, (tm, w1), [sds((128, 1024), BF16)], specs=[SMEM, None])
    w2 = cross(w1h, (3, 1))
    (w_all,) = call(
        asm_w, (tm, wv, w1, swap(w1, "tm", 1), w2, swap(w2, "tm", 1)),
        [sds((1024, 1024), BF16)], specs=[SMEM] + [None] * 5, nbytes=4e6,
    )
    qt, gt = call(
        prep_qg, (off, qv, upv, wv), [sds((2, 256, 256), BF16), sds((2, 256, 256), BF16)],
        specs=[SMEM] + [None] * 3, flops=6e8, nbytes=3e6,
    )
    near = []
    for which in range(2):
        near.append(
            call(
                bind(fwd_near, which), (off, win, tm, qt, kvp, c1) + ((n1,) if which else ()),
                [sds((4, 768, 256), BF16), sds((4, 512, 128), BF16), sds((256, 256), F32), sds((8, 256), F32)],
                specs=[SMEM] * 3 + [None] * (3 + which),
                scratch=[
                    VM((128, 768), BF16), VM((128, 512), BF16), VM((512, 128), BF16), VM((256, 256), F32),
                    VM((768, 256), F32), VM((512, 128), F32),
                ],
                flops=3e9, nbytes=4e6,
            )
        )
    y1s, y2s, mine_x = call(asm_y, (kvp, x1, x2a, x2b), [rows(128), rows(64), rows(256)])
    y1, y2a, y2b = swap(y1s, "tm", 8), swap(y2s, "tm", 16), swap(y2s, "tm", 24)
    (mine_y,) = call(stack, (y1, y2a, y2b), [rows(256)])
    bufs = (mine_x, swap(mine_x, "tm", 1), mine_y, swap(mine_y, "tm", 1))
    pf, attn, stat2 = call(
        fwd_far, (off, qt, gt, near[0][2], near[1][2], near[0][3], near[1][3], *bufs),
        [sds((4, 1024, 128), BF16), sds((512, 256), BF16), sds((16, 512), F32)],
        specs=[SMEM] + [None] * 10,
        scratch=[VM((1024, 128), BF16), VM((128, 1024), BF16), VM((1024, 128), F32), VM((128, 512), BF16)],
        flops=3e9, nbytes=4e6,
    )
    a1 = cross(attn, (1, 3))
    (a01,) = call(beside, (attn, a1), [rows(512)])
    a23 = cross(a01, (3, 1))
    (mixed,) = call(
        project, (tm, a01, a23, w_all), [sds((512, 1024), BF16)],
        specs=[SMEM] + [None] * 3, flops=1e9, nbytes=4e6,
    )
    ret_s, own_far, dqf = call(
        bwd_far, (qt, gt, stat2, pf, *bufs),
        [sds((512, 512), BF16), sds((512, 512), F32), sds((256, 128), F32)],
        scratch=[VM((1024, 128), BF16), VM((1024, 128), BF16)], flops=4e9, nbytes=5e6,
    )
    ret = swap(ret_s, "tm", 1)
    near_s, own_near, dqn = call(
        bwd_keys, (qt, gt, stat2, kvp, c1, near[0][1], near[1][1]),
        [sds((256, 512), BF16), sds((256, 512), F32), sds((256, 256), F32)],
        flops=4e9, nbytes=5e6,
    )

    def back(which, halo, gq_rows, halo_rows, more):
        return call(
            bind(bwd_near, which), (off, tm, qt, gt, stat2, kvp, halo, near[which][0], dqf, dqn, *more),
            [sds((512, 512), F32), rows(halo_rows), sds((gq_rows, 256), BF16)],
            specs=[SMEM] * 2 + [None] * (8 + len(more)),
            scratch=[VM((128, 256), BF16)], flops=4e9, nbytes=4e6,
        )

    own1, hn_s, gq1 = back(1, n1, 256, 256, ())
    own, hc_s, gq = back(0, c1, 512, 384, (own1, own_near, near_s, gq1))
    rest, y1s, y2as, y2bs = call(ret_y, (own_far, ret), [sds((256, 512), F32), rows(128), rows(64), rows(64)])
    yr = [swap(x, "tm", m) for x, m in ((y1s, 8), (y2as, 16), (y2bs, 24))]
    x1s, x2as, x2bs = call(ret_x, (rest, *yr), [rows(128), rows(64), rows(64)])
    xr = [swap(x, "tm", m) for x, m in ((x1s, 2), (x2as, 4), (x2bs, 6))]
    hc, hn = swap(hc_s, "tm", 1), side(hn_s)
    (acc,) = call(gather_own, (own, hc, hn, *yr), [sds((512, 512), F32)], nbytes=3e6)
    gk, gv = call(
        finish, (off, tm, acc, *xr), [sds((512, 256), BF16), sds((512, 256), BF16)],
        specs=[SMEM] * 2 + [None] * 4, flops=3e8, nbytes=3e6,
    )
    return mixed, gq, gk, gv


def solution(mesh):
    placed = (P("tm", "head"),) * 3 + (P("head", None), P("tm", None), P("head"), P("head"))
    return jax.shard_map(
        layer,
        mesh=mesh,
        in_specs=placed,
        out_specs=(P("tm", None), P("tm", "head"), P("tm", "head"), P("tm", "head")),
        check_vma=False,
    )
```

```python
import jax
import jax.numpy as jnp
from jax import lax
from jax.experimental import pallas as pl
from jax.experimental.pallas import tpu as pltpu
from jax.sharding import PartitionSpec as P


F32 = jnp.float32
BF16 = jnp.bfloat16
NEG = -1e30
NT = (((1,), (1,)), ((), ()))
SMEM = pl.BlockSpec(memory_space=pltpu.SMEM)


def sds(shape, dtype):
    return jax.ShapeDtypeStruct(shape, dtype)


def dot(a, b):
    return jnp.dot(a, b, preferred_element_type=F32)


def dot_nt(a, b):
    return lax.dot_general(a, b, NT, preferred_element_type=F32)


def call(body, ins, outs, scratch=(), flops=0, nbytes=0, specs=None, out_specs=None, vmem=24):
    full = lambda x: pl.BlockSpec(x.shape, (lambda *_: (0,) * len(x.shape)))
    specs = specs or [None] * len(ins)
    in_specs = [full(x) if s is None else s for x, s in zip(ins, specs)]
    out_specs = out_specs or [full(o) for o in outs]
    return pl.pallas_call(
        body,
        out_shape=outs,
        grid=(1,),
        in_specs=in_specs,
        out_specs=out_specs,
        scratch_shapes=list(scratch),
        cost_estimate=pl.CostEstimate(flops=int(flops), bytes_accessed=int(nbytes), transcendentals=0),
        compiler_params=pltpu.CompilerParams(vmem_limit_bytes=vmem << 20),
    )(*ins)


def iota(shape, axis):
    return lax.broadcasted_iota(jnp.int32, shape, axis)


def place_row(offset):
    n = iota((1, 256), 1)
    u = jnp.where(n >= 128, 2 * (n - 128) + 1, 4 * (n - 64) + 2)
    u = jnp.where(n >= 64, u, 8 * (n - 32) + 4)
    u = jnp.where(n >= 32, u, 16 * (n - 16) + 8)
    u = jnp.where(n >= 16, u, 32 * (n - 8) + 16)
    u = jnp.where(n >= 8, u, 32 * n)
    return (u + offset) & 255


def rank_row(offset):
    u = (iota((1, 256), 1) - offset) & 255
    n = jnp.where((u & 16) != 0, 8 + (u >> 5), u >> 5)
    n = jnp.where((u & 8) != 0, 16 + (u >> 4), n)
    n = jnp.where((u & 4) != 0, 32 + (u >> 3), n)
    n = jnp.where((u & 2) != 0, 64 + (u >> 2), n)
    return jnp.where((u & 1) != 0, 128 + (u >> 1), n)


def depth(n):
    d = jnp.where(n < 64, 2, 1)
    d = jnp.where(n < 32, 3, d)
    d = jnp.where(n < 16, 4, d)
    return jnp.where(n < 8, 5, d)


def to_depth(offset):
    return (iota((256, 256), 0) == rank_row(offset)).astype(F32).astype(BF16)


def from_depth(offset):
    return (iota((256, 256), 0) == place_row(offset)).astype(F32).astype(BF16)


def lane_first(rows, width=128):
    return (iota((rows, width), 1) % 128) < 64


def zero_pad(x, which):
    z = jnp.zeros_like(x)
    return jnp.concatenate([x, z] if which == 0 else [z, x], axis=0)


def transposed(x):
    return x.T


def parity(tm):
    return tm[0] & 1


def block_rows(tm, which):
    block = (1 - parity(tm)) if which == 0 else parity(tm)
    return pl.ds(pl.multiple_of(256 * block, 256), 256)


def prep_kv(tm, off_hbm, k, v, q, up, w, kvp, c1, n1, x1, x2, qv, upv, wv, kb, vb, off, sem):
    copies = []
    for src, dst in ((k, kb), (v, vb), (q, qv), (up, upv)):
        for which in range(2):
            copies.append(
                pltpu.make_async_copy(
                    src.at[block_rows(tm, which)], dst.at[pl.ds(256 * which, 256)], sem.at[len(copies)]
                )
            )
    copies.append(pltpu.make_async_copy(w, wv, sem.at[8]))
    table = pltpu.make_async_copy(off_hbm, off, sem.at[9])
    table.start()
    for c in copies:
        c.start()
    table.wait()
    perms = [to_depth(off[h]) for h in range(4)]
    for c in copies[:4]:
        c.wait()
    keep = lane_first(256, 256)
    for pair in range(2):
        lanes = slice(pair * 128, pair * 128 + 128)
        for b in range(2):
            rows = slice(b * 256, b * 256 + 256)
            kv = jnp.concatenate([kb[rows, lanes], vb[rows, lanes]], axis=1)
            kvp[rows, pair * 256 : pair * 256 + 256] = jnp.where(
                keep, dot(perms[2 * pair], kv), dot(perms[2 * pair + 1], kv)
            ).astype(BF16)
    x1[0:64] = kvp[0:64]
    x1[64:128] = kvp[256:320]
    x2[0:32] = kvp[0:32]
    x2[32:64] = kvp[256:288]
    c1[...] = kvp[0:384]
    n1[...] = kvp[256:512]
    for c in copies[4:]:
        c.wait()


def prep_qg(off, q, up, w, qt, gt):
    g = dot_nt(w[...], up[...]).astype(BF16)
    qs = (q[...].astype(F32) * 0.125).T.astype(BF16)
    for h in range(4):
        perm = from_depth(off[h])
        hs = slice(64 * h, 64 * h + 64)
        for b in range(2):
            bs = slice(256 * b, 256 * b + 256)
            x = jnp.concatenate([qs[hs, bs], g[hs, bs]], axis=0)
            r = dot(x, perm).astype(BF16)
            qt[b, hs] = r[0:64]
            gt[b, hs] = r[64:128]


def asm_y(kvp, x1, x2a, x2b, y1, y2, both):
    heads = [kvp[0:16], kvp[256:272], x1[0:16], x1[64:80], x2a[0:16], x2a[32:48], x2b[0:16], x2b[32:48]]
    heads = [h.astype(F32) for h in heads]
    y1[...] = jnp.concatenate(heads, axis=0).astype(BF16)
    y2[...] = jnp.concatenate([h[0:8] for h in heads], axis=0).astype(BF16)
    stack(x1, x2a, x2b, both)


def stack(*refs):
    out, at = refs[-1], 0
    for ref in refs[:-1]:
        out[at : at + ref.shape[0]] = ref[...]
        at += ref.shape[0]


def beside(left, right, out):
    out[:, 0 : left.shape[1]] = left[...]
    out[:, left.shape[1] :] = right[...]


def far_rows(bufs, lanes):
    mine_x, other_x, mine_y, other_y = bufs
    out = []
    for mine, other in ((mine_x, other_x), (mine_y, other_y)):
        for half in (slice(0, 128), slice(128, 256)):
            out += [mine[half, lanes], other[half, lanes]]
    return jnp.concatenate(out, axis=0)


def near_count():
    s = (128, 128)
    return jnp.minimum(depth(iota(s, 0)), depth(iota(s, 1))).astype(F32)


def near_keys(kv, c1, lanes):
    return jnp.concatenate([kv[0:128, lanes], kv[256:384, lanes], c1[0:128, lanes], c1[256:384, lanes]], axis=0)


def pair_slices(pair):
    return slice(256 * pair, 256 * pair + 128), slice(256 * pair + 128, 256 * pair + 256)


def side_chunks(which, kv, halo, lanes):
    own, other = slice(256 * which, 256 * which + 256), slice(256 - 256 * which, 512 - 256 * which)
    return [halo[0:256, lanes], kv[own, lanes], kv[other, lanes]]


def both_heads(x, y):
    return jnp.concatenate([zero_pad(x, 0), zero_pad(y, 1)], axis=1)


def fwd_near(which, off, win, tm, qt, kv, c1, *rest):
    if which == 0:
        halo = c1
        pw, p1, acc_out, stat, vt, v1t, dist, sw, s1 = rest
    else:
        halo, pw, p1, acc_out, stat, vt, v1t, dist, sw, s1 = rest
    count = near_count()
    count = jnp.concatenate([count, count], axis=1)
    sign = ((1 - 2 * parity(tm)) * (1 if which == 0 else -1)).astype(F32)
    tops, near_tops = [], []
    for pair in range(2):
        lo, hi = pair_slices(pair)
        heads = [2 * pair, 2 * pair + 1]
        vt[pair] = transposed(jnp.concatenate(side_chunks(which, kv, halo, hi), axis=0))
        v1t[pair] = transposed(near_keys(kv, c1, hi))
        for a, h in enumerate(heads):
            row = place_row(off[h]).astype(F32) * sign
            col = jnp.broadcast_to(row, (128, 256)).T
            dist[pair, :, 256 * a : 256 * a + 256] = jnp.concatenate([col, col], axis=1) - row
        reach = jnp.where(iota((1, 512), 1) < 256, win[heads[0]], win[heads[1]]).astype(F32)
        outer = reach - 256.0
        if which == 1:
            outer = jnp.where((tm[0] == 0) | (tm[0] == 31), -1000.0, outer)
        q0, q1 = [qt[which, 64 * h : 64 * h + 64, :] for h in heads]
        q = both_heads(q0, q1)
        top = None
        for c, keys in enumerate(side_chunks(which, kv, halo, lo)):
            sc = dot(keys, q)
            d = dist[pair]
            ok = (d <= outer, jnp.abs(d) <= reach, d >= 256.0 - reach)[c]
            sc = jnp.where(ok, sc, NEG)
            sw[pair, 256 * c : 256 * c + 256] = sc
            part = jnp.max(sc, axis=0, keepdims=True)
            top = part if top is None else jnp.maximum(top, part)
        sc = dot(near_keys(kv, c1, lo), both_heads(q0[:, 0:128], q1[:, 0:128]))
        s1[pair] = sc
        most = jnp.max(sc, axis=0, keepdims=True)
        first = jnp.maximum(top[:, 0:128], most[:, 0:128])
        second = jnp.maximum(top[:, 256:384], most[:, 128:256])
        near_tops.append(jnp.concatenate([first, second], axis=1))
        tops.append(jnp.concatenate([first, top[:, 128:256], second, top[:, 384:512]], axis=1))
    for pair in range(2):
        total = jnp.zeros((1, 512), F32)
        for c in range(3):
            e = jnp.exp(sw[pair, 256 * c : 256 * c + 256] - tops[pair])
            total += jnp.sum(e, axis=0, keepdims=True)
            pw[pair, 256 * c : 256 * c + 256, :] = e.astype(BF16)
        near_sum = jnp.zeros((1, 256), F32)
        for c in range(4):
            e = count * jnp.exp(s1[pair, 128 * c : 128 * c + 128] - near_tops[pair])
            near_sum += jnp.sum(e, axis=0, keepdims=True)
            p1[pair, 128 * c : 128 * c + 128, :] = e.astype(BF16)
        for a in range(2):
            h = 2 * pair + a
            vh, hs = slice(64 * a, 64 * a + 64), slice(64 * h, 64 * h + 64)
            at = 256 * a
            acc = dot(vt[pair, vh, :], pw[pair, :, at : at + 256])
            near_acc = dot(v1t[pair, vh, :], p1[pair, :, 128 * a : 128 * a + 128])
            acc_out[hs, 0:128] = acc[:, 0:128] + near_acc
            acc_out[hs, 128:256] = acc[:, 128:256]
            stat[h : h + 1, :] = tops[pair][:, at : at + 256]
            stat[4 + h : 5 + h, 0:128] = total[:, at : at + 128] + near_sum[:, 128 * a : 128 * a + 128]
            stat[4 + h : 5 + h, 128:256] = total[:, at + 128 : at + 256]


def far_count(level):
    s = (256 >> level, 128)
    both = jnp.minimum(depth(iota(s, 0)), depth(iota(s, 1) & 63))
    return jnp.maximum(both - level + 1, 0).astype(F32)


def far_lanes(x):
    return jnp.concatenate([x[:, 0:64], x[:, 256:320]], axis=1)


def far_cols(x, hs):
    return jnp.concatenate([x[0, hs, 0:64], x[1, hs, 0:64]], axis=1)


def wide(x, b, filler):
    rows = x.shape[0]
    return jnp.concatenate([x[:, 64 * b : 64 * b + 64], jnp.full((rows, 192), filler, F32)], axis=1)


def unperm_pair(off, pair, src):
    first, second = from_depth(off[2 * pair]), from_depth(off[2 * pair + 1])
    return jnp.where(lane_first(256), dot_nt(first, src), dot_nt(second, src)).astype(BF16)


def fwd_far(off, qt, gt, acc0, acc1, st0, st1, *rest):
    bufs, (pf, attn, stat2, vft, mult, at) = rest[:4], rest[4:]
    for level in range(2, 6):
        n = 256 >> level
        piece = far_count(level)
        for j in range(256 // n):
            mult[256 * (level - 2) + n * j : 256 * (level - 2) + n * j + n] = piece
    cnt = jnp.concatenate([mult[...], mult[...]], axis=1)
    scores, tops, sums, accs = [], [], [], []
    for pair in range(2):
        lo, hi = pair_slices(pair)
        vft[pair] = transposed(far_rows(bufs, hi))
        q = both_heads(*[far_cols(qt, slice(64 * h, 64 * h + 64)) for h in (2 * pair, 2 * pair + 1)])
        sc = jnp.where(cnt > 0, dot(far_rows(bufs, lo), q), NEG)
        tops.append(jnp.max(sc, axis=0, keepdims=True))
        scores.append(sc)
    for pair in range(2):
        e = cnt * jnp.exp(scores[pair] - tops[pair])
        sums.append(jnp.sum(e, axis=0, keepdims=True))
        pf[pair] = e.astype(BF16)
        for a in range(2):
            accs.append(dot(vft[pair, 64 * a : 64 * a + 64, :], pf[pair, :, 128 * a : 128 * a + 128]))
    for pair in range(2):
        for a in range(2):
            h = 2 * pair + a
            hs = slice(64 * h, 64 * h + 64)
            ftop, fsum = [x[pair][:, 128 * a : 128 * a + 128] for x in (tops, sums)]
            for b in range(2):
                bs = slice(256 * b, 256 * b + 256)
                acc_in, stat = (acc0, st0) if b == 0 else (acc1, st1)
                ntop, nsum = stat[h : h + 1, :], stat[4 + h : 5 + h, :]
                ftopw = wide(ftop, b, NEG)
                top = jnp.maximum(ntop, ftopw)
                wn, wf = jnp.exp(ntop - top), jnp.exp(ftopw - top)
                norm = nsum * wn + wide(fsum, b, 0.0) * wf
                acc = acc_in[hs, :] * wn + wide(accs[h], b, 0.0) * wf
                o = (acc / norm).astype(BF16)
                at[hs, bs] = o
                stat2[h : h + 1, bs] = wn / norm
                stat2[4 + h : 5 + h, bs] = wf / norm
                stat2[8 + h : 9 + h, bs] = jnp.sum(
                    gt[b, hs].astype(F32) * o.astype(F32), axis=0, keepdims=True
                )
        for b in range(2):
            bs = slice(256 * b, 256 * b + 256)
            attn[bs, 128 * pair : 128 * pair + 128] = unperm_pair(off, pair, at[128 * pair : 128 * pair + 128, bs])


def scaled(x, by):
    return (x.astype(F32) * by).astype(BF16)


def bwd_far(qt, gt, stat2, pf, *rest):
    bufs, (ret, own_far, dq) = rest[:4], rest[4:]
    keys, dps = [], []
    for pair in range(2):
        lo, hi = pair_slices(pair)
        keys.append(transposed(far_rows(bufs, lo)))
        g = both_heads(*[far_cols(gt, slice(64 * h, 64 * h + 64)) for h in (2 * pair, 2 * pair + 1)])
        dps.append(dot(far_rows(bufs, hi), g))
    for pair in range(2):
        lo, hi = pair_slices(pair)
        heads = (2 * pair, 2 * pair + 1)
        cf = [far_lanes(stat2[4 + h : 5 + h, :]) for h in heads]
        delta = jnp.concatenate([far_lanes(stat2[8 + h : 9 + h, :]) for h in heads], axis=1)
        qs = both_heads(*[scaled(far_cols(qt, slice(64 * h, 64 * h + 64)), c) for h, c in zip(heads, cf)])
        gs = both_heads(*[scaled(far_cols(gt, slice(64 * h, 64 * h + 64)), c) for h, c in zip(heads, cf)])
        ds = (pf[pair].astype(F32) * (dps[pair] - delta)).astype(BF16)
        dk, dv = dot_nt(ds, qs), dot_nt(pf[pair], gs)
        for a, h in enumerate(heads):
            dq[64 * h : 64 * h + 64, :] = (
                dot(keys[pair][64 * a : 64 * a + 64, :], ds[:, 128 * a : 128 * a + 128]) * cf[a]
            )
        for j in range(4):
            mine, theirs = slice(256 * j, 256 * j + 128), slice(256 * j + 128, 256 * j + 256)
            rows = slice(128 * j, 128 * j + 128)
            own_far[rows, lo] = dk[mine]
            own_far[rows, hi] = dv[mine]
            ret[rows, lo] = dk[theirs].astype(BF16)
            ret[rows, hi] = dv[theirs].astype(BF16)


def bwd_keys(qt, gt, stat2, kv, c1, p10, p11, ret, own_near, dq):
    def by_head(x, pair):
        return [
            jnp.concatenate([x[b, 64 * h : 64 * h + 64, 0:128] for b in range(2)], axis=1)
            for h in (2 * pair, 2 * pair + 1)
        ]

    def stats(row):
        return jnp.concatenate([stat2[row : row + 1, 0:128], stat2[row : row + 1, 256:384]], axis=1)

    dps = []
    for pair in range(2):
        dps.append(dot(near_keys(kv, c1, pair_slices(pair)[1]), both_heads(*by_head(gt, pair))))
    for pair in range(2):
        lo, hi = pair_slices(pair)
        heads = (2 * pair, 2 * pair + 1)
        k1t = transposed(near_keys(kv, c1, lo))
        cn = [stats(h) for h in heads]
        delta = jnp.concatenate([stats(8 + h) for h in heads], axis=1)
        left, right = p10[pair], p11[pair]
        p = jnp.concatenate([left[:, 0:128], right[:, 0:128], left[:, 128:256], right[:, 128:256]], axis=1)
        ds = (p.astype(F32) * (dps[pair] - delta)).astype(BF16)
        qs = both_heads(*[scaled(x, c) for x, c in zip(by_head(qt, pair), cn)])
        gs = both_heads(*[scaled(x, c) for x, c in zip(by_head(gt, pair), cn)])
        dk, dv = dot_nt(ds, qs), dot_nt(p, gs)
        for a, h in enumerate(heads):
            dq[64 * h : 64 * h + 64, :] = dot(k1t[64 * a : 64 * a + 64, :], ds[:, 256 * a : 256 * a + 256]) * cn[a]
        own_near[:, lo] = dk[0:256]
        own_near[:, hi] = dv[0:256]
        ret[:, lo] = dk[256:512].astype(BF16)
        ret[:, hi] = dv[256:512].astype(BF16)


def bwd_near(which, off, tm, qt, gt, stat2, kv, halo, pw, dqf, dqn, *rest):
    if which == 1:
        own, halo_out, gq, dqt, dps = rest
    else:
        own_in, own_near, near_s, gq_in, own, halo_out, gq, dqt, dps = rest
        halo_out[256:384] = near_s[128:256]
        gq[block_rows(tm, 1), :] = gq_in[...]
    bs = slice(256 * which, 256 * which + 256)
    ob = slice(256 - 256 * which, 512 - 256 * which)
    for pair in range(2):
        vx = jnp.concatenate(side_chunks(which, kv, halo, pair_slices(pair)[1]), axis=0)
        dps[pair] = dot(vx, both_heads(*[gt[which, 64 * h : 64 * h + 64] for h in (2 * pair, 2 * pair + 1)]))
    for pair in range(2):
        lo, hi = pair_slices(pair)
        heads = (2 * pair, 2 * pair + 1)
        kt = transposed(jnp.concatenate(side_chunks(which, kv, halo, lo), axis=0))
        cn = [stat2[h : h + 1, bs] for h in heads]
        delta = jnp.concatenate([stat2[8 + h : 9 + h, bs] for h in heads], axis=1)
        ds = (pw[pair].astype(F32) * (dps[pair] - delta)).astype(BF16)
        qs = both_heads(*[scaled(qt[which, 64 * h : 64 * h + 64], c) for h, c in zip(heads, cn)])
        gs = both_heads(*[scaled(gt[which, 64 * h : 64 * h + 64], c) for h, c in zip(heads, cn)])
        for a, h in enumerate(heads):
            hs, vh = slice(64 * h, 64 * h + 64), slice(64 * a, 64 * a + 64)
            near = jnp.concatenate(
                [dqn[hs, 128 * which : 128 * which + 128], jnp.zeros((64, 128), F32)], axis=1
            )
            total = dot(kt[vh, :], ds[:, 256 * a : 256 * a + 256]) * cn[a] + near + wide(dqf[hs, :], which, 0.0)
            dqt[pair, vh, :] = (total * 0.125).astype(BF16)
        for lanes, left, right in ((lo, ds, qs), (hi, pw[pair], gs)):
            d = dot_nt(left, right)
            if which == 1:
                halo_out[:, lanes] = d[0:256].astype(BF16)
                own[bs, lanes] = d[256:512]
                own[ob, lanes] = d[512:768]
            else:
                halo_out[0:128, lanes] = (d[0:128] + near_s[0:128, lanes].astype(F32)).astype(BF16)
                halo_out[128:256, lanes] = d[128:256].astype(BF16)
                own[bs, lanes] = d[256:512] + own_in[bs, lanes]
                own[ob, lanes] = d[512:768] + own_in[ob, lanes]
                own[0:128, lanes] += own_near[0:128, lanes]
                own[256:384, lanes] += own_near[128:256, lanes]
        r = unperm_pair(off, pair, dqt[pair])
        if which == 1:
            gq[:, 128 * pair : 128 * pair + 128] = r
        else:
            gq[block_rows(tm, 0), 128 * pair : 128 * pair + 128] = r


def ret_y(own_far, ret, rest, y1, y2a, y2b):
    total = own_far[...] + ret[...].astype(F32)
    rest[...] = total[0:256]
    y1[...] = total[256:384].astype(BF16)
    y2a[...] = total[384:448].astype(BF16)
    y2b[...] = total[448:512].astype(BF16)


def ret_x(rest, y1, y2a, y2b, x1, x2a, x2b):
    deep = y1[...].astype(F32)
    deeper = y2a[...].astype(F32) + y2b[...].astype(F32)
    total = []
    for j, at in enumerate((0, 64, 128, 160, 192, 224)):
        size = 64 if at < 128 else 32
        top = deep[32 + 16 * j : 48 + 16 * j]
        head = rest[at : at + 16] + top
        total += [head[0:8] + deeper[16 + 8 * j : 24 + 8 * j], head[8:16], rest[at + 16 : at + size]]
    x1[...] = jnp.concatenate(total[0:6], axis=0).astype(BF16)
    x2a[...] = jnp.concatenate(total[6:12], axis=0).astype(BF16)
    x2b[...] = jnp.concatenate(total[12:18], axis=0).astype(BF16)


def gather_own(own, hc, hn, y1, y2a, y2b, acc):
    acc[...] = own[...]
    acc[0:384] += hc[...].astype(F32)
    acc[256:512] += hn[...].astype(F32)
    for b in range(2):
        at = 256 * b
        acc[at : at + 16] += y1[16 * b : 16 * b + 16].astype(F32)
        acc[at : at + 8] += (y2a[0:16].astype(F32) + y2b[0:16].astype(F32))[8 * b : 8 * b + 8]


def finish(off, tm, acc, x1, x2a, x2b, gk, gv):
    keep = lane_first(256, 256)
    for pair in range(2):
        first, second = from_depth(off[2 * pair]), from_depth(off[2 * pair + 1])
        lanes = slice(128 * pair, 128 * pair + 128)
        cols = slice(256 * pair, 256 * pair + 256)
        for b in range(2):
            at = 256 * b
            head = acc[at : at + 64, cols] + x1[64 * b : 64 * b + 64, cols].astype(F32)
            deep = x2a[32 * b : 32 * b + 32, cols].astype(F32) + x2b[32 * b : 32 * b + 32, cols].astype(F32)
            x = jnp.concatenate([head[0:32] + deep, head[32:64], acc[at + 64 : at + 256, cols]], axis=0).astype(BF16)
            r = jnp.where(keep, dot(first, x), dot(second, x)).astype(BF16)
            gk[block_rows(tm, b), lanes] = r[:, 0:128]
            gv[block_rows(tm, b), lanes] = r[:, 128:256]


def half_rows(tm, w, out):
    out[...] = w[pl.ds(pl.multiple_of(128 * parity(tm), 128), 128), :]


def asm_w(tm, own, first, other, mine, theirs, out):
    out[0:256] = own[...]
    out[256:512] = first[...]
    out[512:768] = other[...]
    p = parity(tm)
    out[pl.ds(pl.multiple_of(768 + 128 * p, 128), 128), :] = mine[...]
    out[pl.ds(pl.multiple_of(896 - 128 * p, 128), 128), :] = theirs[...]


def project(tm, a01, a23, w, out):
    r = dot(jnp.concatenate([a01[...], a23[...]], axis=1), w[...]).astype(BF16)
    out[block_rows(tm, 0), :] = r[0:256]
    out[block_rows(tm, 1), :] = r[256:512]


def swap(x, axis, mask):
    return lax.ppermute(x, axis, [(i, i ^ mask) for i in range(lax.axis_size(axis))])


def cross(x, masks):
    heads = lax.axis_size("head")
    pairs = []
    for i in range(lax.axis_size("tm")):
        pairs += [(i * heads + z, i * heads + (z ^ masks[i % 2])) for z in range(heads)]
    return lax.ppermute(x, ("tm", "head"), pairs)


def side(x):
    pairs = [(i, i + 1 if i % 2 else i - 1) for i in range(1, lax.axis_size("tm") - 1)]
    return lax.ppermute(x, "tm", pairs)


def bind(f, *args):
    def body(*refs):
        f(*args, *refs)

    return body


def layer(q, k, v, w, up, win, off):
    tm = lax.axis_index("tm").astype(jnp.int32).reshape(1)
    VM = pltpu.VMEM
    hbm = pl.BlockSpec(memory_space=pltpu.HBM)
    rows = lambda n: sds((n, 512), BF16)
    kvp, c1s, n1s, x1s, x2s, qv, upv, wv = call(
        prep_kv, (tm,) + tuple(pltpu.with_memory_space_constraint(x, pltpu.HBM) for x in (off, k, v, q, up, w)),
        [rows(512), rows(384), rows(256), rows(128), rows(64),
         sds((512, 256), BF16), sds((512, 1024), BF16), sds((256, 1024), BF16)],
        specs=[SMEM] + [hbm] * 6,
        scratch=[VM((512, 256), BF16), VM((512, 256), BF16), pltpu.SMEM((4,), jnp.int32), pltpu.SemaphoreType.DMA((10,))],
        flops=3e8, nbytes=3e6,
    )
    x1, x2a, x2b = swap(x1s, "tm", 2), swap(x2s, "tm", 4), swap(x2s, "tm", 6)
    c1 = swap(c1s, "tm", 1)
    n1 = side(n1s)
    w1 = cross(wv, (1, 3))
    (w1h,) = call(half_rows, (tm, w1), [sds((128, 1024), BF16)], specs=[SMEM, None])
    w2 = cross(w1h, (3, 1))
    (w_all,) = call(
        asm_w, (tm, wv, w1, swap(w1, "tm", 1), w2, swap(w2, "tm", 1)),
        [sds((1024, 1024), BF16)], specs=[SMEM] + [None] * 5, nbytes=4e6,
    )
    qt, gt = call(
        prep_qg, (off, qv, upv, wv), [sds((2, 256, 256), BF16), sds((2, 256, 256), BF16)],
        specs=[SMEM] + [None] * 3, flops=6e8, nbytes=3e6,
    )
    near = []
    for which in range(2):
        near.append(
            call(
                bind(fwd_near, which), (off, win, tm, qt, kvp, c1) + ((n1,) if which else ()),
                [sds((2, 768, 512), BF16), sds((2, 512, 256), BF16), sds((256, 256), F32), sds((8, 256), F32)],
                specs=[SMEM] * 3 + [None] * (3 + which),
                scratch=[
                    VM((2, 128, 768), BF16), VM((2, 128, 512), BF16),
                    VM((2, 256, 512), F32), VM((2, 768, 512), F32), VM((2, 512, 256), F32),
                ],
                flops=3e9, nbytes=4e6,
            )
        )
    y1s, y2s, mine_x = call(asm_y, (kvp, x1, x2a, x2b), [rows(128), rows(64), rows(256)])
    y1, y2a, y2b = swap(y1s, "tm", 8), swap(y2s, "tm", 16), swap(y2s, "tm", 24)
    (mine_y,) = call(stack, (y1, y2a, y2b), [rows(256)])
    bufs = (mine_x, swap(mine_x, "tm", 1), mine_y, swap(mine_y, "tm", 1))
    pf, attn, stat2 = call(
        fwd_far, (off, qt, gt, near[0][2], near[1][2], near[0][3], near[1][3], *bufs),
        [sds((2, 1024, 256), BF16), sds((512, 256), BF16), sds((16, 512), F32)],
        specs=[SMEM] + [None] * 10,
        scratch=[VM((2, 128, 1024), BF16), VM((1024, 128), F32), VM((256, 512), BF16)],
        flops=3e9, nbytes=4e6,
    )
    a1 = cross(attn, (1, 3))
    (a01,) = call(beside, (attn, a1), [rows(512)])
    a23 = cross(a01, (3, 1))
    (mixed,) = call(
        project, (tm, a01, a23, w_all), [sds((512, 1024), BF16)],
        specs=[SMEM] + [None] * 3, flops=1e9, nbytes=4e6,
    )
    ret_s, own_far, dqf = call(
        bwd_far, (qt, gt, stat2, pf, *bufs),
        [sds((512, 512), BF16), sds((512, 512), F32), sds((256, 128), F32)],
        flops=4e9, nbytes=5e6,
    )
    ret = swap(ret_s, "tm", 1)
    near_s, own_near, dqn = call(
        bwd_keys, (qt, gt, stat2, kvp, c1, near[0][1], near[1][1]),
        [sds((256, 512), BF16), sds((256, 512), F32), sds((256, 256), F32)],
        flops=4e9, nbytes=5e6,
    )

    def back(which, halo, gq_rows, halo_rows, more):
        return call(
            bind(bwd_near, which), (off, tm, qt, gt, stat2, kvp, halo, near[which][0], dqf, dqn, *more),
            [sds((512, 512), F32), rows(halo_rows), sds((gq_rows, 256), BF16)],
            specs=[SMEM] * 2 + [None] * (8 + len(more)),
            scratch=[VM((2, 128, 256), BF16), VM((2, 768, 512), F32)], flops=4e9, nbytes=4e6,
        )

    own1, hn_s, gq1 = back(1, n1, 256, 256, ())
    own, hc_s, gq = back(0, c1, 512, 384, (own1, own_near, near_s, gq1))
    rest, y1s, y2as, y2bs = call(ret_y, (own_far, ret), [sds((256, 512), F32), rows(128), rows(64), rows(64)])
    yr = [swap(x, "tm", m) for x, m in ((y1s, 8), (y2as, 16), (y2bs, 24))]
    x1s, x2as, x2bs = call(ret_x, (rest, *yr), [rows(128), rows(64), rows(64)])
    xr = [swap(x, "tm", m) for x, m in ((x1s, 2), (x2as, 4), (x2bs, 6))]
    hc, hn = swap(hc_s, "tm", 1), side(hn_s)
    (acc,) = call(gather_own, (own, hc, hn, *yr), [sds((512, 512), F32)], nbytes=3e6)
    gk, gv = call(
        finish, (off, tm, acc, *xr), [sds((512, 256), BF16), sds((512, 256), BF16)],
        specs=[SMEM] * 2 + [None] * 4, flops=3e8, nbytes=3e6,
    )
    return mixed, gq, gk, gv


def solution(mesh):
    placed = (P("tm", "head"),) * 3 + (P("head", None), P("tm", None), P("head"), P("head"))
    return jax.shard_map(
        layer,
        mesh=mesh,
        in_specs=placed,
        out_specs=(P("tm", None), P("tm", "head"), P("tm", "head"), P("tm", "head")),
        check_vma=False,
    )
```

```python
import jax
import jax.numpy as jnp
from jax import lax
from jax.experimental import pallas as pl
from jax.experimental.pallas import tpu as pltpu
from jax.sharding import PartitionSpec as P


F32 = jnp.float32
BF16 = jnp.bfloat16
NEG = -1e30
NT = (((1,), (1,)), ((), ()))
SMEM = pl.BlockSpec(memory_space=pltpu.SMEM)


def sds(shape, dtype):
    return jax.ShapeDtypeStruct(shape, dtype)


def dot(a, b):
    return jnp.dot(a, b, preferred_element_type=F32)


def dot_nt(a, b):
    return lax.dot_general(a, b, NT, preferred_element_type=F32)


def call(body, ins, outs, scratch=(), flops=0, nbytes=0, specs=None, out_specs=None, vmem=24):
    full = lambda x: pl.BlockSpec(x.shape, (lambda *_: (0,) * len(x.shape)))
    specs = specs or [None] * len(ins)
    in_specs = [full(x) if s is None else s for x, s in zip(ins, specs)]
    out_specs = out_specs or [full(o) for o in outs]
    return pl.pallas_call(
        body,
        out_shape=outs,
        grid=(1,),
        in_specs=in_specs,
        out_specs=out_specs,
        scratch_shapes=list(scratch),
        cost_estimate=pl.CostEstimate(flops=int(flops), bytes_accessed=int(nbytes), transcendentals=0),
        compiler_params=pltpu.CompilerParams(vmem_limit_bytes=vmem << 20),
    )(*ins)


def iota(shape, axis):
    return lax.broadcasted_iota(jnp.int32, shape, axis)


def place_row(offset):
    n = iota((1, 256), 1)
    u = jnp.where(n >= 128, 2 * (n - 128) + 1, 4 * (n - 64) + 2)
    u = jnp.where(n >= 64, u, 8 * (n - 32) + 4)
    u = jnp.where(n >= 32, u, 16 * (n - 16) + 8)
    u = jnp.where(n >= 16, u, 32 * (n - 8) + 16)
    u = jnp.where(n >= 8, u, 32 * n)
    return (u + offset) & 255


def rank_row(offset):
    u = (iota((1, 256), 1) - offset) & 255
    n = jnp.where((u & 16) != 0, 8 + (u >> 5), u >> 5)
    n = jnp.where((u & 8) != 0, 16 + (u >> 4), n)
    n = jnp.where((u & 4) != 0, 32 + (u >> 3), n)
    n = jnp.where((u & 2) != 0, 64 + (u >> 2), n)
    return jnp.where((u & 1) != 0, 128 + (u >> 1), n)


def depth(n):
    d = jnp.where(n < 64, 2, 1)
    d = jnp.where(n < 32, 3, d)
    d = jnp.where(n < 16, 4, d)
    return jnp.where(n < 8, 5, d)


def to_depth(offset):
    return (iota((256, 256), 0) == rank_row(offset)).astype(F32).astype(BF16)


def from_depth(offset):
    return (iota((256, 256), 0) == place_row(offset)).astype(F32).astype(BF16)


def lane_first(rows, width=128):
    return (iota((rows, width), 1) % 128) < 64


def zero_pad(x, which):
    z = jnp.zeros_like(x)
    return jnp.concatenate([x, z] if which == 0 else [z, x], axis=0)


def transposed(x):
    return x.T


def parity(tm):
    return tm[0] & 1


def block_rows(tm, which):
    block = (1 - parity(tm)) if which == 0 else parity(tm)
    return pl.ds(pl.multiple_of(256 * block, 256), 256)


def prep_kv(tm, off_hbm, k, v, q, up, w, kvp, c1, n1, x1, x2, qv, upv, wv, kb, vb, off, sem):
    copies = []
    for src, dst in ((k, kb), (v, vb), (q, qv), (up, upv)):
        for which in range(2):
            copies.append(
                pltpu.make_async_copy(
                    src.at[block_rows(tm, which)], dst.at[pl.ds(256 * which, 256)], sem.at[len(copies)]
                )
            )
    copies.append(pltpu.make_async_copy(w, wv, sem.at[8]))
    table = pltpu.make_async_copy(off_hbm, off, sem.at[9])
    table.start()
    for c in copies:
        c.start()
    table.wait()
    perms = [to_depth(off[h]) for h in range(4)]
    for c in copies[:4]:
        c.wait()
    keep = lane_first(256, 256)
    for pair in range(2):
        lanes = slice(pair * 128, pair * 128 + 128)
        for b in range(2):
            rows = slice(b * 256, b * 256 + 256)
            kv = jnp.concatenate([kb[rows, lanes], vb[rows, lanes]], axis=1)
            kvp[rows, pair * 256 : pair * 256 + 256] = jnp.where(
                keep, dot(perms[2 * pair], kv), dot(perms[2 * pair + 1], kv)
            ).astype(BF16)
    x1[0:64] = kvp[0:64]
    x1[64:128] = kvp[256:320]
    x2[0:32] = kvp[0:32]
    x2[32:64] = kvp[256:288]
    c1[...] = kvp[0:384]
    n1[...] = kvp[256:512]
    for c in copies[4:]:
        c.wait()


def prep_qg(off, q, up, w, qt, gt):
    g = dot_nt(w[...], up[...]).astype(BF16)
    qs = (q[...].astype(F32) * 0.125).T.astype(BF16)
    for h in range(4):
        perm = from_depth(off[h])
        hs = slice(64 * h, 64 * h + 64)
        for b in range(2):
            bs = slice(256 * b, 256 * b + 256)
            x = jnp.concatenate([qs[hs, bs], g[hs, bs]], axis=0)
            r = dot(x, perm).astype(BF16)
            qt[b, hs] = r[0:64]
            gt[b, hs] = r[64:128]


def asm_y(kvp, x1, x2a, x2b, y1, y2, both):
    heads = [kvp[0:16], kvp[256:272], x1[0:16], x1[64:80], x2a[0:16], x2a[32:48], x2b[0:16], x2b[32:48]]
    heads = [h.astype(F32) for h in heads]
    y1[...] = jnp.concatenate(heads, axis=0).astype(BF16)
    y2[...] = jnp.concatenate([h[0:8] for h in heads], axis=0).astype(BF16)
    stack(x1, x2a, x2b, both)


def stack(*refs):
    out, at = refs[-1], 0
    for ref in refs[:-1]:
        out[at : at + ref.shape[0]] = ref[...]
        at += ref.shape[0]


def beside(left, right, out):
    out[:, 0 : left.shape[1]] = left[...]
    out[:, left.shape[1] :] = right[...]


def far_rows(bufs, lanes):
    mine_x, other_x, mine_y, other_y = bufs
    out = []
    for mine, other in ((mine_x, other_x), (mine_y, other_y)):
        for half in (slice(0, 128), slice(128, 256)):
            out += [mine[half, lanes], other[half, lanes]]
    return jnp.concatenate(out, axis=0)


def near_count():
    s = (128, 128)
    return jnp.minimum(depth(iota(s, 0)), depth(iota(s, 1))).astype(F32)


def near_keys(kv, c1, lanes):
    return jnp.concatenate([kv[0:128, lanes], kv[256:384, lanes], c1[0:128, lanes], c1[256:384, lanes]], axis=0)


def pair_slices(pair):
    return slice(256 * pair, 256 * pair + 128), slice(256 * pair + 128, 256 * pair + 256)


def side_chunks(which, kv, halo, lanes):
    own, other = slice(256 * which, 256 * which + 256), slice(256 - 256 * which, 512 - 256 * which)
    return [halo[0:256, lanes], kv[own, lanes], kv[other, lanes]]


def both_heads(x, y):
    return jnp.concatenate([zero_pad(x, 0), zero_pad(y, 1)], axis=1)


def fwd_near(which, off, win, tm, qt, kv, c1, *rest):
    if which == 0:
        halo = c1
        pw, p1, acc_out, stat, vt, v1t, dist, sw, s1 = rest
    else:
        halo, pw, p1, acc_out, stat, vt, v1t, dist, sw, s1 = rest
    count = near_count()
    count = jnp.concatenate([count, count], axis=1)
    sign = ((1 - 2 * parity(tm)) * (1 if which == 0 else -1)).astype(F32)
    tops, near_tops = [], []
    for pair in range(2):
        lo, hi = pair_slices(pair)
        heads = [2 * pair, 2 * pair + 1]
        vt[pair] = transposed(jnp.concatenate(side_chunks(which, kv, halo, hi), axis=0))
        v1t[pair] = transposed(near_keys(kv, c1, hi))
        for a, h in enumerate(heads):
            row = place_row(off[h]).astype(F32) * sign
            col = jnp.broadcast_to(row, (128, 256)).T
            dist[pair, :, 256 * a : 256 * a + 256] = jnp.concatenate([col, col], axis=1) - row
        reach = jnp.where(iota((1, 512), 1) < 256, win[heads[0]], win[heads[1]]).astype(F32)
        outer = reach - 256.0
        if which == 1:
            outer = jnp.where((tm[0] == 0) | (tm[0] == 31), -1000.0, outer)
        q0, q1 = [qt[which, 64 * h : 64 * h + 64, :] for h in heads]
        q = both_heads(q0, q1)
        top = None
        for c, keys in enumerate(side_chunks(which, kv, halo, lo)):
            sc = dot(keys, q)
            d = dist[pair]
            ok = (d <= outer, jnp.abs(d) <= reach, d >= 256.0 - reach)[c]
            sc = jnp.where(ok, sc, NEG)
            sw[pair, 256 * c : 256 * c + 256] = sc
            part = jnp.max(sc, axis=0, keepdims=True)
            top = part if top is None else jnp.maximum(top, part)
        sc = dot(near_keys(kv, c1, lo), both_heads(q0[:, 0:128], q1[:, 0:128]))
        s1[pair] = sc
        most = jnp.max(sc, axis=0, keepdims=True)
        first = jnp.maximum(top[:, 0:128], most[:, 0:128])
        second = jnp.maximum(top[:, 256:384], most[:, 128:256])
        near_tops.append(jnp.concatenate([first, second], axis=1))
        tops.append(jnp.concatenate([first, top[:, 128:256], second, top[:, 384:512]], axis=1))
    for pair in range(2):
        total = jnp.zeros((1, 512), F32)
        for c in range(3):
            e = jnp.exp(sw[pair, 256 * c : 256 * c + 256] - tops[pair])
            total += jnp.sum(e, axis=0, keepdims=True)
            pw[pair, 256 * c : 256 * c + 256, :] = e.astype(BF16)
        near_sum = jnp.zeros((1, 256), F32)
        for c in range(4):
            e = count * jnp.exp(s1[pair, 128 * c : 128 * c + 128] - near_tops[pair])
            near_sum += jnp.sum(e, axis=0, keepdims=True)
            p1[pair, 128 * c : 128 * c + 128, :] = e.astype(BF16)
        for a in range(2):
            h = 2 * pair + a
            vh, hs = slice(64 * a, 64 * a + 64), slice(64 * h, 64 * h + 64)
            at = 256 * a
            acc = dot(vt[pair, vh, :], pw[pair, :, at : at + 256])
            near_acc = dot(v1t[pair, vh, :], p1[pair, :, 128 * a : 128 * a + 128])
            acc_out[hs, 0:128] = acc[:, 0:128] + near_acc
            acc_out[hs, 128:256] = acc[:, 128:256]
            stat[h : h + 1, :] = tops[pair][:, at : at + 256]
            stat[4 + h : 5 + h, 0:128] = total[:, at : at + 128] + near_sum[:, 128 * a : 128 * a + 128]
            stat[4 + h : 5 + h, 128:256] = total[:, at + 128 : at + 256]


def far_count(level):
    s = (256 >> level, 128)
    both = jnp.minimum(depth(iota(s, 0)), depth(iota(s, 1) & 63))
    return jnp.maximum(both - level + 1, 0).astype(F32)


def far_lanes(x):
    return jnp.concatenate([x[:, 0:64], x[:, 256:320]], axis=1)


def far_cols(x, hs):
    return jnp.concatenate([x[0, hs, 0:64], x[1, hs, 0:64]], axis=1)


def wide(x, b, filler):
    rows = x.shape[0]
    return jnp.concatenate([x[:, 64 * b : 64 * b + 64], jnp.full((rows, 192), filler, F32)], axis=1)


def unperm_pair(off, pair, src):
    first, second = from_depth(off[2 * pair]), from_depth(off[2 * pair + 1])
    return jnp.where(lane_first(256), dot_nt(first, src), dot_nt(second, src)).astype(BF16)


def fwd_far(off, qt, gt, acc0, acc1, st0, st1, *rest):
    bufs, (pf, attn, stat2, vft, mult, at) = rest[:4], rest[4:]
    for level in range(2, 6):
        n = 256 >> level
        piece = far_count(level)
        for j in range(256 // n):
            mult[256 * (level - 2) + n * j : 256 * (level - 2) + n * j + n] = piece
    cnt = jnp.concatenate([mult[...], mult[...]], axis=1)
    scores, tops, sums, accs = [], [], [], []
    for pair in range(2):
        lo, hi = pair_slices(pair)
        vft[pair] = transposed(far_rows(bufs, hi))
        q = both_heads(*[far_cols(qt, slice(64 * h, 64 * h + 64)) for h in (2 * pair, 2 * pair + 1)])
        sc = jnp.where(cnt > 0, dot(far_rows(bufs, lo), q), NEG)
        tops.append(jnp.max(sc, axis=0, keepdims=True))
        scores.append(sc)
    for pair in range(2):
        e = cnt * jnp.exp(scores[pair] - tops[pair])
        sums.append(jnp.sum(e, axis=0, keepdims=True))
        pf[pair] = e.astype(BF16)
        for a in range(2):
            accs.append(dot(vft[pair, 64 * a : 64 * a + 64, :], pf[pair, :, 128 * a : 128 * a + 128]))
    for pair in range(2):
        for a in range(2):
            h = 2 * pair + a
            hs = slice(64 * h, 64 * h + 64)
            ftop, fsum = [x[pair][:, 128 * a : 128 * a + 128] for x in (tops, sums)]
            for b in range(2):
                bs = slice(256 * b, 256 * b + 256)
                acc_in, stat = (acc0, st0) if b == 0 else (acc1, st1)
                ntop, nsum = stat[h : h + 1, :], stat[4 + h : 5 + h, :]
                ftopw = wide(ftop, b, NEG)
                top = jnp.maximum(ntop, ftopw)
                wn, wf = jnp.exp(ntop - top), jnp.exp(ftopw - top)
                norm = nsum * wn + wide(fsum, b, 0.0) * wf
                acc = acc_in[hs, :] * wn + wide(accs[h], b, 0.0) * wf
                o = (acc / norm).astype(BF16)
                at[hs, bs] = o
                stat2[h : h + 1, bs] = wn / norm
                stat2[4 + h : 5 + h, bs] = wf / norm
                stat2[8 + h : 9 + h, bs] = jnp.sum(
                    gt[b, hs].astype(F32) * o.astype(F32), axis=0, keepdims=True
                )
        for b in range(2):
            bs = slice(256 * b, 256 * b + 256)
            attn[bs, 128 * pair : 128 * pair + 128] = unperm_pair(off, pair, at[128 * pair : 128 * pair + 128, bs])


def scaled(x, by):
    return (x.astype(F32) * by).astype(BF16)


def bwd_far(qt, gt, stat2, pf, *rest):
    bufs, (ret, own_far, dq) = rest[:4], rest[4:]
    keys, dps = [], []
    for pair in range(2):
        lo, hi = pair_slices(pair)
        keys.append(transposed(far_rows(bufs, lo)))
        g = both_heads(*[far_cols(gt, slice(64 * h, 64 * h + 64)) for h in (2 * pair, 2 * pair + 1)])
        dps.append(dot(far_rows(bufs, hi), g))
    for pair in range(2):
        lo, hi = pair_slices(pair)
        heads = (2 * pair, 2 * pair + 1)
        cf = [far_lanes(stat2[4 + h : 5 + h, :]) for h in heads]
        delta = jnp.concatenate([far_lanes(stat2[8 + h : 9 + h, :]) for h in heads], axis=1)
        qs = both_heads(*[scaled(far_cols(qt, slice(64 * h, 64 * h + 64)), c) for h, c in zip(heads, cf)])
        gs = both_heads(*[scaled(far_cols(gt, slice(64 * h, 64 * h + 64)), c) for h, c in zip(heads, cf)])
        ds = (pf[pair].astype(F32) * (dps[pair] - delta)).astype(BF16)
        dk, dv = dot_nt(ds, qs), dot_nt(pf[pair], gs)
        for a, h in enumerate(heads):
            dq[64 * h : 64 * h + 64, :] = (
                dot(keys[pair][64 * a : 64 * a + 64, :], ds[:, 128 * a : 128 * a + 128]) * cf[a]
            )
        for j in range(4):
            mine, theirs = slice(256 * j, 256 * j + 128), slice(256 * j + 128, 256 * j + 256)
            rows = slice(128 * j, 128 * j + 128)
            own_far[rows, lo] = dk[mine]
            own_far[rows, hi] = dv[mine]
            ret[rows, lo] = dk[theirs].astype(BF16)
            ret[rows, hi] = dv[theirs].astype(BF16)


def bwd_keys(qt, gt, stat2, kv, c1, p10, p11, ret, own_near, dq):
    def by_head(x, pair):
        return [
            jnp.concatenate([x[b, 64 * h : 64 * h + 64, 0:128] for b in range(2)], axis=1)
            for h in (2 * pair, 2 * pair + 1)
        ]

    def stats(row):
        return jnp.concatenate([stat2[row : row + 1, 0:128], stat2[row : row + 1, 256:384]], axis=1)

    dps = []
    for pair in range(2):
        dps.append(dot(near_keys(kv, c1, pair_slices(pair)[1]), both_heads(*by_head(gt, pair))))
    for pair in range(2):
        lo, hi = pair_slices(pair)
        heads = (2 * pair, 2 * pair + 1)
        k1t = transposed(near_keys(kv, c1, lo))
        cn = [stats(h) for h in heads]
        delta = jnp.concatenate([stats(8 + h) for h in heads], axis=1)
        left, right = p10[pair], p11[pair]
        p = jnp.concatenate([left[:, 0:128], right[:, 0:128], left[:, 128:256], right[:, 128:256]], axis=1)
        ds = (p.astype(F32) * (dps[pair] - delta)).astype(BF16)
        qs = both_heads(*[scaled(x, c) for x, c in zip(by_head(qt, pair), cn)])
        gs = both_heads(*[scaled(x, c) for x, c in zip(by_head(gt, pair), cn)])
        dk, dv = dot_nt(ds, qs), dot_nt(p, gs)
        for a, h in enumerate(heads):
            dq[64 * h : 64 * h + 64, :] = dot(k1t[64 * a : 64 * a + 64, :], ds[:, 256 * a : 256 * a + 256]) * cn[a]
        own_near[:, lo] = dk[0:256]
        own_near[:, hi] = dv[0:256]
        ret[:, lo] = dk[256:512].astype(BF16)
        ret[:, hi] = dv[256:512].astype(BF16)


def bwd_near(which, off, tm, qt, gt, stat2, kv, halo, pw, dqf, dqn, *rest):
    if which == 1:
        own, halo_out, gq, dqt, dps = rest
    else:
        own_in, own_near, near_s, gq_in, own, halo_out, gq, dqt, dps = rest
        halo_out[256:384] = near_s[128:256]
        gq[block_rows(tm, 1), :] = gq_in[...]
    bs = slice(256 * which, 256 * which + 256)
    ob = slice(256 - 256 * which, 512 - 256 * which)
    for pair in range(2):
        vx = jnp.concatenate(side_chunks(which, kv, halo, pair_slices(pair)[1]), axis=0)
        dps[pair] = dot(vx, both_heads(*[gt[which, 64 * h : 64 * h + 64] for h in (2 * pair, 2 * pair + 1)]))
    for pair in range(2):
        lo, hi = pair_slices(pair)
        heads = (2 * pair, 2 * pair + 1)
        kt = transposed(jnp.concatenate(side_chunks(which, kv, halo, lo), axis=0))
        cn = [stat2[h : h + 1, bs] for h in heads]
        delta = jnp.concatenate([stat2[8 + h : 9 + h, bs] for h in heads], axis=1)
        ds = (pw[pair].astype(F32) * (dps[pair] - delta)).astype(BF16)
        qs = both_heads(*[scaled(qt[which, 64 * h : 64 * h + 64], c) for h, c in zip(heads, cn)])
        gs = both_heads(*[scaled(gt[which, 64 * h : 64 * h + 64], c) for h, c in zip(heads, cn)])
        for a, h in enumerate(heads):
            hs, vh = slice(64 * h, 64 * h + 64), slice(64 * a, 64 * a + 64)
            near = jnp.concatenate(
                [dqn[hs, 128 * which : 128 * which + 128], jnp.zeros((64, 128), F32)], axis=1
            )
            total = dot(kt[vh, :], ds[:, 256 * a : 256 * a + 256]) * cn[a] + near + wide(dqf[hs, :], which, 0.0)
            dqt[pair, vh, :] = (total * 0.125).astype(BF16)
        for lanes, left, right in ((lo, ds, qs), (hi, pw[pair], gs)):
            d = dot_nt(left, right)
            if which == 1:
                halo_out[:, lanes] = d[0:256].astype(BF16)
                own[bs, lanes] = d[256:512]
                own[ob, lanes] = d[512:768]
            else:
                halo_out[0:128, lanes] = (d[0:128] + near_s[0:128, lanes].astype(F32)).astype(BF16)
                halo_out[128:256, lanes] = d[128:256].astype(BF16)
                own[bs, lanes] = d[256:512] + own_in[bs, lanes]
                own[ob, lanes] = d[512:768] + own_in[ob, lanes]
                own[0:128, lanes] += own_near[0:128, lanes]
                own[256:384, lanes] += own_near[128:256, lanes]
        r = unperm_pair(off, pair, dqt[pair])
        if which == 1:
            gq[:, 128 * pair : 128 * pair + 128] = r
        else:
            gq[block_rows(tm, 0), 128 * pair : 128 * pair + 128] = r


def ret_y(own_far, ret, rest, y1, y2a, y2b):
    total = own_far[...] + ret[...].astype(F32)
    rest[...] = total[0:256]
    y1[...] = total[256:384].astype(BF16)
    y2a[...] = total[384:448].astype(BF16)
    y2b[...] = total[448:512].astype(BF16)


def ret_x(rest, y1, y2a, y2b, x1, x2a, x2b):
    deep = y1[...].astype(F32)
    deeper = y2a[...].astype(F32) + y2b[...].astype(F32)
    total = []
    for j, at in enumerate((0, 64, 128, 160, 192, 224)):
        size = 64 if at < 128 else 32
        top = deep[32 + 16 * j : 48 + 16 * j]
        head = rest[at : at + 16] + top
        total += [head[0:8] + deeper[16 + 8 * j : 24 + 8 * j], head[8:16], rest[at + 16 : at + size]]
    x1[...] = jnp.concatenate(total[0:6], axis=0).astype(BF16)
    x2a[...] = jnp.concatenate(total[6:12], axis=0).astype(BF16)
    x2b[...] = jnp.concatenate(total[12:18], axis=0).astype(BF16)


def gather_own(own, hc, hn, y1, y2a, y2b, acc):
    acc[...] = own[...]
    acc[0:384] += hc[...].astype(F32)
    acc[256:512] += hn[...].astype(F32)
    for b in range(2):
        at = 256 * b
        acc[at : at + 16] += y1[16 * b : 16 * b + 16].astype(F32)
        acc[at : at + 8] += (y2a[0:16].astype(F32) + y2b[0:16].astype(F32))[8 * b : 8 * b + 8]


def finish(off, tm, acc, x1, x2a, x2b, gk, gv, kb, vb, sem):
    keep = lane_first(256, 256)
    perms = [from_depth(off[h]) for h in range(4)]
    copies = []
    for b in range(2):
        at = 256 * b
        rows = slice(at, at + 256)
        for pair in range(2):
            lanes = slice(128 * pair, 128 * pair + 128)
            cols = slice(256 * pair, 256 * pair + 256)
            head = acc[at : at + 64, cols] + x1[64 * b : 64 * b + 64, cols].astype(F32)
            deep = x2a[32 * b : 32 * b + 32, cols].astype(F32) + x2b[32 * b : 32 * b + 32, cols].astype(F32)
            x = jnp.concatenate([head[0:32] + deep, head[32:64], acc[at + 64 : at + 256, cols]], axis=0).astype(BF16)
            r = jnp.where(keep, dot(perms[2 * pair], x), dot(perms[2 * pair + 1], x)).astype(BF16)
            kb[rows, lanes] = r[:, 0:128]
            vb[rows, lanes] = r[:, 128:256]
        for src, dst in ((kb, gk), (vb, gv)):
            copies.append(pltpu.make_async_copy(src.at[rows], dst.at[block_rows(tm, b)], sem.at[len(copies)]))
            copies[-1].start()
    for c in copies:
        c.wait()


def half_rows(tm, w, out):
    out[...] = w[pl.ds(pl.multiple_of(128 * parity(tm), 128), 128), :]


def asm_w(tm, own, first, other, mine, theirs, out):
    out[0:256] = own[...]
    out[256:512] = first[...]
    out[512:768] = other[...]
    p = parity(tm)
    out[pl.ds(pl.multiple_of(768 + 128 * p, 128), 128), :] = mine[...]
    out[pl.ds(pl.multiple_of(896 - 128 * p, 128), 128), :] = theirs[...]


def project(tm, a01, a23, w, out, buf, sem):
    a = jnp.concatenate([a01[...], a23[...]], axis=1)
    copies = []
    for c in range(4):
        cols = slice(256 * c, 256 * c + 256)
        buf[:, cols] = dot(a, w[:, cols]).astype(BF16)
        for b in range(2):
            src = buf.at[256 * b : 256 * b + 256, cols]
            copies.append(pltpu.make_async_copy(src, out.at[block_rows(tm, b), cols], sem.at[len(copies)]))
            copies[-1].start()
    for c in copies:
        c.wait()


def swap(x, axis, mask):
    return lax.ppermute(x, axis, [(i, i ^ mask) for i in range(lax.axis_size(axis))])


def cross(x, masks):
    heads = lax.axis_size("head")
    pairs = []
    for i in range(lax.axis_size("tm")):
        pairs += [(i * heads + z, i * heads + (z ^ masks[i % 2])) for z in range(heads)]
    return lax.ppermute(x, ("tm", "head"), pairs)


def side(x):
    pairs = [(i, i + 1 if i % 2 else i - 1) for i in range(1, lax.axis_size("tm") - 1)]
    return lax.ppermute(x, "tm", pairs)


def bind(f, *args):
    def body(*refs):
        f(*args, *refs)

    return body


def layer(q, k, v, w, up, win, off):
    tm = lax.axis_index("tm").astype(jnp.int32).reshape(1)
    VM = pltpu.VMEM
    hbm = pl.BlockSpec(memory_space=pltpu.HBM)
    rows = lambda n: sds((n, 512), BF16)
    kvp, c1s, n1s, x1s, x2s, qv, upv, wv = call(
        prep_kv, (tm,) + tuple(pltpu.with_memory_space_constraint(x, pltpu.HBM) for x in (off, k, v, q, up, w)),
        [rows(512), rows(384), rows(256), rows(128), rows(64),
         sds((512, 256), BF16), sds((512, 1024), BF16), sds((256, 1024), BF16)],
        specs=[SMEM] + [hbm] * 6,
        scratch=[VM((512, 256), BF16), VM((512, 256), BF16), pltpu.SMEM((4,), jnp.int32), pltpu.SemaphoreType.DMA((10,))],
        flops=3e8, nbytes=3e6,
    )
    x1, x2a, x2b = swap(x1s, "tm", 2), swap(x2s, "tm", 4), swap(x2s, "tm", 6)
    c1 = swap(c1s, "tm", 1)
    n1 = side(n1s)
    w1 = cross(wv, (1, 3))
    (w1h,) = call(half_rows, (tm, w1), [sds((128, 1024), BF16)], specs=[SMEM, None])
    w2 = cross(w1h, (3, 1))
    (w_all,) = call(
        asm_w, (tm, wv, w1, swap(w1, "tm", 1), w2, swap(w2, "tm", 1)),
        [sds((1024, 1024), BF16)], specs=[SMEM] + [None] * 5, nbytes=4e6,
    )
    qt, gt = call(
        prep_qg, (off, qv, upv, wv), [sds((2, 256, 256), BF16), sds((2, 256, 256), BF16)],
        specs=[SMEM] + [None] * 3, flops=6e8, nbytes=3e6,
    )
    near = []
    for which in range(2):
        near.append(
            call(
                bind(fwd_near, which), (off, win, tm, qt, kvp, c1) + ((n1,) if which else ()),
                [sds((2, 768, 512), BF16), sds((2, 512, 256), BF16), sds((256, 256), F32), sds((8, 256), F32)],
                specs=[SMEM] * 3 + [None] * (3 + which),
                scratch=[
                    VM((2, 128, 768), BF16), VM((2, 128, 512), BF16),
                    VM((2, 256, 512), F32), VM((2, 768, 512), F32), VM((2, 512, 256), F32),
                ],
                flops=3e9, nbytes=4e6,
            )
        )
    y1s, y2s, mine_x = call(asm_y, (kvp, x1, x2a, x2b), [rows(128), rows(64), rows(256)])
    y1, y2a, y2b = swap(y1s, "tm", 8), swap(y2s, "tm", 16), swap(y2s, "tm", 24)
    (mine_y,) = call(stack, (y1, y2a, y2b), [rows(256)])
    bufs = (mine_x, swap(mine_x, "tm", 1), mine_y, swap(mine_y, "tm", 1))
    pf, attn, stat2 = call(
        fwd_far, (off, qt, gt, near[0][2], near[1][2], near[0][3], near[1][3], *bufs),
        [sds((2, 1024, 256), BF16), sds((512, 256), BF16), sds((16, 512), F32)],
        specs=[SMEM] + [None] * 10,
        scratch=[VM((2, 128, 1024), BF16), VM((1024, 128), F32), VM((256, 512), BF16)],
        flops=3e9, nbytes=4e6,
    )
    a1 = cross(attn, (1, 3))
    (a01,) = call(beside, (attn, a1), [rows(512)])
    a23 = cross(a01, (3, 1))
    (mixed,) = call(
        project, (tm, a01, a23, w_all), [sds((512, 1024), BF16)],
        specs=[SMEM] + [None] * 3, out_specs=[pl.BlockSpec(memory_space=pl.ANY)],
        scratch=[VM((512, 1024), BF16), pltpu.SemaphoreType.DMA((8,))], flops=1e9, nbytes=4e6,
    )
    ret_s, own_far, dqf = call(
        bwd_far, (qt, gt, stat2, pf, *bufs),
        [sds((512, 512), BF16), sds((512, 512), F32), sds((256, 128), F32)],
        flops=4e9, nbytes=5e6,
    )
    ret = swap(ret_s, "tm", 1)
    near_s, own_near, dqn = call(
        bwd_keys, (qt, gt, stat2, kvp, c1, near[0][1], near[1][1]),
        [sds((256, 512), BF16), sds((256, 512), F32), sds((256, 256), F32)],
        flops=4e9, nbytes=5e6,
    )

    def back(which, halo, gq_rows, halo_rows, more):
        return call(
            bind(bwd_near, which), (off, tm, qt, gt, stat2, kvp, halo, near[which][0], dqf, dqn, *more),
            [sds((512, 512), F32), rows(halo_rows), sds((gq_rows, 256), BF16)],
            specs=[SMEM] * 2 + [None] * (8 + len(more)),
            scratch=[VM((2, 128, 256), BF16), VM((2, 768, 512), F32)], flops=4e9, nbytes=4e6,
        )

    own1, hn_s, gq1 = back(1, n1, 256, 256, ())
    own, hc_s, gq = back(0, c1, 512, 384, (own1, own_near, near_s, gq1))
    rest, y1s, y2as, y2bs = call(ret_y, (own_far, ret), [sds((256, 512), F32), rows(128), rows(64), rows(64)])
    yr = [swap(x, "tm", m) for x, m in ((y1s, 8), (y2as, 16), (y2bs, 24))]
    x1s, x2as, x2bs = call(ret_x, (rest, *yr), [rows(128), rows(64), rows(64)])
    xr = [swap(x, "tm", m) for x, m in ((x1s, 2), (x2as, 4), (x2bs, 6))]
    hc, hn = swap(hc_s, "tm", 1), side(hn_s)
    (acc,) = call(gather_own, (own, hc, hn, *yr), [sds((512, 512), F32)], nbytes=3e6)
    gk, gv = call(
        finish, (off, tm, acc, *xr), [sds((512, 256), BF16), sds((512, 256), BF16)],
        out_specs=[pl.BlockSpec(memory_space=pl.ANY)] * 2,
        scratch=[VM((512, 256), BF16), VM((512, 256), BF16), pltpu.SemaphoreType.DMA((4,))],
        specs=[SMEM] * 2 + [None] * 4, flops=3e8, nbytes=3e6,
    )
    return mixed, gq, gk, gv


def solution(mesh):
    placed = (P("tm", "head"),) * 3 + (P("head", None), P("tm", None), P("head"), P("head"))
    return jax.shard_map(
        layer,
        mesh=mesh,
        in_specs=placed,
        out_specs=(P("tm", None), P("tm", "head"), P("tm", "head"), P("tm", "head")),
        check_vma=False,
    )
```
